32 devices in a mesh: pairs: 2 (over y), gx: 4 (over z), gy: 2 (over x), gz: 2 (over core).
Axes of the slice: x: 2, y: 2, z: 4, core: 2. Of those that a mesh axis runs over, the one named last changes fastest.
Arguments:
- sections: bfloat16 [2, 2048, 2048], P('gz', ('pairs', 'gy'), 'gx'), parts along dimension 1, may hold values from -16 to 16
- fine_offsets: int32 [4], P('pairs'), parts along dimension 0, may hold values from 0 to 31
- coarse_offset: int32 [2], P('pairs'), parts along dimension 0, may hold values from 0 to 63
- tissue_mask: int32 [64, 64], P(('pairs', 'gy'), 'gx'), parts along dimension 0, may hold values 0 or 1
Outputs:
- flow: float32 [2, 2, 64, 32], P(None, 'gz', ('pairs', 'gy'), 'gx'), parts along dimension 2
The draws below stay inside these ranges and needn't reach their ends.
There are 2 independent parts, one for each index of `pairs`. The reference program is written for one: setup_inputs(seed, part) draws one part's arguments, and reference() takes and returns one part's arrays. A program takes and returns all parts, laid end to end along the dimension named above; each array names one. Nothing has to cross between parts.
All inputs are finite; a program needn't handle non-finite values. No bound on the sum of `tissue_mask` on one device may be relied on, other than what follows from the above.
Results may differ from the reference program's by a relative error of at most 0.00075.
Values may be sent and summed in bfloat16 or wider, within the bound.
A program may use at most 64 MiB of HBM per device.

```python
import jax
import jax.numpy as jnp
from jax import lax

P_SIZE = 64
STRIDE = 32
DOWN = 8
TY = 512
TX = 512
NY = 1024
NX = 2048
FR = 16
FC = 16
NCR = 1
NCC = 4
N_GX = 4
N_GY = 2


def roll_rows(column_block, amount):
    return jnp.roll(column_block, amount, axis=0)


def roll_columns(row_block, amount):
    return jnp.roll(row_block, amount, axis=1)


def draw_sections(key, part):
    random_seedlings = jax.random.split(jax.random.fold_in(key, 7), 6)
    texture = jax.random.normal(random_seedlings[0], (NY, NX), jnp.float32)
    down_moves = jax.random.randint(random_seedlings[3], (NX // TX,), -(3 * P_SIZE // 2), 3 * P_SIZE // 2 + 1)
    side_moves = jax.random.randint(random_seedlings[4], (NY // TY,), -(3 * P_SIZE // 2), 3 * P_SIZE // 2 + 1)
    shifted = jax.vmap(roll_rows, in_axes=(1, 0), out_axes=1)(texture.reshape(NY, NX // TX, TX), down_moves).reshape(NY, NX)
    shifted = jax.vmap(roll_columns, in_axes=(0, 0), out_axes=0)(shifted.reshape(NY // TY, TY, NX), side_moves).reshape(NY, NX)
    noise_field = jax.random.normal(random_seedlings[5], (NY, NX), jnp.float32)
    second = 0.8 * shifted + 0.6 * noise_field
    return jnp.clip(jnp.stack([texture, second]), -16.0, 16.0).astype(jnp.bfloat16)


def plant(values, own_key, smallest, high):
    place = [jax.random.randint(jax.random.fold_in(own_key, axis), (), 0, length) for axis, length in enumerate(values.shape)]
    longest = values.shape.index(max(values.shape))
    neighbour = place[:longest] + [(place[longest] + 1) % values.shape[longest]] + place[longest + 1:]
    return values.at[tuple(place)].set(smallest).at[tuple(neighbour)].set(high)


def setup_inputs(seed: int = 0, part: int = 0) -> dict:
    splits = jax.random.split(jax.random.key(seed), 5)
    part_keys = jax.random.split(jax.random.fold_in(splits[4], part), 5)
    sections = draw_sections(jax.random.fold_in(jax.random.fold_in(splits[4], part), 71), part)
    fine_offsets = jax.random.randint(part_keys[1], (2,), 0, STRIDE).astype(jnp.int32)
    coarse_offset = jax.random.randint(part_keys[2], (1,), 0, P_SIZE).astype(jnp.int32)
    tissue_mask = plant((jax.random.randint(part_keys[3], (FR * N_GY, FC * N_GX), 0, 4) < 3).astype(jnp.int32), jax.random.fold_in(part_keys[3], 1), 0, 1)
    return {"sections": sections, "fine_offsets": fine_offsets, "coarse_offset": coarse_offset, "tissue_mask": tissue_mask}


sharpness_divisor = 12.0


def peak_offsets(first_patch, second_patch, prior_shift):
    square_edge_pixels = first_patch.shape[-1]
    number_squares = first_patch.shape[0]
    first_spec = jnp.fft.fft2(first_patch)
    second_spec = jnp.fft.fft2(second_patch)
    signed = ((jnp.arange(square_edge_pixels) + square_edge_pixels // 2) % square_edge_pixels - square_edge_pixels // 2).astype(first_patch.dtype)
    phases = 2.0 * jnp.pi * (signed[None, :, None] * prior_shift[0][:, None, None] + signed[None, None, :] * prior_shift[1][:, None, None]) / square_edge_pixels
    spectrum = second_spec * jnp.conj(first_spec) * (jnp.cos(phases) + 1j * jnp.sin(phases))
    match_landscape = jnp.real(jnp.fft.ifft2(spectrum))
    maximum_response = (sharpness_divisor / (square_edge_pixels * square_edge_pixels)) * match_landscape.reshape(number_squares, square_edge_pixels * square_edge_pixels)
    weights = jax.nn.softmax(maximum_response, axis=-1).reshape(number_squares, square_edge_pixels, square_edge_pixels)
    along_rows = jnp.sum(weights * signed[None, :, None], axis=(1, 2))
    along_columns = jnp.sum(weights * signed[None, None, :], axis=(1, 2))
    return jnp.stack([along_rows, along_columns])


def reference(sections, fine_offsets, coarse_offset, tissue_mask):
    pixels = sections.astype(jnp.float32)
    summed = pixels.reshape(2, NY // DOWN, DOWN, NX // DOWN, DOWN).sum(axis=(2, 4)) / DOWN
    coarse = lax.optimization_barrier(summed.astype(jnp.bfloat16)).astype(jnp.float32)
    coarse_rows = NCR * N_GY
    widened = jnp.pad(coarse, ((0, 0), (0, 0), (0, P_SIZE)))
    window = lax.dynamic_slice_in_dim(widened, coarse_offset[0].astype(jnp.int32), NCC * P_SIZE, 2)
    coarse_patches = window.reshape(2, coarse_rows, P_SIZE, NCC, P_SIZE).transpose(0, 1, 3, 2, 4).reshape(2, coarse_rows * NCC, P_SIZE, P_SIZE)
    coarse_flow = peak_offsets(coarse_patches[0], coarse_patches[1], jnp.zeros((2, coarse_rows * NCC), jnp.float32))
    coarse_flow = coarse_flow.reshape(2, coarse_rows, NCC)
    blended_flow = 0.5 * (coarse_flow + jnp.mean(coarse_flow, axis=2, keepdims=True))
    padded = jnp.pad(sections, ((0, 0), (0, P_SIZE), (0, P_SIZE)))
    row_offset = fine_offsets[0].astype(jnp.int32)
    column_offset = fine_offsets[1].astype(jnp.int32)
    columns = jnp.arange(FC * N_GX, dtype=jnp.int32)
    centre_column = columns * STRIDE + column_offset + P_SIZE // 2
    column_pick = jnp.clip((centre_column // DOWN - coarse_offset[0]) // P_SIZE, 0, NCC - 1)

    def one_row(row_index):
        zero_index = jnp.zeros((), jnp.int32)
        beginning_line = (row_offset + STRIDE * row_index).astype(jnp.int32)
        band_rows = lax.dynamic_slice(padded, (zero_index, beginning_line, column_offset), (2, P_SIZE, NX + STRIDE)).astype(jnp.float32)
        pieces = band_rows.reshape(2, P_SIZE, FC * N_GX + 1, STRIDE)
        patches = jnp.concatenate([pieces[:, :, :-1, :], pieces[:, :, 1:, :]], axis=3).transpose(0, 2, 1, 3)
        local_centre = (row_index % FR) * STRIDE + row_offset + P_SIZE // 2
        row_pick = jnp.minimum(local_centre // (DOWN * P_SIZE), NCR - 1) + (row_index // FR) * NCR
        prior_flow = DOWN * blended_flow[:, row_pick, :][:, column_pick]
        found_flow = peak_offsets(patches[0], patches[1], prior_flow)
        return prior_flow + tissue_mask[row_index].astype(jnp.float32)[None, :] * found_flow

    patch_flow = lax.map(one_row, jnp.arange(FR * N_GY, dtype=jnp.int32)).transpose(1, 0, 2)
    paired = patch_flow.reshape(2, FR * N_GY, FC * N_GX // 2, 2)
    parity = jnp.arange(FR * N_GY) % 2
    layers = [jnp.where(((parity + section_side) % 2 == 0)[None, :, None], paired[..., 0], paired[..., 1]) for section_side in range(2)]
    return jnp.stack(layers, axis=1)
```

```python
import jax
import jax.numpy as jnp
import numpy as np
from jax import lax
from jax.experimental import pallas as pl
from jax.experimental.pallas import tpu as pltpu
from jax.sharding import PartitionSpec as P

P_SIZE = 64
STRIDE = 32
DOWN = 8
HALF = P_SIZE // 2
GROUP = 4
SHARP = 12.0
VMEM_BYTES = 56 * 2**20
MESH = pl.DeviceIdType.MESH
F32 = jnp.float32
BF16 = jnp.bfloat16


def split_table(table):
    high = np.asarray(table, np.float32).astype(jnp.bfloat16)
    low = (np.asarray(table, np.float64) - high.astype(np.float64)).astype(np.float32)
    return high, low.astype(jnp.bfloat16)


def make_tables():
    turn = 2.0 * np.pi / P_SIZE
    k = np.arange(HALF)
    x = np.arange(2 * GROUP * STRIDE)
    angle = turn * (np.outer(x, k) % P_SIZE)
    real = np.cos(angle)
    imag = -np.sin(angle)
    imag[:, 0] = np.cos(np.pi * x)
    forward_x = np.concatenate([np.tile(real, (1, GROUP)), np.tile(imag, (1, GROUP))], axis=1)
    high, low = split_table(forward_x)
    table_x = np.concatenate([high, low], axis=0)
    ky = np.arange(P_SIZE)
    angle = turn * (np.outer(ky, ky) % P_SIZE)
    high, low = split_table(np.concatenate([np.cos(angle), np.sin(angle)], axis=0))
    table_y = np.concatenate([high, low, high], axis=1)
    angle = turn * (np.outer(ky, ky) % P_SIZE)
    cosine, sine = np.cos(angle), np.sin(angle)
    inverse_y = np.block([[cosine, -sine], [sine, cosine]])
    high, low = split_table(inverse_y)
    table_iy = np.concatenate([high, low, high], axis=1)
    angle = turn * (np.outer(k, ky) % P_SIZE)
    real = 2.0 * np.cos(angle)
    imag = -2.0 * np.sin(angle)
    real[0] = 1.0
    imag[0] = np.cos(np.pi * ky)
    scale = SHARP / float(P_SIZE) ** 4
    eye = np.eye(GROUP)
    inverse_x = np.concatenate([np.kron(eye, real), np.kron(eye, imag)], axis=0) * scale
    high, low = split_table(inverse_x)
    table_ix = np.concatenate([high, high, low], axis=0)
    return table_x, table_y, table_iy, table_ix


def iota(shape, dim):
    return lax.broadcasted_iota(jnp.int32, shape, dim)


def two_terms(value):
    high = value.astype(BF16)
    return high, (value - high.astype(F32)).astype(BF16)


def bdot(a, b):
    return jnp.dot(a, b, preferred_element_type=F32)


def signed_of(index):
    return jnp.where(index >= HALF, index - P_SIZE, index).astype(F32)


def cis(turns):
    rest = turns - jnp.floor(turns + 0.5)
    a = rest * np.float32(np.pi)
    q = a * a
    s = np.float32(-1 / 39916800.0)
    for c in (1 / 362880.0, -1 / 5040.0, 1 / 120.0, -1 / 6.0, 1.0):
        s = s * q + np.float32(c)
    s = s * a
    c = np.float32(1 / 479001600.0)
    for d in (-1 / 3628800.0, 1 / 40320.0, -1 / 720.0, 1 / 24.0, -0.5, 1.0):
        c = c * q + np.float32(d)
    return 1.0 - 2.0 * s * s, 2.0 * s * c


def segment_max(value):
    width = value.shape[1]
    place = iota(value.shape, 1) & (P_SIZE - 1)
    step = 1
    while step < P_SIZE:
        near = pltpu.roll(value, step, 1)
        far = pltpu.roll(value, width - P_SIZE + step, 1)
        value = jnp.maximum(value, jnp.where(place >= step, near, far))
        step *= 2
    return value


def forward_y(table, spectrum_x):
    high, low = two_terms(spectrum_x)
    return bdot(table, jnp.concatenate([high, high, low], axis=0))


def planes(product, unit):
    base = unit * 2 * P_SIZE
    lanes = GROUP * HALF
    cosine = product[base : base + P_SIZE]
    sine = product[base + P_SIZE : base + 2 * P_SIZE]
    return cosine[:, :lanes], sine[:, :lanes], cosine[:, lanes:], sine[:, lanes:]


def cross(first, second, unit, nyquist):
    a1, a2, a3, a4 = planes(first, unit)
    b1, b2, b3, b4 = planes(second, unit)
    ar = a1 + jnp.where(nyquist, 0.0, a4)
    ai = jnp.where(nyquist, 0.0, a3) - a2
    br = b1 + jnp.where(nyquist, 0.0, b4)
    bi = jnp.where(nyquist, 0.0, b3) - b2
    return (br * ar + bi * ai, bi * ar - br * ai, b3 * a3 + b4 * a4, b3 * a4 - b4 * a3)


def landscape(units, table_iy, table_ix):
    stacked = []
    for zr, zi in units:
        high, low = two_terms(jnp.concatenate([zr, zi], axis=0))
        stacked.append(jnp.concatenate([high, high, low], axis=0))
    back = bdot(table_iy, jnp.concatenate(stacked, axis=1) if len(stacked) > 1 else stacked[0])
    lanes = GROUP * HALF
    rows = []
    for unit in range(len(units)):
        piece = back[:, unit * lanes : (unit + 1) * lanes]
        rows.append(jnp.concatenate([piece[:P_SIZE], piece[P_SIZE:]], axis=1))
    value = jnp.concatenate(rows, axis=0) if len(rows) > 1 else rows[0]
    high, low = two_terms(value)
    return bdot(jnp.concatenate([high, low, high], axis=1), table_ix)


def exact_dot(a, b):
    terms = []
    for _ in range(3):
        terms.append(a.astype(BF16))
        a = a - terms[-1].astype(F32)
    return bdot(jnp.concatenate(terms, axis=1), jnp.concatenate([b, b, b], axis=0))


def kernel(
    n_gx, n_gy, fine_hbm, coarse_hbm, tile_hbm, mask_hbm, *rest
):
    hbm_tables, (out,), scratch = rest[:4], rest[4:5], rest[5:]
    table_refs, scratch = scratch[:4], scratch[4:]
    (tile, ext, coarse, own, given, got, spec, spec_high, spec_low, ctab, logits, peaks, stats) = scratch[:13]
    send_sem, recv_sem, csend, crecv, local_sem, table_sem, back_sem = scratch[13:20]
    fine_off, coarse_off, mask, small_sem = scratch[20:]
    tx, ty, tiy_ref, tix_ref = table_refs
    pairs, gx, gy, gz = (lax.axis_index(a) for a in ("pairs", "gx", "gy", "gz"))
    rows, width = tile.shape
    half = rows // 2
    edge = ext.shape[2] - width

    def device(x, y, z):
        return (pairs, x, y, z)

    load = pltpu.make_async_copy(tile_hbm, tile, local_sem.at[2])
    load.start()
    small_copies = [
        pltpu.make_async_copy(source, target, small_sem.at[n])
        for n, (source, target) in enumerate(
            ((fine_hbm, fine_off), (coarse_hbm, coarse_off), (mask_hbm, mask))
        )
    ]
    for copy in small_copies:
        copy.start()

    barrier = pltpu.get_barrier_semaphore()
    count = 0
    for dy in (-1, 0, 1):
        for x in range(n_gx):
            for z in range(2):
                y = gy + dy
                near = (x - gx <= 1) & (x - gx >= -1) if dy else (x != gx) | (z != gz)
                use = (y >= 0) & (y < n_gy) & near
                count = count + jnp.where(use, 1, 0)

                @pl.when(use)
                def _():
                    pl.semaphore_signal(
                        barrier, inc=1, device_id=device(x, y, z), device_id_type=MESH
                    )

    table_copies = [
        pltpu.make_async_copy(source, target, table_sem.at[n])
        for n, (source, target) in enumerate(zip(hbm_tables, table_refs))
    ]
    for copy in table_copies:
        copy.start()
    first_half = pltpu.make_async_copy(
        tile_hbm.at[pl.ds(0, half + P_SIZE), :],
        ext.at[0, pl.ds(0, half + P_SIZE), pl.ds(0, width)],
        local_sem.at[0],
    )
    second_half = pltpu.make_async_copy(
        tile_hbm.at[pl.ds(half, half), :], ext.at[1, pl.ds(0, half), pl.ds(0, width)], local_sem.at[1]
    )

    @pl.when(gz == 0)
    def _():
        first_half.start()

    @pl.when(gz == 1)
    def _():
        second_half.start()

    load.wait()
    pool_rows = jnp.where((iota((rows // DOWN, rows), 1) >> 3) == iota((rows // DOWN, rows), 0), 1.0, 0.0)
    summed = bdot(pool_rows.astype(BF16), tile[...])
    lanes = iota((width, 2 * P_SIZE), 1)
    block = iota((width, 2 * P_SIZE), 0) >> 3
    packed = jnp.zeros((rows // DOWN // 2, 2 * P_SIZE), F32)
    for part in range(2):
        piece = summed[part * (rows // DOWN // 2) : (part + 1) * (rows // DOWN // 2)]
        pool = jnp.where(block == lanes - part * P_SIZE, 1.0, 0.0).astype(BF16)
        for _ in range(3):
            term = piece.astype(BF16)
            packed = packed + bdot(term, pool)
            piece = piece - term.astype(F32)
    packed = (packed * (1.0 / DOWN)).astype(BF16)
    own[...] = packed
    coarse[gx, gz] = packed

    @pl.when(gx + 1 >= n_gx)
    def _():
        ext[:, :, width:] = jnp.zeros((2, half + P_SIZE, edge), BF16)

    @pl.when((gz == 1) & (gy + 1 >= n_gy))
    def _():
        ext[:, half:, :width] = jnp.zeros((2, P_SIZE, width), BF16)
        ext[:, half:, width:] = jnp.zeros((2, P_SIZE, edge), BF16)

    pl.semaphore_wait(barrier, count)

    def halo_copy(kind, c, section, x, y):
        columns = pl.ds(0, width) if c == 0 else pl.ds(0, edge)
        into = pl.ds(0, width) if c == 0 else pl.ds(width, edge)
        source, target = (
            (pl.ds(0, half + P_SIZE), pl.ds(0, half + P_SIZE)),
            (pl.ds(half, half), pl.ds(0, half)),
            (pl.ds(0, P_SIZE), pl.ds(half, P_SIZE)),
        )[kind]
        slot = kind * 4 + c * 2
        return pltpu.make_async_remote_copy(
            src_ref=tile.at[source, columns],
            dst_ref=ext.at[section, target, into],
            send_sem=send_sem.at[slot],
            recv_sem=recv_sem.at[slot + section],
            device_id=device(x, y, 0 if kind == 0 else 1),
            device_id_type=MESH,
        )

    def coarse_copy(x, z, from_x, from_z):
        return pltpu.make_async_remote_copy(
            src_ref=own,
            dst_ref=coarse.at[from_x, from_z],
            send_sem=csend.at[x, z],
            recv_sem=crecv.at[from_x, from_z],
            device_id=device(x, gy, z),
            device_id_type=MESH,
        )

    for x in range(n_gx):
        for z in range(2):

            @pl.when((x != gx) | (z != gz))
            def _():
                coarse_copy(x, z, gx, gz).start()

    def sends():
        out = []
        for c in (1, 0):
            for kind in range(3):
                use = gx - c >= 0
                if kind == 2:
                    use = use & (gy - 1 >= 0)
                elif c == 0:
                    use = use & (gz != kind)
                out.append((use, kind, c, gx - c, gy - 1 if kind == 2 else gy))
        return out

    for use, kind, c, x, y in sends():

        @pl.when(use)
        def _():
            halo_copy(kind, c, gz, x, y).start()

    def arrivals(wanted):
        for c in (0, 1):
            for section in range(2):
                for kind in range(3):
                    if wanted != c:
                        continue
                    use = (gz == 0) if kind == 0 else (gz == 1)
                    if c == 1:
                        use = use & (gx + 1 < n_gx)
                    if kind == 2:
                        use = use & (gy + 1 < n_gy)
                    elif c == 0:
                        use = use & (gz != section)

                    @pl.when(use)
                    def _():
                        halo_copy(kind, c, section, gx, gy).wait_recv()

    tile_width = mask.shape[1] * STRIDE
    patch_rows = half // STRIDE
    groups = mask.shape[1] // GROUP
    lanes = GROUP * HALF
    wide = GROUP * P_SIZE
    for copy in small_copies:
        copy.wait()
    roff, coff, off = fine_off[0], fine_off[1], coarse_off[0]
    for copy in table_copies:
        copy.wait()
    table_iy, table_ix = tiy_ref[...], tix_ref[...]

    span = tx.shape[0] // 2
    at = iota((span, 2 * lanes), 0) - coff - STRIDE * ((iota((span, 2 * lanes), 1) >> 5) & (GROUP - 1))
    inside = jnp.where((at >= 0) & (at < P_SIZE), 1.0, 0.0).astype(BF16)
    coarse_groups = n_gx // GROUP
    block = (2 * P_SIZE, 2 * lanes)
    from_left = (iota(block, 0) & (P_SIZE - 1)) - P_SIZE * ((iota(block, 1) >> 5) & (GROUP - 1)) - off
    plain = [tx[0 : 2 * P_SIZE], tx[span : span + 2 * P_SIZE]]
    for step in range(min(GROUP + 1, n_gx)):
        at_step = from_left + step * P_SIZE
        keep = jnp.where((at_step >= 0) & (at_step < P_SIZE), 1.0, 0.0).astype(BF16)
        for term in range(2):
            base = (2 * step + term) * 2 * P_SIZE
            ctab[base : base + 2 * P_SIZE] = plain[term] * keep
    tx[0:span] = tx[0:span] * inside
    tx[span:] = tx[span:] * inside

    nyquist = (iota((P_SIZE, lanes), 1) & (HALF - 1)) == 0
    frow = signed_of(iota((P_SIZE, wide), 0))

    def along_x_of(section, top, size, g):
        data = ext[section, pl.ds(top, size), g * lanes : g * lanes + span]
        value = bdot(jnp.concatenate([data, data], axis=1), tx[...])
        spec[section, 2 * g, pl.ds(top, size), :] = value[:, :lanes]
        spec[section, 2 * g + 1, pl.ds(top, size), :] = value[:, lanes:]

    inner = groups - 1

    @pl.when(gz == 0)
    def _():
        first_half.wait()

    @pl.when(gz == 1)
    def _():
        second_half.wait()

    for g in range(inner):
        along_x_of(gz, 0, half, g)

    for x in range(n_gx):
        for z in range(2):

            @pl.when((x != gx) | (z != gz))
            def _():
                coarse_copy(x, z, x, z).wait_recv()

    left = iota((HALF, 2 * P_SIZE), 1) < P_SIZE
    flows_y, flows_x = [], []
    ones = jnp.where((iota((wide, wide), 0) >> 6) == (iota((wide, wide), 1) >> 6), 1.0, 0.0)
    ones = ones.astype(BF16)
    fcol = signed_of(iota((1, wide), 1) & (P_SIZE - 1))
    for cg in range(coarse_groups):
        sources = range(cg * GROUP, min(cg * GROUP + GROUP + 1, n_gx))
        lines = []
        for section in range(2):
            terms = []
            for source in sources:
                data = coarse[source, section].astype(F32)
                both = jnp.concatenate(
                    [jnp.where(left, data, 0.0), jnp.where(left, 0.0, data)], axis=0
                ).astype(BF16)
                terms += [both, both]
            lines.append(jnp.concatenate(terms, axis=1))
        value = bdot(jnp.concatenate(lines, axis=0), ctab[0 : len(sources) * 4 * P_SIZE])
        first = forward_y(ty[...], value[:P_SIZE])
        second = forward_y(ty[...], value[P_SIZE:])
        hr, hi, yr, yi = cross(first, second, 0, nyquist)
        value = landscape(
            [(hr - jnp.where(nyquist, yi, 0.0), hi + jnp.where(nyquist, yr, 0.0))], table_iy, table_ix
        )
        top = segment_max(jnp.broadcast_to(jnp.max(value, axis=0, keepdims=True), (8, wide)))[0:1]
        weight = jnp.exp(value - top)
        s0 = jnp.sum(weight, axis=0, keepdims=True)
        s1 = jnp.sum(weight * frow, axis=0, keepdims=True)
        rows = iota((8, wide), 0)
        both = jnp.where(rows == 0, s0, jnp.where(rows == 1, s1, jnp.where(rows == 2, s0 * fcol, 0.0)))
        total = exact_dot(both, ones)
        flows_y.append(total[1:2] / total[0:1])
        flows_x.append(total[2:3] / total[0:1])

    def blend(flows):
        mean = sum(jnp.sum(f, axis=1, keepdims=True) for f in flows) / float(P_SIZE * n_gx)
        return [(0.5 * DOWN) * (f + mean) for f in flows]

    blended_y, blended_x = blend(flows_y), blend(flows_x)
    rows = iota((8, wide), 0)
    blended = [
        jnp.where(rows == 0, y, jnp.where(rows == 1, x, 0.0)) for y, x in zip(blended_y, blended_x)
    ]

    def pick(column):
        centre = gx * tile_width + column * STRIDE + coff + P_SIZE // 2
        chosen = jnp.clip(((centre >> 3) - off) >> 6, 0, n_gx - 1)
        total = None
        for cg in range(coarse_groups):
            hot = jnp.where(iota(column.shape, 0) == (chosen - cg * GROUP) * P_SIZE, 1.0, 0.0)
            term = exact_dot(blended[cg], hot.astype(BF16))
            total = term if total is None else total + term
        return total

    fky = signed_of(iota((P_SIZE, lanes), 0)) * (1.0 / P_SIZE)
    middle = iota((P_SIZE, lanes), 0) == HALF
    kx = (iota((1, lanes), 1) & (HALF - 1)).astype(F32) * (1.0 / P_SIZE)

    arrivals(0)
    for g in range(inner):
        along_x_of(1 - gz, 0, half, g)
        for section in range(2):
            along_x_of(section, half, P_SIZE, g)

    for g in range(groups):
        if g == inner:
            arrivals(1)
            for section in range(2):
                along_x_of(section, 0, half + P_SIZE, g)
        prior = pick(g * GROUP + (iota((wide, lanes), 1) >> 5))
        dy, dx = prior[0:1], prior[1:2]
        eyr, eyi = cis(fky * dy)
        exr, exi = cis(kx * dx)
        nr, ni = cis(0.5 * dx)
        fr = jnp.where(nyquist, nr * eyr + jnp.where(middle, ni * eyi, 0.0), 0.0)
        eyi = jnp.where(middle, 0.0, eyi)
        fi = jnp.where(nyquist, nr * eyi, 0.0)
        er = eyr * exr - eyi * exi
        ei = eyr * exi + eyi * exr
        part = slice(g * 2 * lanes, (g + 1) * 2 * lanes)
        for section in range(2):
            for t in range(2):
                high, low = two_terms(spec[section, 2 * g + t, pl.ds(roff, (patch_rows + 1) * STRIDE), :])
                part = slice((2 * g + t) * lanes, (2 * g + t + 1) * lanes)
                spec_high[section, :, part] = high
                spec_low[section, :, part] = low
        part = slice(g * 2 * lanes, (g + 1) * 2 * lanes)
        for q in range(patch_rows // GROUP):
            units = []
            for unit in range(GROUP):
                window = slice((q * GROUP + unit) * STRIDE, (q * GROUP + unit) * STRIDE + P_SIZE)
                first, second = (
                    bdot(
                        ty[...],
                        jnp.concatenate(
                            [
                                spec_high[t, window, part],
                                spec_high[t, window, part],
                                spec_low[t, window, part],
                            ],
                            axis=0,
                        ),
                    )
                    for t in range(2)
                )
                xr, xi, yr, yi = cross(first, second, 0, nyquist)
                hr = xr * er - xi * ei
                hi = xr * ei + xi * er
                units.append((hr - (yr * fi + yi * fr), hi + (yr * fr - yi * fi)))
            value = landscape(units, table_iy, table_ix)
            base = g * patch_rows + q * GROUP
            for unit in range(GROUP):
                piece = value[unit * P_SIZE : (unit + 1) * P_SIZE]
                logits[base + unit] = piece
                peaks[base + unit : base + unit + 1] = jnp.max(piece, axis=0, keepdims=True)

    peaks[...] = segment_max(peaks[...])

    def weigh(n, carry):
        weight = jnp.exp(logits[n] - peaks[pl.ds(n, 1)])
        stats[0, pl.ds(n, 1)] = jnp.sum(weight, axis=0, keepdims=True)
        stats[1, pl.ds(n, 1)] = jnp.sum(weight * frow, axis=0, keepdims=True)
        return carry

    lax.fori_loop(0, groups * patch_rows, weigh, 0, unroll=4)

    columns = mask.shape[1]
    side = columns // 2

    def lane_of(column):
        return (column & 1) * side + (column >> 1)

    put = jnp.where(lane_of(iota((wide, 128), 0) >> 6) == iota((wide, 128), 1), 1.0, 0.0)
    s0 = stats[0]
    sums = exact_dot(jnp.concatenate([s0, stats[1], s0 * fcol], axis=0), put.astype(BF16))
    units = groups * patch_rows

    def gather(stat):
        total = None
        for g in range(groups):
            piece = sums[stat * units + g * patch_rows : stat * units + (g + 1) * patch_rows]
            if g:
                piece = pltpu.roll(piece, g * GROUP // 2, 1)
            total = piece if total is None else total + piece
        return total

    den, along_y, along_x = gather(0), gather(1), gather(2)
    lane = iota((wide, 128), 1)
    prior = pick(jnp.where(lane < side, 2 * lane, jnp.minimum(2 * (lane - side) + 1, columns - 1)))
    here = pl.ds(pl.multiple_of(gz * patch_rows, 8), patch_rows)
    place = jnp.where(lane_of(iota((columns, 128), 0)) == iota((columns, 128), 1), 1.0, 0.0)
    valid = bdot(mask[here, :].astype(F32).astype(BF16), place.astype(BF16))
    den = jnp.where(iota((patch_rows, 128), 1) < columns, den, 1.0)
    same = ((iota((patch_rows, 128), 0) + gz) & 1) == 0
    kept = []
    for c, total in enumerate((along_y, along_x)):
        value = prior[c : c + 1] + valid * (total / den)
        odd = pltpu.roll(value, 128 - side, 1)
        given[c] = jnp.where(same, odd, value)
        kept.append(jnp.where(same, value, odd))
    back = pltpu.make_async_remote_copy(
        src_ref=given,
        dst_ref=got,
        send_sem=back_sem.at[0],
        recv_sem=back_sem.at[1],
        device_id=device(gx, gy, 1 - gz),
        device_id_type=MESH,
    )
    back.start()
    for x in range(n_gx):
        for z in range(2):

            @pl.when((x != gx) | (z != gz))
            def _():
                coarse_copy(x, z, gx, gz).wait_send()

    for use, kind, c, x, y in sends():

        @pl.when(use)
        def _():
            halo_copy(kind, c, gz, x, y).wait_send()

    back.wait()
    upper = jnp.full((patch_rows, 128), gz, jnp.int32) == 0
    for c in range(2):
        value = jnp.concatenate(
            [jnp.where(upper, kept[c], got[c]), jnp.where(upper, got[c], kept[c])], axis=0
        )
        out[c] = jnp.transpose(value)[:side]


def solution(mesh):
    n_gx, n_gy = mesh.shape["gx"], mesh.shape["gy"]
    tables = make_tables()
    vmem = pl.BlockSpec(memory_space=pltpu.VMEM)
    anywhere = pl.BlockSpec(memory_space=pl.ANY)

    def local(sections, fine_offsets, coarse_offset, tissue_mask):
        tile = sections[0]
        rows, width = tile.shape
        half = rows // 2
        assert rows // DOWN == P_SIZE and width // DOWN == P_SIZE and n_gx % GROUP == 0
        patch_rows, patch_cols = half // STRIDE, width // STRIDE
        dma = pltpu.SemaphoreType.DMA
        groups = patch_cols // GROUP
        units = patch_rows * groups
        wide = GROUP * P_SIZE
        flow = pl.pallas_call(
            lambda *refs: kernel(n_gx, n_gy, *refs),
            out_shape=pltpu.VMEM((2, patch_cols // 2, 2 * patch_rows), F32),
            in_specs=[anywhere] * (4 + len(tables)),
            out_specs=vmem,
            scratch_shapes=[pltpu.VMEM(t.shape, BF16) for t in tables]
            + [
                pltpu.VMEM((rows, width), BF16),
                pltpu.VMEM((2, half + P_SIZE, width + 128), BF16),
                pltpu.VMEM((n_gx, 2, HALF, 2 * P_SIZE), BF16),
                pltpu.VMEM((HALF, 2 * P_SIZE), BF16),
                pltpu.VMEM((2, patch_rows, 128), F32),
                pltpu.VMEM((2, patch_rows, 128), F32),
                pltpu.VMEM((2, 2 * groups, half + P_SIZE, wide // 2), F32),
                pltpu.VMEM((2, half + STRIDE, groups * wide), BF16),
                pltpu.VMEM((2, half + STRIDE, groups * wide), BF16),
                pltpu.VMEM((min(GROUP + 1, n_gx) * 4 * P_SIZE, wide), BF16),
                pltpu.VMEM((units, P_SIZE, wide), F32),
                pltpu.VMEM((units, wide), F32),
                pltpu.VMEM((2, units, wide), F32),
                dma((12,)),
                dma((12,)),
                dma((n_gx, 2)),
                dma((n_gx, 2)),
                dma((3,)),
                dma((len(tables),)),
                dma((2,)),
                pltpu.SMEM(fine_offsets.shape, jnp.int32),
                pltpu.SMEM((1,), jnp.int32),
                pltpu.VMEM(tissue_mask.shape, jnp.int32),
                dma((3,)),
            ],
            compiler_params=pltpu.CompilerParams(
                collective_id=0, has_side_effects=True, vmem_limit_bytes=VMEM_BYTES
            ),
            name="flow",
        )(fine_offsets, coarse_offset, tile, tissue_mask, *[jnp.asarray(t) for t in tables])
        return jnp.swapaxes(flow, 1, 2)[:, None]

    placed = (P("gz", ("pairs", "gy"), "gx"), P("pairs"), P("pairs"), P(("pairs", "gy"), "gx"))
    return jax.shard_map(
        local,
        mesh=mesh,
        in_specs=placed,
        out_specs=P(None, "gz", ("pairs", "gy"), "gx"),
        check_vma=False,
    )
```

```python
import jax
import jax.numpy as jnp
import numpy as np
from jax import lax
from jax.experimental import pallas as pl
from jax.experimental.pallas import tpu as pltpu
from jax.sharding import PartitionSpec as P

P_SIZE = 64
STRIDE = 32
DOWN = 8
HALF = P_SIZE // 2
GROUP = 4
SHARP = 12.0
BESIDE = 1
VMEM_BYTES = 56 * 2**20
MESH = pl.DeviceIdType.MESH
F32 = jnp.float32
BF16 = jnp.bfloat16


def split_table(table):
    high = np.asarray(table, np.float32).astype(jnp.bfloat16)
    low = (np.asarray(table, np.float64) - high.astype(np.float64)).astype(np.float32)
    return high, low.astype(jnp.bfloat16)


def make_tables():
    turn = 2.0 * np.pi / P_SIZE
    k = np.arange(HALF)
    x = np.arange(2 * GROUP * STRIDE)
    angle = turn * (np.outer(x, k) % P_SIZE)
    real = np.cos(angle)
    imag = -np.sin(angle)
    imag[:, 0] = np.cos(np.pi * x)
    forward_x = np.concatenate([np.tile(real, (1, GROUP)), np.tile(imag, (1, GROUP))], axis=1)
    high, low = split_table(forward_x)
    table_x = np.concatenate([high, low], axis=0)
    ky = np.arange(P_SIZE)
    angle = turn * (np.outer(ky, ky) % P_SIZE)
    high, low = split_table(np.concatenate([np.cos(angle), np.sin(angle)], axis=0))
    table_y = np.concatenate([high, low, high], axis=1)
    angle = turn * (np.outer(ky, ky) % P_SIZE)
    cosine, sine = np.cos(angle), np.sin(angle)
    inverse_y = np.block([[cosine, -sine], [sine, cosine]])
    high, low = split_table(inverse_y)
    table_iy = np.concatenate([high, low, high], axis=1)
    angle = turn * (np.outer(k, ky) % P_SIZE)
    real = 2.0 * np.cos(angle)
    imag = -2.0 * np.sin(angle)
    real[0] = 1.0
    imag[0] = np.cos(np.pi * ky)
    scale = SHARP * np.log2(np.e) / float(P_SIZE) ** 4
    eye = np.eye(GROUP)
    inverse_x = np.concatenate([np.kron(eye, real), np.kron(eye, imag)], axis=0) * scale
    high, low = split_table(inverse_x)
    table_ix = np.concatenate([high, high, low], axis=0)
    return table_x, table_y, table_iy, table_ix


def iota(shape, dim):
    return lax.broadcasted_iota(jnp.int32, shape, dim)


def two_terms(value):
    high = value.astype(BF16)
    return high, (value - high.astype(F32)).astype(BF16)


def bdot(a, b):
    return jnp.dot(a, b, preferred_element_type=F32)


def signed_of(index):
    return jnp.where(index >= HALF, index - P_SIZE, index).astype(F32)


def cis(turns):
    rest = turns - jnp.floor(turns + 0.5)
    a = rest * np.float32(np.pi)
    q = a * a
    s = np.float32(-1 / 39916800.0)
    for c in (1 / 362880.0, -1 / 5040.0, 1 / 120.0, -1 / 6.0, 1.0):
        s = s * q + np.float32(c)
    s = s * a
    c = np.float32(1 / 479001600.0)
    for d in (-1 / 3628800.0, 1 / 40320.0, -1 / 720.0, 1 / 24.0, -0.5, 1.0):
        c = c * q + np.float32(d)
    return 1.0 - 2.0 * s * s, 2.0 * s * c


def segment_max(value):
    width = value.shape[1]
    place = iota(value.shape, 1) & (P_SIZE - 1)
    step = 1
    while step < P_SIZE:
        near = pltpu.roll(value, step, 1)
        far = pltpu.roll(value, width - P_SIZE + step, 1)
        value = jnp.maximum(value, jnp.where(place >= step, near, far))
        step *= 2
    return value


def forward_y(table, spectrum_x):
    high, low = two_terms(spectrum_x)
    return bdot(table, jnp.concatenate([high, high, low], axis=0))


def planes(product, unit):
    base = unit * 2 * P_SIZE
    lanes = GROUP * HALF
    cosine = product[base : base + P_SIZE]
    sine = product[base + P_SIZE : base + 2 * P_SIZE]
    return cosine[:, :lanes], sine[:, :lanes], cosine[:, lanes:], sine[:, lanes:]


def cross(first, second, unit, nyquist):
    a1, a2, a3, a4 = planes(first, unit)
    b1, b2, b3, b4 = planes(second, unit)
    ar = a1 + jnp.where(nyquist, 0.0, a4)
    ai = jnp.where(nyquist, 0.0, a3) - a2
    br = b1 + jnp.where(nyquist, 0.0, b4)
    bi = jnp.where(nyquist, 0.0, b3) - b2
    return (br * ar + bi * ai, bi * ar - br * ai, b3 * a3 + b4 * a4, b3 * a4 - b4 * a3)


def landscape(units, table_iy, table_ix):
    stacked = []
    for zr, zi in units:
        high, low = two_terms(jnp.concatenate([zr, zi], axis=0))
        stacked.append(jnp.concatenate([high, high, low], axis=0))
    back = bdot(table_iy, jnp.concatenate(stacked, axis=1) if len(stacked) > 1 else stacked[0])
    lanes = GROUP * HALF
    rows = []
    for unit in range(len(units)):
        piece = back[:, unit * lanes : (unit + 1) * lanes]
        rows.append(jnp.concatenate([piece[:P_SIZE], piece[P_SIZE:]], axis=1))
    value = jnp.concatenate(rows, axis=0) if len(rows) > 1 else rows[0]
    high, low = two_terms(value)
    return bdot(jnp.concatenate([high, low, high], axis=1), table_ix)


def exact_dot(a, b):
    terms = []
    for _ in range(3):
        terms.append(a.astype(BF16))
        a = a - terms[-1].astype(F32)
    return bdot(jnp.concatenate(terms, axis=1), jnp.concatenate([b, b, b], axis=0))


def kernel(
    n_gx, n_gy, fine_hbm, coarse_hbm, tile_hbm, mask_hbm, *rest
):
    hbm_tables, (out,), scratch = rest[:4], rest[4:5], rest[5:]
    table_refs, scratch = scratch[:4], scratch[4:]
    (tile, ext, coarse, own, given, got, spec, spec_high, spec_low, ctab, logits, peaks, stats) = scratch[:13]
    send_sem, recv_sem, csend, crecv, local_sem, table_sem, back_sem = scratch[13:20]
    fine_off, coarse_off, mask, small_sem, packs, landed, crossed = scratch[20:27]
    mine, flows, fsend, frecv, known = scratch[27:]
    tx, ty, tiy_ref, tix_ref = table_refs
    pairs, gx, gy, gz = (lax.axis_index(a) for a in ("pairs", "gx", "gy", "gz"))
    rows, width = tile.shape
    half = rows // 2
    edge = ext.shape[2] - width

    def device(x, y, z):
        return (pairs, x, y, z)

    load = pltpu.make_async_copy(tile_hbm, tile, local_sem.at[2])
    load.start()
    small_copies = [
        pltpu.make_async_copy(source, target, small_sem.at[n])
        for n, (source, target) in enumerate(
            ((fine_hbm, fine_off), (coarse_hbm, coarse_off), (mask_hbm, mask))
        )
    ]
    for copy in small_copies:
        copy.start()

    barrier = pltpu.get_barrier_semaphore()
    greeted = [(gx, gy, 1 - gz, None), (gx - 1, gy, gz, gx >= 1)]
    for z in range(2):
        greeted.append((gx + 1, gy, z, gx + 1 < n_gx))
    for x in (gx, gx + 1):
        for z in range(2):
            greeted.append((x, gy + 1, z, (gz == 1) & (gy + 1 < n_gy) & (x < n_gx)))
    for x, y, z, use in greeted:

        def greet():
            pl.semaphore_signal(barrier, inc=1, device_id=device(x, y, z), device_id_type=MESH)

        if use is None:
            greet()
        else:
            pl.when(use)(greet)

    has_left = jnp.where(gx >= 1, 1, 0)
    count = 1 + 2 * has_left + jnp.where(gx + 1 < n_gx, 1, 0) + jnp.where(gy >= 1, 1 + has_left, 0)

    table_copies = [
        pltpu.make_async_copy(source, target, table_sem.at[n])
        for n, (source, target) in enumerate(zip(hbm_tables, table_refs))
    ]
    for copy in table_copies:
        copy.start()
    first_half = pltpu.make_async_copy(
        tile_hbm.at[pl.ds(0, half + P_SIZE), :],
        ext.at[0, pl.ds(0, half + P_SIZE), pl.ds(0, width)],
        local_sem.at[0],
    )
    second_half = pltpu.make_async_copy(
        tile_hbm.at[pl.ds(half, half), :], ext.at[1, pl.ds(0, half), pl.ds(0, width)], local_sem.at[1]
    )

    @pl.when(gz == 0)
    def _():
        first_half.start()

    @pl.when(gz == 1)
    def _():
        second_half.start()

    pool_rows = jnp.where((iota((rows // DOWN, rows), 1) >> 3) == iota((rows // DOWN, rows), 0), 1.0, 0.0)
    lanes = iota((width, 2 * P_SIZE), 1)
    block = iota((width, 2 * P_SIZE), 0) >> 3
    pool = jnp.where(block == (lanes & (P_SIZE - 1)), 1.0, 0.0).astype(BF16)
    pool_rows = pool_rows.astype(BF16)
    load.wait()
    piece = bdot(pool_rows, tile[...])
    terms = []
    for _ in range(3):
        terms.append(piece.astype(BF16))
        piece = piece - terms[-1].astype(F32)
    packed = bdot(jnp.concatenate(terms, axis=1), jnp.concatenate([pool] * 3, axis=0))
    packed = jnp.where(iota((HALF, 2 * P_SIZE), 1) < P_SIZE, packed[:HALF], packed[HALF:])
    packed = (packed * (1.0 / DOWN)).astype(BF16)
    own[...] = packed
    coarse[0, gz] = packed

    @pl.when(gx + 1 >= n_gx)
    def _():
        ext[:, :, width:] = jnp.zeros((2, half + P_SIZE, edge), BF16)
        coarse[1] = jnp.zeros(coarse.shape[1:], BF16)

    @pl.when((gz == 1) & (gy + 1 >= n_gy))
    def _():
        ext[:, half:, :width] = jnp.zeros((2, P_SIZE, width), BF16)
        ext[:, half:, width:] = jnp.zeros((2, P_SIZE, edge), BF16)

    pl.semaphore_wait(barrier, count)

    long, short = half // 2, P_SIZE // 2

    def halo_copy(kind, c, section, x, y):
        if c == 0:
            source, target = (
                (pl.ds(0, half + P_SIZE), pl.ds(0, half + P_SIZE)),
                (pl.ds(half, half), pl.ds(0, half)),
                (pl.ds(0, P_SIZE), pl.ds(half, P_SIZE)),
            )[kind]
            source = tile.at[source, :]
            target = ext.at[section, target, pl.ds(0, width)]
        else:
            source, target = (
                (pl.ds(0, long + short), pl.ds(0, long + short)),
                (pl.ds(long + short, long), pl.ds(0, long)),
                (pl.ds(2 * long + short, short), pl.ds(long, short)),
            )[kind]
            source = packs.at[source, :]
            target = landed.at[section, target, :]
        slot = kind * 4 + c * 2
        return pltpu.make_async_remote_copy(
            src_ref=source,
            dst_ref=target,
            send_sem=send_sem.at[slot],
            recv_sem=recv_sem.at[slot + section],
            device_id=device(x, y, 0 if kind == 0 else 1),
            device_id_type=MESH,
        )

    def coarse_copy(n, place, section):
        return pltpu.make_async_remote_copy(
            src_ref=own,
            dst_ref=coarse.at[place, section],
            send_sem=csend.at[n],
            recv_sem=crecv.at[place, section],
            device_id=device(gx, gy, 1 - gz) if n == 2 else device(gx - 1, gy, n),
            device_id_type=MESH,
        )

    coarse_copy(2, 0, gz).start()

    @pl.when(gx >= 1)
    def _():
        for n in range(2):
            coarse_copy(n, 1, gz).start()

    def tell(way, n):
        x = gx + 1 if way == 0 else gx - 1

        @pl.when((x >= 0) & (x < n_gx))
        def _():
            pl.semaphore_signal(
                known.at[way, n], inc=1, device_id=device(x, gy, gz), device_id_type=MESH
            )

    def relay(way):
        for n in range(n_gx - 1):
            behind = gx - 1 - n if way == 0 else gx + 1 + n

            @pl.when((behind >= 0) & (behind < n_gx))
            def _():
                if n:
                    pl.semaphore_wait(known.at[way, n - 1], 1)
                if n < n_gx - 2:
                    tell(way, n)

    relay(0)

    def sends():
        out = []
        for c in (0, 1):
            for kind in range(3):
                use = gx - c >= 0
                if kind == 2:
                    use = use & (gy - 1 >= 0)
                elif c == 0:
                    use = use & (gz != kind)
                out.append((use, kind, c, gx - c, gy - 1 if kind == 2 else gy))
        return out

    for use, kind, c, x, y in sends():
        if c == 0:

            @pl.when(use)
            def _():
                halo_copy(kind, c, gz, x, y).start()

    @pl.when(gx >= 1)
    def _():
        put = 0
        for top, size in ((0, long), (half, short), (half, long), (0, short)):
            upper = tile[top : top + size, :128].astype(F32)
            lower = tile[top + size : top + 2 * size, :128].astype(F32)
            both = jnp.where(iota((size, 128), 1) < P_SIZE, upper, pltpu.roll(lower, P_SIZE, 1))
            packs[put : put + size] = both.astype(BF16)
            put += size

    for use, kind, c, x, y in sends():
        if c == 1:

            @pl.when(use)
            def _():
                halo_copy(kind, c, gz, x, y).start()

    def arrivals(c, kinds):
        for section in range(2):
            for kind in kinds:
                use = (gz == 0) if kind == 0 else (gz == 1)
                if c == 1:
                    use = use & (gx + 1 < n_gx)
                if kind == 2:
                    use = use & (gy + 1 < n_gy)
                elif c == 0:
                    use = use & (gz != section)

                @pl.when(use)
                def _():
                    halo_copy(kind, c, section, gx, gy).wait_recv()

    tile_width = mask.shape[1] * STRIDE
    patch_rows = half // STRIDE
    groups = mask.shape[1] // GROUP
    lanes = GROUP * HALF
    wide = GROUP * P_SIZE
    for copy in small_copies:
        copy.wait()
    roff, coff, off = fine_off[0], fine_off[1], coarse_off[0]
    for copy in table_copies:
        copy.wait()
    table_iy, table_ix = tiy_ref[...], tix_ref[...]

    span = tx.shape[0] // 2
    at = iota((span, 2 * lanes), 0) - coff - STRIDE * ((iota((span, 2 * lanes), 1) >> 5) & (GROUP - 1))
    inside = jnp.where((at >= 0) & (at < P_SIZE), 1.0, 0.0).astype(BF16)
    block = (2 * P_SIZE, 2 * lanes)
    from_left = (iota(block, 0) & (P_SIZE - 1)) - P_SIZE * ((iota(block, 1) >> 5) & (GROUP - 1)) - off
    plain = [tx[0 : 2 * P_SIZE], tx[span : span + 2 * P_SIZE]]
    for step in range(2):
        at_step = from_left + step * P_SIZE
        keep = jnp.where((at_step >= 0) & (at_step < P_SIZE), 1.0, 0.0).astype(BF16)
        for term in range(2):
            base = (2 * step + term) * 2 * P_SIZE
            ctab[base : base + 2 * P_SIZE] = plain[term] * keep
    tx[0:span] = tx[0:span] * inside
    tx[span:] = tx[span:] * inside

    nyquist = (iota((P_SIZE, lanes), 1) & (HALF - 1)) == 0
    frow = signed_of(iota((P_SIZE, wide), 0))

    def along_x_of(section, top, size, g):
        data = ext[section, pl.ds(top, size), g * lanes : g * lanes + span]
        value = bdot(jnp.concatenate([data, data], axis=1), tx[...])
        spec[section, 2 * g, pl.ds(top, size), :] = value[:, :lanes]
        spec[section, 2 * g + 1, pl.ds(top, size), :] = value[:, lanes:]

    inner = groups - 1

    @pl.when(gz == 0)
    def _():
        first_half.wait()

    @pl.when(gz == 1)
    def _():
        second_half.wait()

    for g in range(inner):
        along_x_of(gz, 0, half, g)

    arrivals(0, (0, 1))
    for g in range(inner):
        along_x_of(1 - gz, 0, half, g)

    def split(g, top, size):
        for section in range(2):
            for t in range(2):
                high, low = two_terms(spec[section, 2 * g + t, pl.ds(roff + top, size), :])
                part = slice((2 * g + t) * lanes, (2 * g + t + 1) * lanes)
                spec_high[section, top : top + size, part] = high
                spec_low[section, top : top + size, part] = low

    def forward(g, first_row, last_row):
        part = slice(g * 2 * lanes, (g + 1) * 2 * lanes)
        for row in range(first_row, last_row):
            window = slice(row * STRIDE, row * STRIDE + P_SIZE)
            first, second = (
                bdot(
                    ty[...],
                    jnp.concatenate(
                        [
                            spec_high[t, window, part],
                            spec_high[t, window, part],
                            spec_low[t, window, part],
                        ],
                        axis=0,
                    ),
                )
                for t in range(2)
            )
            for n, plane in enumerate(cross(first, second, 0, nyquist)):
                crossed[g * patch_rows + row, n] = plane
            yield

    upper_rows, middle_row = patch_rows - 2, half - STRIDE

    def upper(g):
        split(g, 0, middle_row)
        yield from forward(g, 0, upper_rows)

    def lower(g):
        split(g, middle_row, P_SIZE)
        yield from forward(g, upper_rows, patch_rows)

    def last_columns():
        for below in range(2):
            use = gx + 1 < n_gx
            if below:
                use = use & ((gz == 0) | (gy + 1 < n_gy))

            @pl.when(use)
            def _():
                for section in range(2):
                    top, size, source = (half, short, long) if below else (0, long, 0)
                    data = landed[section, source : source + size]
                    ext[section, top : top + size, width:] = data
                    data = pltpu.roll(data.astype(F32), P_SIZE, 1).astype(BF16)
                    ext[section, top + size : top + 2 * size, width:] = data

        for section in range(2):
            along_x_of(section, 0, half + P_SIZE, inner)

    coarse_copy(2, 0, 1 - gz).wait_recv()

    @pl.when(gx + 1 < n_gx)
    def _():
        for section in range(2):
            coarse_copy(0, 1, section).wait_recv()

    beside = upper(0)

    def step(count):
        for _ in range(count):
            next(beside, None)

    left = iota((HALF, 2 * P_SIZE), 1) < P_SIZE
    ones = jnp.where((iota((wide, 128), 0) >> 6) == 0, 1.0, 0.0).astype(BF16)
    fcol = signed_of(iota((1, wide), 1) & (P_SIZE - 1))
    lines = []
    for section in range(2):
        terms = []
        for source in range(2):
            data = coarse[source, section].astype(F32)
            both = jnp.concatenate(
                [jnp.where(left, data, 0.0), jnp.where(left, 0.0, data)], axis=0
            ).astype(BF16)
            terms += [both, both]
        lines.append(jnp.concatenate(terms, axis=1))
    value = bdot(jnp.concatenate(lines, axis=0), ctab[...])
    step(BESIDE)
    first = forward_y(ty[...], value[:P_SIZE])
    second = forward_y(ty[...], value[P_SIZE:])
    step(BESIDE)
    hr, hi, yr, yi = cross(first, second, 0, nyquist)
    value = landscape(
        [(hr - jnp.where(nyquist, yi, 0.0), hi + jnp.where(nyquist, yr, 0.0))], table_iy, table_ix
    )
    step(BESIDE)
    top = segment_max(jnp.broadcast_to(jnp.max(value, axis=0, keepdims=True), (8, wide)))[0:1]
    step(BESIDE)
    weight = jnp.exp2(value - top)
    s0 = jnp.sum(weight, axis=0, keepdims=True)
    s1 = jnp.sum(weight * frow, axis=0, keepdims=True)
    rows = iota((8, wide), 0)
    both = jnp.where(rows == 0, s0, jnp.where(rows == 1, s1, jnp.where(rows == 2, s0 * fcol, 0.0)))
    total = exact_dot(both, ones)
    rows = iota((8, 128), 0)
    found = jnp.where(rows == 0, total[1:2] / total[0:1], total[2:3] / total[0:1])
    mine[...] = found
    flows[gx] = found

    def flow_copy(x, place):
        return pltpu.make_async_remote_copy(
            src_ref=mine,
            dst_ref=flows.at[place],
            send_sem=fsend.at[x],
            recv_sem=frecv.at[place],
            device_id=device(x, gy, gz),
            device_id_type=MESH,
        )

    relay(1)
    for x in range(n_gx):

        @pl.when(x != gx)
        def _():
            flow_copy(x, gx).start()

    for _ in beside:
        pass
    for g in range(1, inner):
        for _ in upper(g):
            pass
    arrivals(0, (2,))
    for g in range(inner):
        for section in range(2):
            along_x_of(section, half, P_SIZE, g)
    for g in range(inner):
        for _ in lower(g):
            pass
    arrivals(1, (0, 1, 2))
    last_columns()
    for part in (upper, lower):
        for _ in part(inner):
            pass

    for x in range(n_gx):

        @pl.when(x != gx)
        def _():
            flow_copy(x, x).wait_recv()

    mean = sum(flows[x] for x in range(n_gx)) / float(n_gx)
    blended = [(0.5 * DOWN) * (flows[x] + mean) for x in range(n_gx)]

    def pick(column):
        centre = gx * tile_width + column * STRIDE + coff + P_SIZE // 2
        chosen = jnp.clip(((centre >> 3) - off) >> 6, 0, n_gx - 1)
        total = blended[0]
        for x in range(1, n_gx):
            total = jnp.where(chosen == x, blended[x], total)
        return total

    fky = signed_of(iota((P_SIZE, lanes), 0)) * (1.0 / P_SIZE)
    middle = iota((P_SIZE, lanes), 0) == HALF
    kx = (iota((1, lanes), 1) & (HALF - 1)).astype(F32) * (1.0 / P_SIZE)

    def backward(g):
        prior = pick(g * GROUP + (iota((8, lanes), 1) >> 5))
        dy, dx = prior[0:1], prior[1:2]
        eyr, eyi = cis(fky * dy)
        exr, exi = cis(kx * dx)
        nr, ni = cis(0.5 * dx)
        fr = jnp.where(nyquist, nr * eyr + jnp.where(middle, ni * eyi, 0.0), 0.0)
        eyi = jnp.where(middle, 0.0, eyi)
        fi = jnp.where(nyquist, nr * eyi, 0.0)
        er = eyr * exr - eyi * exi
        ei = eyr * exi + eyi * exr
        for q in range(patch_rows // GROUP):
            base = g * patch_rows + q * GROUP
            units = []
            for unit in range(GROUP):
                xr, xi, yr, yi = (crossed[base + unit, n] for n in range(4))
                hr = xr * er - xi * ei
                hi = xr * ei + xi * er
                units.append((hr - (yr * fi + yi * fr), hi + (yr * fr - yi * fi)))
            value = landscape(units, table_iy, table_ix)
            for unit in range(GROUP):
                piece = value[unit * P_SIZE : (unit + 1) * P_SIZE]
                logits[base + unit] = piece
                peaks[base + unit : base + unit + 1] = jnp.max(piece, axis=0, keepdims=True)

    for g in range(groups):
        backward(g)

    peaks[...] = segment_max(peaks[...])

    def weigh(n, carry):
        weight = jnp.exp2(logits[n] - peaks[pl.ds(n, 1)])
        stats[0, pl.ds(n, 1)] = jnp.sum(weight, axis=0, keepdims=True)
        stats[1, pl.ds(n, 1)] = jnp.sum(weight * frow, axis=0, keepdims=True)
        return carry

    lax.fori_loop(0, groups * patch_rows, weigh, 0, unroll=4)

    columns = mask.shape[1]
    side = columns // 2

    def lane_of(column):
        return (column & 1) * side + (column >> 1)

    put = jnp.where(lane_of(iota((wide, 128), 0) >> 6) == iota((wide, 128), 1), 1.0, 0.0)
    s0 = stats[0]
    sums = exact_dot(jnp.concatenate([s0, stats[1], s0 * fcol], axis=0), put.astype(BF16))
    units = groups * patch_rows

    def gather(stat):
        total = None
        for g in range(groups):
            piece = sums[stat * units + g * patch_rows : stat * units + (g + 1) * patch_rows]
            if g:
                piece = pltpu.roll(piece, g * GROUP // 2, 1)
            total = piece if total is None else total + piece
        return total

    den, along_y, along_x = gather(0), gather(1), gather(2)
    lane = iota((8, 128), 1)
    prior = pick(jnp.where(lane < side, 2 * lane, jnp.minimum(2 * (lane - side) + 1, columns - 1)))
    here = pl.ds(pl.multiple_of(gz * patch_rows, 8), patch_rows)
    place = jnp.where(lane_of(iota((columns, 128), 0)) == iota((columns, 128), 1), 1.0, 0.0)
    valid = bdot(mask[here, :].astype(F32).astype(BF16), place.astype(BF16))
    den = jnp.where(iota((patch_rows, 128), 1) < columns, den, 1.0)
    same = ((iota((patch_rows, 128), 0) + gz) & 1) == 0
    kept = []
    for c, total in enumerate((along_y, along_x)):
        value = prior[c : c + 1] + valid * (total / den)
        odd = pltpu.roll(value, 128 - side, 1)
        given[c] = jnp.where(same, odd, value)
        kept.append(jnp.where(same, value, odd))
    back = pltpu.make_async_remote_copy(
        src_ref=given,
        dst_ref=got,
        send_sem=back_sem.at[0],
        recv_sem=back_sem.at[1],
        device_id=device(gx, gy, 1 - gz),
        device_id_type=MESH,
    )
    back.start()
    coarse_copy(2, 0, gz).wait_send()

    @pl.when(gx >= 1)
    def _():
        for n in range(2):
            coarse_copy(n, 1, gz).wait_send()

    for x in range(n_gx):

        @pl.when(x != gx)
        def _():
            flow_copy(x, gx).wait_send()

    for use, kind, c, x, y in sends():

        @pl.when(use)
        def _():
            halo_copy(kind, c, gz, x, y).wait_send()

    back.wait()
    upper = jnp.full((patch_rows, 128), gz, jnp.int32) == 0
    for c in range(2):
        value = jnp.concatenate(
            [jnp.where(upper, kept[c], got[c]), jnp.where(upper, got[c], kept[c])], axis=0
        )
        out[c] = jnp.transpose(value)[:side]


def solution(mesh):
    n_gx, n_gy = mesh.shape["gx"], mesh.shape["gy"]
    tables = make_tables()
    vmem = pl.BlockSpec(memory_space=pltpu.VMEM)
    anywhere = pl.BlockSpec(memory_space=pl.ANY)

    def local(sections, fine_offsets, coarse_offset, tissue_mask):
        tile = sections[0]
        rows, width = tile.shape
        half = rows // 2
        assert rows // DOWN == P_SIZE and width // DOWN == P_SIZE and n_gx % GROUP == 0
        patch_rows, patch_cols = half // STRIDE, width // STRIDE
        dma = pltpu.SemaphoreType.DMA
        groups = patch_cols // GROUP
        units = patch_rows * groups
        wide = GROUP * P_SIZE
        flow = pl.pallas_call(
            lambda *refs: kernel(n_gx, n_gy, *refs),
            out_shape=pltpu.VMEM((2, patch_cols // 2, 2 * patch_rows), F32),
            in_specs=[anywhere] * (4 + len(tables)),
            out_specs=vmem,
            scratch_shapes=[pltpu.VMEM(t.shape, BF16) for t in tables]
            + [
                pltpu.VMEM((rows, width), BF16),
                pltpu.VMEM((2, half + P_SIZE, width + 128), BF16),
                pltpu.VMEM((2, 2, HALF, 2 * P_SIZE), BF16),
                pltpu.VMEM((HALF, 2 * P_SIZE), BF16),
                pltpu.VMEM((2, patch_rows, 128), F32),
                pltpu.VMEM((2, patch_rows, 128), F32),
                pltpu.VMEM((2, 2 * groups, half + P_SIZE, wide // 2), F32),
                pltpu.VMEM((2, half + STRIDE, groups * wide), BF16),
                pltpu.VMEM((2, half + STRIDE, groups * wide), BF16),
                pltpu.VMEM((8 * P_SIZE, wide), BF16),
                pltpu.VMEM((units, P_SIZE, wide), F32),
                pltpu.VMEM((units, wide), F32),
                pltpu.VMEM((2, units, wide), F32),
                dma((12,)),
                dma((12,)),
                dma((3,)),
                dma((2, 2)),
                dma((3,)),
                dma((len(tables),)),
                dma((2,)),
                pltpu.SMEM(fine_offsets.shape, jnp.int32),
                pltpu.SMEM((1,), jnp.int32),
                pltpu.VMEM(tissue_mask.shape, jnp.int32),
                dma((3,)),
                pltpu.VMEM((half + P_SIZE, 128), BF16),
                pltpu.VMEM((2, (half + P_SIZE) // 2, 128), BF16),
                pltpu.VMEM((units, 4, P_SIZE, wide // 2), F32),
                pltpu.VMEM((8, 128), F32),
                pltpu.VMEM((n_gx, 8, 128), F32),
                dma((n_gx,)),
                dma((n_gx,)),
                pltpu.SemaphoreType.REGULAR((2, n_gx)),
            ],
            compiler_params=pltpu.CompilerParams(
                collective_id=0, has_side_effects=True, vmem_limit_bytes=VMEM_BYTES
            ),
            name="flow",
        )(fine_offsets, coarse_offset, tile, tissue_mask, *[jnp.asarray(t) for t in tables])
        return jnp.swapaxes(flow, 1, 2)[:, None]

    placed = (P("gz", ("pairs", "gy"), "gx"), P("pairs"), P("pairs"), P(("pairs", "gy"), "gx"))
    return jax.shard_map(
        local,
        mesh=mesh,
        in_specs=placed,
        out_specs=P(None, "gz", ("pairs", "gy"), "gx"),
        check_vma=False,
    )
```

```python
import jax
import jax.numpy as jnp
import numpy as np
from jax import lax
from jax.experimental import pallas as pl
from jax.experimental.pallas import tpu as pltpu
from jax.sharding import PartitionSpec as P

P_SIZE = 64
STRIDE = 32
DOWN = 8
HALF = P_SIZE // 2
GROUP = 4
SHARP = 12.0
BESIDE = 1
VMEM_BYTES = 56 * 2**20
MESH = pl.DeviceIdType.MESH
F32 = jnp.float32
BF16 = jnp.bfloat16


def split_table(table):
    high = np.asarray(table, np.float32).astype(jnp.bfloat16)
    low = (np.asarray(table, np.float64) - high.astype(np.float64)).astype(np.float32)
    return high, low.astype(jnp.bfloat16)


def make_tables():
    turn = 2.0 * np.pi / P_SIZE
    k = np.arange(HALF)
    x = np.arange(2 * GROUP * STRIDE)
    angle = turn * (np.outer(x, k) % P_SIZE)
    real = np.cos(angle)
    imag = -np.sin(angle)
    imag[:, 0] = np.cos(np.pi * x)
    forward_x = np.concatenate([np.tile(real, (1, GROUP)), np.tile(imag, (1, GROUP))], axis=1)
    high, low = split_table(forward_x)
    table_x = np.concatenate([high, low], axis=0)
    ky = np.arange(P_SIZE)
    angle = turn * (np.outer(ky, ky) % P_SIZE)
    high, low = split_table(np.concatenate([np.cos(angle), np.sin(angle)], axis=0))
    table_y = np.concatenate([high, low, high], axis=1)
    angle = turn * (np.outer(ky, ky) % P_SIZE)
    cosine, sine = np.cos(angle), np.sin(angle)
    inverse_y = np.block([[cosine, -sine], [sine, cosine]])
    high, low = split_table(inverse_y)
    table_iy = np.concatenate([high, low, high], axis=1)
    angle = turn * (np.outer(k, ky) % P_SIZE)
    real = 2.0 * np.cos(angle)
    imag = -2.0 * np.sin(angle)
    real[0] = 1.0
    imag[0] = np.cos(np.pi * ky)
    scale = SHARP * np.log2(np.e) / float(P_SIZE) ** 4
    eye = np.eye(GROUP)
    inverse_x = np.concatenate([np.kron(eye, real), np.kron(eye, imag)], axis=0) * scale
    high, low = split_table(inverse_x)
    table_ix = np.concatenate([high, high, low], axis=0)
    return table_x, table_y, table_iy, table_ix


def iota(shape, dim):
    return lax.broadcasted_iota(jnp.int32, shape, dim)


def two_terms(value):
    high = value.astype(BF16)
    return high, (value - high.astype(F32)).astype(BF16)


def bdot(a, b):
    return jnp.dot(a, b, preferred_element_type=F32)


def signed_of(index):
    return jnp.where(index >= HALF, index - P_SIZE, index).astype(F32)


def cis(turns):
    rest = turns - jnp.floor(turns + 0.5)
    a = rest * np.float32(np.pi)
    q = a * a
    s = np.float32(-1 / 39916800.0)
    for c in (1 / 362880.0, -1 / 5040.0, 1 / 120.0, -1 / 6.0, 1.0):
        s = s * q + np.float32(c)
    s = s * a
    c = np.float32(1 / 479001600.0)
    for d in (-1 / 3628800.0, 1 / 40320.0, -1 / 720.0, 1 / 24.0, -0.5, 1.0):
        c = c * q + np.float32(d)
    return 1.0 - 2.0 * s * s, 2.0 * s * c


def segment_max(value):
    width = value.shape[1]
    place = iota(value.shape, 1) & (P_SIZE - 1)
    step = 1
    while step < P_SIZE:
        near = pltpu.roll(value, step, 1)
        far = pltpu.roll(value, width - P_SIZE + step, 1)
        value = jnp.maximum(value, jnp.where(place >= step, near, far))
        step *= 2
    return value


def forward_y(table, spectrum_x):
    high, low = two_terms(spectrum_x)
    return bdot(table, jnp.concatenate([high, high, low], axis=0))


def planes(product, unit):
    base = unit * 2 * P_SIZE
    lanes = GROUP * HALF
    cosine = product[base : base + P_SIZE]
    sine = product[base + P_SIZE : base + 2 * P_SIZE]
    return cosine[:, :lanes], sine[:, :lanes], cosine[:, lanes:], sine[:, lanes:]


def cross(first, second, unit, nyquist):
    a1, a2, a3, a4 = planes(first, unit)
    b1, b2, b3, b4 = planes(second, unit)
    ar = a1 + jnp.where(nyquist, 0.0, a4)
    ai = jnp.where(nyquist, 0.0, a3) - a2
    br = b1 + jnp.where(nyquist, 0.0, b4)
    bi = jnp.where(nyquist, 0.0, b3) - b2
    return (br * ar + bi * ai, bi * ar - br * ai, b3 * a3 + b4 * a4, b3 * a4 - b4 * a3)


def landscape(units, table_iy, table_ix):
    stacked = []
    for zr, zi in units:
        high, low = two_terms(jnp.concatenate([zr, zi], axis=0))
        stacked.append(jnp.concatenate([high, high, low], axis=0))
    back = bdot(table_iy, jnp.concatenate(stacked, axis=1) if len(stacked) > 1 else stacked[0])
    lanes = GROUP * HALF
    rows = []
    for unit in range(len(units)):
        piece = back[:, unit * lanes : (unit + 1) * lanes]
        rows.append(jnp.concatenate([piece[:P_SIZE], piece[P_SIZE:]], axis=1))
    value = jnp.concatenate(rows, axis=0) if len(rows) > 1 else rows[0]
    high, low = two_terms(value)
    return bdot(jnp.concatenate([high, low, high], axis=1), table_ix)


def exact_dot(a, b):
    terms = []
    for _ in range(3):
        terms.append(a.astype(BF16))
        a = a - terms[-1].astype(F32)
    return bdot(jnp.concatenate(terms, axis=1), jnp.concatenate([b, b, b], axis=0))


def kernel(
    n_gx, n_gy, fine_hbm, coarse_hbm, tile_hbm, mask_hbm, *rest
):
    hbm_tables, (out,), scratch = rest[:4], rest[4:5], rest[5:]
    table_refs, scratch = scratch[:4], scratch[4:]
    (tile, ext, coarse, own, given, got, spec, spec_high, spec_low, ctab, logits, peaks, stats) = scratch[:13]
    send_sem, recv_sem, csend, crecv, local_sem, table_sem, back_sem = scratch[13:20]
    fine_off, coarse_off, mask, small_sem, packs, landed, crossed = scratch[20:27]
    mine, flows, fsend, frecv, known = scratch[27:]
    tx, ty, tiy_ref, tix_ref = table_refs
    pairs, gx, gy, gz = (lax.axis_index(a) for a in ("pairs", "gx", "gy", "gz"))
    rows, width = tile.shape
    half = rows // 2
    edge = ext.shape[2] - width

    def device(x, y, z):
        return (pairs, x, y, z)

    load = pltpu.make_async_copy(tile_hbm, tile, local_sem.at[2])
    load.start()
    small_copies = [
        pltpu.make_async_copy(source, target, small_sem.at[n])
        for n, (source, target) in enumerate(
            ((fine_hbm, fine_off), (coarse_hbm, coarse_off), (mask_hbm, mask))
        )
    ]
    for copy in small_copies:
        copy.start()

    barrier = pltpu.get_barrier_semaphore()
    greeted = [(gx, gy, 1 - gz, None), (gx - 1, gy, gz, gx >= 1)]
    for z in range(2):
        greeted.append((gx + 1, gy, z, gx + 1 < n_gx))
    for x in (gx, gx + 1):
        for z in range(2):
            greeted.append((x, gy + 1, z, (gz == 1) & (gy + 1 < n_gy) & (x < n_gx)))
    for x, y, z, use in greeted:

        def greet():
            pl.semaphore_signal(barrier, inc=1, device_id=device(x, y, z), device_id_type=MESH)

        if use is None:
            greet()
        else:
            pl.when(use)(greet)

    has_left = jnp.where(gx >= 1, 1, 0)
    count = 1 + 2 * has_left + jnp.where(gx + 1 < n_gx, 1, 0) + jnp.where(gy >= 1, 1 + has_left, 0)

    table_copies = [
        pltpu.make_async_copy(source, target, table_sem.at[n])
        for n, (source, target) in enumerate(zip(hbm_tables, table_refs))
    ]
    for copy in table_copies:
        copy.start()
    first_half = pltpu.make_async_copy(
        tile_hbm.at[pl.ds(0, half + P_SIZE), :],
        ext.at[0, pl.ds(0, half + P_SIZE), pl.ds(0, width)],
        local_sem.at[0],
    )
    second_half = pltpu.make_async_copy(
        tile_hbm.at[pl.ds(half, half), :], ext.at[1, pl.ds(0, half), pl.ds(0, width)], local_sem.at[1]
    )

    @pl.when(gz == 0)
    def _():
        first_half.start()

    @pl.when(gz == 1)
    def _():
        second_half.start()

    pool_rows = jnp.where((iota((rows // DOWN, rows), 1) >> 3) == iota((rows // DOWN, rows), 0), 1.0, 0.0)
    lanes = iota((width, 2 * P_SIZE), 1)
    block = iota((width, 2 * P_SIZE), 0) >> 3
    pool = jnp.where(block == (lanes & (P_SIZE - 1)), 1.0, 0.0).astype(BF16)
    pool_rows = pool_rows.astype(BF16)
    load.wait()
    piece = bdot(pool_rows, tile[...])
    terms = []
    for _ in range(3):
        terms.append(piece.astype(BF16))
        piece = piece - terms[-1].astype(F32)
    packed = bdot(jnp.concatenate(terms, axis=1), jnp.concatenate([pool] * 3, axis=0))
    packed = jnp.where(iota((HALF, 2 * P_SIZE), 1) < P_SIZE, packed[:HALF], packed[HALF:])
    packed = (packed * (1.0 / DOWN)).astype(BF16)
    own[...] = packed
    coarse[0, gz] = packed

    @pl.when(gx + 1 >= n_gx)
    def _():
        ext[:, :, width:] = jnp.zeros((2, half + P_SIZE, edge), BF16)
        coarse[1] = jnp.zeros(coarse.shape[1:], BF16)

    @pl.when((gz == 1) & (gy + 1 >= n_gy))
    def _():
        ext[:, half:, :width] = jnp.zeros((2, P_SIZE, width), BF16)
        ext[:, half:, width:] = jnp.zeros((2, P_SIZE, edge), BF16)

    pl.semaphore_wait(barrier, count)

    long, short = half // 2, P_SIZE // 2

    def halo_copy(kind, c, section, x, y):
        if c == 0:
            source, target = (
                (pl.ds(0, half + P_SIZE), pl.ds(0, half + P_SIZE)),
                (pl.ds(half, half), pl.ds(0, half)),
                (pl.ds(0, P_SIZE), pl.ds(half, P_SIZE)),
            )[kind]
            source = tile.at[source, :]
            target = ext.at[section, target, pl.ds(0, width)]
        else:
            source, target = (
                (pl.ds(0, long + short), pl.ds(0, long + short)),
                (pl.ds(long + short, long), pl.ds(0, long)),
                (pl.ds(2 * long + short, short), pl.ds(long, short)),
            )[kind]
            source = packs.at[source, :]
            target = landed.at[section, target, :]
        slot = kind * 4 + c * 2
        return pltpu.make_async_remote_copy(
            src_ref=source,
            dst_ref=target,
            send_sem=send_sem.at[slot],
            recv_sem=recv_sem.at[slot + section],
            device_id=device(x, y, 0 if kind == 0 else 1),
            device_id_type=MESH,
        )

    def coarse_copy(n, place, section):
        return pltpu.make_async_remote_copy(
            src_ref=own,
            dst_ref=coarse.at[place, section],
            send_sem=csend.at[n],
            recv_sem=crecv.at[place, section],
            device_id=device(gx, gy, 1 - gz) if n == 2 else device(gx - 1, gy, n),
            device_id_type=MESH,
        )

    coarse_copy(2, 0, gz).start()

    @pl.when(gx >= 1)
    def _():
        for n in range(2):
            coarse_copy(n, 1, gz).start()

    def tell(way, n):
        x = gx + 1 if way == 0 else gx - 1

        @pl.when((x >= 0) & (x < n_gx))
        def _():
            pl.semaphore_signal(
                known.at[way, n], inc=1, device_id=device(x, gy, gz), device_id_type=MESH
            )

    def relay(way, first, last):
        for n in range(first, last):
            behind = gx - 1 - n if way == 0 else gx + 1 + n

            @pl.when((behind >= 0) & (behind < n_gx))
            def _():
                if n:
                    pl.semaphore_wait(known.at[way, n - 1], 1)
                if n < n_gx - 2:
                    tell(way, n)

    relay(1, 0, 1)
    relay(0, 0, n_gx - 1)

    def sends():
        out = []
        for c in (0, 1):
            for kind in range(3):
                use = gx - c >= 0
                if kind == 2:
                    use = use & (gy - 1 >= 0)
                elif c == 0:
                    use = use & (gz != kind)
                out.append((use, kind, c, gx - c, gy - 1 if kind == 2 else gy))
        return out

    for use, kind, c, x, y in sends():
        if c == 0:

            @pl.when(use)
            def _():
                halo_copy(kind, c, gz, x, y).start()

    @pl.when(gx >= 1)
    def _():
        put = 0
        for top, size in ((0, long), (half, short), (half, long), (0, short)):
            upper = tile[top : top + size, :128].astype(F32)
            lower = tile[top + size : top + 2 * size, :128].astype(F32)
            both = jnp.where(iota((size, 128), 1) < P_SIZE, upper, pltpu.roll(lower, P_SIZE, 1))
            packs[put : put + size] = both.astype(BF16)
            put += size

    for use, kind, c, x, y in sends():
        if c == 1:

            @pl.when(use)
            def _():
                halo_copy(kind, c, gz, x, y).start()

    def arrivals(c, kinds):
        for section in range(2):
            for kind in kinds:
                use = (gz == 0) if kind == 0 else (gz == 1)
                if c == 1:
                    use = use & (gx + 1 < n_gx)
                if kind == 2:
                    use = use & (gy + 1 < n_gy)
                elif c == 0:
                    use = use & (gz != section)

                @pl.when(use)
                def _():
                    halo_copy(kind, c, section, gx, gy).wait_recv()

    tile_width = mask.shape[1] * STRIDE
    patch_rows = half // STRIDE
    groups = mask.shape[1] // GROUP
    lanes = GROUP * HALF
    wide = GROUP * P_SIZE
    for copy in small_copies:
        copy.wait()
    roff, coff, off = fine_off[0], fine_off[1], coarse_off[0]
    for copy in table_copies:
        copy.wait()
    table_iy, table_ix = tiy_ref[...], tix_ref[...]

    span = tx.shape[0] // 2
    at = iota((span, 2 * lanes), 0) - coff - STRIDE * ((iota((span, 2 * lanes), 1) >> 5) & (GROUP - 1))
    inside = jnp.where((at >= 0) & (at < P_SIZE), 1.0, 0.0).astype(BF16)
    block = (2 * P_SIZE, 2 * lanes)
    from_left = (iota(block, 0) & (P_SIZE - 1)) - P_SIZE * ((iota(block, 1) >> 5) & (GROUP - 1)) - off
    plain = [tx[0 : 2 * P_SIZE], tx[span : span + 2 * P_SIZE]]
    for step in range(2):
        at_step = from_left + step * P_SIZE
        keep = jnp.where((at_step >= 0) & (at_step < P_SIZE), 1.0, 0.0).astype(BF16)
        for term in range(2):
            base = (2 * step + term) * 2 * P_SIZE
            ctab[base : base + 2 * P_SIZE] = plain[term] * keep
    tx[0:span] = tx[0:span] * inside
    tx[span:] = tx[span:] * inside

    nyquist = (iota((P_SIZE, lanes), 1) & (HALF - 1)) == 0
    frow = signed_of(iota((P_SIZE, wide), 0))

    def along_x_of(section, top, size, g):
        data = ext[section, pl.ds(top, size), g * lanes : g * lanes + span]
        value = bdot(jnp.concatenate([data, data], axis=1), tx[...])
        spec[section, 2 * g, pl.ds(top, size), :] = value[:, :lanes]
        spec[section, 2 * g + 1, pl.ds(top, size), :] = value[:, lanes:]

    inner = groups - 1

    @pl.when(gz == 0)
    def _():
        first_half.wait()

    @pl.when(gz == 1)
    def _():
        second_half.wait()

    for g in range(inner):
        along_x_of(gz, 0, half, g)

    relay(1, 1, n_gx - 1)
    arrivals(0, (0, 1))
    for g in range(inner):
        along_x_of(1 - gz, 0, half, g)

    def split(g, top, size):
        for section in range(2):
            for t in range(2):
                high, low = two_terms(spec[section, 2 * g + t, pl.ds(roff + top, size), :])
                part = slice((2 * g + t) * lanes, (2 * g + t + 1) * lanes)
                spec_high[section, top : top + size, part] = high
                spec_low[section, top : top + size, part] = low

    def forward(g, first_row, last_row):
        part = slice(g * 2 * lanes, (g + 1) * 2 * lanes)
        for row in range(first_row, last_row):
            window = slice(row * STRIDE, row * STRIDE + P_SIZE)
            first, second = (
                bdot(
                    ty[...],
                    jnp.concatenate(
                        [
                            spec_high[t, window, part],
                            spec_high[t, window, part],
                            spec_low[t, window, part],
                        ],
                        axis=0,
                    ),
                )
                for t in range(2)
            )
            for n, plane in enumerate(cross(first, second, 0, nyquist)):
                crossed[g * patch_rows + row, n] = plane
            yield

    upper_rows, middle_row = patch_rows - 2, half - STRIDE

    def upper(g):
        split(g, 0, middle_row)
        yield from forward(g, 0, upper_rows)

    def lower(g):
        split(g, middle_row, P_SIZE)
        yield from forward(g, upper_rows, patch_rows)

    def last_columns():
        for below in range(2):
            use = gx + 1 < n_gx
            if below:
                use = use & ((gz == 0) | (gy + 1 < n_gy))

            @pl.when(use)
            def _():
                for section in range(2):
                    top, size, source = (half, short, long) if below else (0, long, 0)
                    data = landed[section, source : source + size]
                    ext[section, top : top + size, width:] = data
                    data = pltpu.roll(data.astype(F32), P_SIZE, 1).astype(BF16)
                    ext[section, top + size : top + 2 * size, width:] = data

        for section in range(2):
            along_x_of(section, 0, half + P_SIZE, inner)

    coarse_copy(2, 0, 1 - gz).wait_recv()

    @pl.when(gx + 1 < n_gx)
    def _():
        for section in range(2):
            coarse_copy(0, 1, section).wait_recv()

    beside = upper(0)

    def step(count):
        for _ in range(count):
            next(beside, None)

    left = iota((HALF, 2 * P_SIZE), 1) < P_SIZE
    ones = jnp.where((iota((wide, 128), 0) >> 6) == 0, 1.0, 0.0).astype(BF16)
    fcol = signed_of(iota((1, wide), 1) & (P_SIZE - 1))
    lines = []
    for section in range(2):
        terms = []
        for source in range(2):
            data = coarse[source, section].astype(F32)
            both = jnp.concatenate(
                [jnp.where(left, data, 0.0), jnp.where(left, 0.0, data)], axis=0
            ).astype(BF16)
            terms += [both, both]
        lines.append(jnp.concatenate(terms, axis=1))
    value = bdot(jnp.concatenate(lines, axis=0), ctab[...])
    step(BESIDE)
    first = forward_y(ty[...], value[:P_SIZE])
    second = forward_y(ty[...], value[P_SIZE:])
    step(BESIDE)
    hr, hi, yr, yi = cross(first, second, 0, nyquist)
    value = landscape(
        [(hr - jnp.where(nyquist, yi, 0.0), hi + jnp.where(nyquist, yr, 0.0))], table_iy, table_ix
    )
    step(BESIDE)
    top = segment_max(jnp.broadcast_to(jnp.max(value, axis=0, keepdims=True), (8, wide)))[0:1]
    step(BESIDE)
    weight = jnp.exp2(value - top)
    s0 = jnp.sum(weight, axis=0, keepdims=True)
    s1 = jnp.sum(weight * frow, axis=0, keepdims=True)
    rows = iota((8, wide), 0)
    both = jnp.where(rows == 0, s0, jnp.where(rows == 1, s1, jnp.where(rows == 2, s0 * fcol, 0.0)))
    total = exact_dot(both, ones)
    rows = iota((8, 128), 0)
    found = jnp.where(rows == 0, total[1:2] / total[0:1], total[2:3] / total[0:1])
    mine[...] = found
    flows[gx] = found

    def flow_copy(x, place):
        return pltpu.make_async_remote_copy(
            src_ref=mine,
            dst_ref=flows.at[place],
            send_sem=fsend.at[x],
            recv_sem=frecv.at[place],
            device_id=device(x, gy, gz),
            device_id_type=MESH,
        )

    for x in range(n_gx):

        @pl.when(x != gx)
        def _():
            flow_copy(x, gx).start()

    for _ in beside:
        pass
    for g in range(1, inner):
        for _ in upper(g):
            pass
    arrivals(0, (2,))
    for g in range(inner):
        for section in range(2):
            along_x_of(section, half, P_SIZE, g)
    for g in range(inner):
        for _ in lower(g):
            pass
    arrivals(1, (0, 1, 2))
    last_columns()
    for part in (upper, lower):
        for _ in part(inner):
            pass

    for x in range(n_gx):

        @pl.when(x != gx)
        def _():
            flow_copy(x, x).wait_recv()

    mean = sum(flows[x] for x in range(n_gx)) / float(n_gx)
    blended = [(0.5 * DOWN) * (flows[x] + mean) for x in range(n_gx)]

    def pick(column):
        centre = gx * tile_width + column * STRIDE + coff + P_SIZE // 2
        chosen = jnp.clip(((centre >> 3) - off) >> 6, 0, n_gx - 1)
        total = blended[0]
        for x in range(1, n_gx):
            total = jnp.where(chosen == x, blended[x], total)
        return total

    fky = signed_of(iota((P_SIZE, lanes), 0)) * (1.0 / P_SIZE)
    middle = iota((P_SIZE, lanes), 0) == HALF
    kx = (iota((1, lanes), 1) & (HALF - 1)).astype(F32) * (1.0 / P_SIZE)

    def backward(g):
        prior = pick(g * GROUP + (iota((8, lanes), 1) >> 5))
        dy, dx = prior[0:1], prior[1:2]
        eyr, eyi = cis(fky * dy)
        exr, exi = cis(kx * dx)
        nr, ni = cis(0.5 * dx)
        fr = jnp.where(nyquist, nr * eyr + jnp.where(middle, ni * eyi, 0.0), 0.0)
        eyi = jnp.where(middle, 0.0, eyi)
        fi = jnp.where(nyquist, nr * eyi, 0.0)
        er = eyr * exr - eyi * exi
        ei = eyr * exi + eyi * exr
        for q in range(patch_rows // GROUP):
            base = g * patch_rows + q * GROUP
            units = []
            for unit in range(GROUP):
                xr, xi, yr, yi = (crossed[base + unit, n] for n in range(4))
                hr = xr * er - xi * ei
                hi = xr * ei + xi * er
                units.append((hr - (yr * fi + yi * fr), hi + (yr * fr - yi * fi)))
            value = landscape(units, table_iy, table_ix)
            for unit in range(GROUP):
                piece = value[unit * P_SIZE : (unit + 1) * P_SIZE]
                logits[base + unit] = piece
                peaks[base + unit : base + unit + 1] = jnp.max(piece, axis=0, keepdims=True)

    def weigh(g):
        rows = slice(g * patch_rows, (g + 1) * patch_rows)
        top = segment_max(peaks[rows])
        for row in range(patch_rows):
            n = g * patch_rows + row
            weight = jnp.exp2(logits[n] - top[row : row + 1])
            stats[0, n : n + 1] = jnp.sum(weight, axis=0, keepdims=True)
            stats[1, n : n + 1] = jnp.sum(weight * frow, axis=0, keepdims=True)

    for g in range(groups):
        backward(g)
        if g:
            weigh(g - 1)
    weigh(groups - 1)

    columns = mask.shape[1]
    side = columns // 2

    def lane_of(column):
        return (column & 1) * side + (column >> 1)

    put = jnp.where(lane_of(iota((wide, 128), 0) >> 6) == iota((wide, 128), 1), 1.0, 0.0)
    s0 = stats[0]
    sums = exact_dot(jnp.concatenate([s0, stats[1], s0 * fcol], axis=0), put.astype(BF16))
    units = groups * patch_rows

    def gather(stat):
        total = None
        for g in range(groups):
            piece = sums[stat * units + g * patch_rows : stat * units + (g + 1) * patch_rows]
            if g:
                piece = pltpu.roll(piece, g * GROUP // 2, 1)
            total = piece if total is None else total + piece
        return total

    den, along_y, along_x = gather(0), gather(1), gather(2)
    lane = iota((8, 128), 1)
    prior = pick(jnp.where(lane < side, 2 * lane, jnp.minimum(2 * (lane - side) + 1, columns - 1)))
    here = pl.ds(pl.multiple_of(gz * patch_rows, 8), patch_rows)
    place = jnp.where(lane_of(iota((columns, 128), 0)) == iota((columns, 128), 1), 1.0, 0.0)
    valid = bdot(mask[here, :].astype(F32).astype(BF16), place.astype(BF16))
    den = jnp.where(iota((patch_rows, 128), 1) < columns, den, 1.0)
    same = ((iota((patch_rows, 128), 0) + gz) & 1) == 0
    kept = []
    for c, total in enumerate((along_y, along_x)):
        value = prior[c : c + 1] + valid * (total / den)
        odd = pltpu.roll(value, 128 - side, 1)
        given[c] = jnp.where(same, odd, value)
        kept.append(jnp.where(same, value, odd))
    back = pltpu.make_async_remote_copy(
        src_ref=given,
        dst_ref=got,
        send_sem=back_sem.at[0],
        recv_sem=back_sem.at[1],
        device_id=device(gx, gy, 1 - gz),
        device_id_type=MESH,
    )
    back.start()
    coarse_copy(2, 0, gz).wait_send()

    @pl.when(gx >= 1)
    def _():
        for n in range(2):
            coarse_copy(n, 1, gz).wait_send()

    for x in range(n_gx):

        @pl.when(x != gx)
        def _():
            flow_copy(x, gx).wait_send()

    for use, kind, c, x, y in sends():

        @pl.when(use)
        def _():
            halo_copy(kind, c, gz, x, y).wait_send()

    back.wait()
    upper = jnp.full((patch_rows, 128), gz, jnp.int32) == 0
    for c in range(2):
        value = jnp.concatenate(
            [jnp.where(upper, kept[c], got[c]), jnp.where(upper, got[c], kept[c])], axis=0
        )
        out[c] = jnp.transpose(value)[:side]


def solution(mesh):
    n_gx, n_gy = mesh.shape["gx"], mesh.shape["gy"]
    tables = make_tables()
    vmem = pl.BlockSpec(memory_space=pltpu.VMEM)
    anywhere = pl.BlockSpec(memory_space=pl.ANY)

    def local(sections, fine_offsets, coarse_offset, tissue_mask):
        tile = sections[0]
        rows, width = tile.shape
        half = rows // 2
        assert rows // DOWN == P_SIZE and width // DOWN == P_SIZE and n_gx % GROUP == 0
        patch_rows, patch_cols = half // STRIDE, width // STRIDE
        dma = pltpu.SemaphoreType.DMA
        groups = patch_cols // GROUP
        units = patch_rows * groups
        wide = GROUP * P_SIZE
        flow = pl.pallas_call(
            lambda *refs: kernel(n_gx, n_gy, *refs),
            out_shape=pltpu.VMEM((2, patch_cols // 2, 2 * patch_rows), F32),
            in_specs=[anywhere] * (4 + len(tables)),
            out_specs=vmem,
            scratch_shapes=[pltpu.VMEM(t.shape, BF16) for t in tables]
            + [
                pltpu.VMEM((rows, width), BF16),
                pltpu.VMEM((2, half + P_SIZE, width + 128), BF16),
                pltpu.VMEM((2, 2, HALF, 2 * P_SIZE), BF16),
                pltpu.VMEM((HALF, 2 * P_SIZE), BF16),
                pltpu.VMEM((2, patch_rows, 128), F32),
                pltpu.VMEM((2, patch_rows, 128), F32),
                pltpu.VMEM((2, 2 * groups, half + P_SIZE, wide // 2), F32),
                pltpu.VMEM((2, half + STRIDE, groups * wide), BF16),
                pltpu.VMEM((2, half + STRIDE, groups * wide), BF16),
                pltpu.VMEM((8 * P_SIZE, wide), BF16),
                pltpu.VMEM((units, P_SIZE, wide), F32),
                pltpu.VMEM((units, wide), F32),
                pltpu.VMEM((2, units, wide), F32),
                dma((12,)),
                dma((12,)),
                dma((3,)),
                dma((2, 2)),
                dma((3,)),
                dma((len(tables),)),
                dma((2,)),
                pltpu.SMEM(fine_offsets.shape, jnp.int32),
                pltpu.SMEM((1,), jnp.int32),
                pltpu.VMEM(tissue_mask.shape, jnp.int32),
                dma((3,)),
                pltpu.VMEM((half + P_SIZE, 128), BF16),
                pltpu.VMEM((2, (half + P_SIZE) // 2, 128), BF16),
                pltpu.VMEM((units, 4, P_SIZE, wide // 2), F32),
                pltpu.VMEM((8, 128), F32),
                pltpu.VMEM((n_gx, 8, 128), F32),
                dma((n_gx,)),
                dma((n_gx,)),
                pltpu.SemaphoreType.REGULAR((2, n_gx)),
            ],
            compiler_params=pltpu.CompilerParams(
                collective_id=0, has_side_effects=True, vmem_limit_bytes=VMEM_BYTES
            ),
            name="flow",
        )(fine_offsets, coarse_offset, tile, tissue_mask, *[jnp.asarray(t) for t in tables])
        return jnp.swapaxes(flow, 1, 2)[:, None]

    placed = (P("gz", ("pairs", "gy"), "gx"), P("pairs"), P("pairs"), P(("pairs", "gy"), "gx"))
    return jax.shard_map(
        local,
        mesh=mesh,
        in_specs=placed,
        out_specs=P(None, "gz", ("pairs", "gy"), "gx"),
        check_vma=False,
    )
```

```python
import jax
import jax.numpy as jnp
import numpy as np
from jax import lax
from jax.experimental import pallas as pl
from jax.experimental.pallas import tpu as pltpu
from jax.sharding import PartitionSpec as P

P_SIZE = 64
STRIDE = 32
DOWN = 8
HALF = P_SIZE // 2
GROUP = 4
SHARP = 12.0
BESIDE = 1
VMEM_BYTES = 56 * 2**20
MESH = pl.DeviceIdType.MESH
F32 = jnp.float32
BF16 = jnp.bfloat16


def split_table(table):
    high = np.asarray(table, np.float32).astype(jnp.bfloat16)
    low = (np.asarray(table, np.float64) - high.astype(np.float64)).astype(np.float32)
    return high, low.astype(jnp.bfloat16)


def make_tables():
    turn = 2.0 * np.pi / P_SIZE
    k = np.arange(HALF)
    x = np.arange(2 * GROUP * STRIDE)
    angle = turn * (np.outer(x, k) % P_SIZE)
    real = np.cos(angle)
    imag = -np.sin(angle)
    imag[:, 0] = np.cos(np.pi * x)
    forward_x = np.concatenate([np.tile(real, (1, GROUP)), np.tile(imag, (1, GROUP))], axis=1)
    high, low = split_table(forward_x)
    table_x = np.concatenate([high, low], axis=0)
    ky = np.arange(P_SIZE)
    angle = turn * (np.outer(ky, ky) % P_SIZE)
    high, low = split_table(np.concatenate([np.cos(angle), np.sin(angle)], axis=0))
    table_y = np.concatenate([high, low, high], axis=1)
    angle = turn * (np.outer(ky, ky) % P_SIZE)
    cosine, sine = np.cos(angle), np.sin(angle)
    inverse_y = np.block([[cosine, -sine], [sine, cosine]])
    high, low = split_table(inverse_y)
    table_iy = np.concatenate([high, low, high], axis=1)
    angle = turn * (np.outer(k, ky) % P_SIZE)
    real = 2.0 * np.cos(angle)
    imag = -2.0 * np.sin(angle)
    real[0] = 1.0
    imag[0] = np.cos(np.pi * ky)
    scale = SHARP * np.log2(np.e) / float(P_SIZE) ** 4
    eye = np.eye(GROUP)
    inverse_x = np.concatenate([np.kron(eye, real), np.kron(eye, imag)], axis=0) * scale
    high, low = split_table(inverse_x)
    table_ix = np.concatenate([high, high, low], axis=0)
    return table_x, table_y, table_iy, table_ix


def iota(shape, dim):
    return lax.broadcasted_iota(jnp.int32, shape, dim)


def two_terms(value):
    high = value.astype(BF16)
    return high, (value - high.astype(F32)).astype(BF16)


def bdot(a, b):
    return jnp.dot(a, b, preferred_element_type=F32)


def signed_of(index):
    return jnp.where(index >= HALF, index - P_SIZE, index).astype(F32)


def cis(turns):
    rest = turns - jnp.floor(turns + 0.5)
    a = rest * np.float32(np.pi)
    q = a * a
    s = np.float32(-1 / 39916800.0)
    for c in (1 / 362880.0, -1 / 5040.0, 1 / 120.0, -1 / 6.0, 1.0):
        s = s * q + np.float32(c)
    s = s * a
    c = np.float32(1 / 479001600.0)
    for d in (-1 / 3628800.0, 1 / 40320.0, -1 / 720.0, 1 / 24.0, -0.5, 1.0):
        c = c * q + np.float32(d)
    return 1.0 - 2.0 * s * s, 2.0 * s * c


def segment_max(value):
    width = value.shape[1]
    place = iota(value.shape, 1) & (P_SIZE - 1)
    step = 1
    while step < P_SIZE:
        near = pltpu.roll(value, step, 1)
        far = pltpu.roll(value, width - P_SIZE + step, 1)
        value = jnp.maximum(value, jnp.where(place >= step, near, far))
        step *= 2
    return value


def forward_y(table, spectrum_x):
    high, low = two_terms(spectrum_x)
    return bdot(table, jnp.concatenate([high, high, low], axis=0))


def planes(product, unit):
    base = unit * 2 * P_SIZE
    lanes = GROUP * HALF
    cosine = product[base : base + P_SIZE]
    sine = product[base + P_SIZE : base + 2 * P_SIZE]
    return cosine[:, :lanes], sine[:, :lanes], cosine[:, lanes:], sine[:, lanes:]


def cross(first, second, unit, nyquist):
    a1, a2, a3, a4 = planes(first, unit)
    b1, b2, b3, b4 = planes(second, unit)
    ar = a1 + jnp.where(nyquist, 0.0, a4)
    ai = jnp.where(nyquist, 0.0, a3) - a2
    br = b1 + jnp.where(nyquist, 0.0, b4)
    bi = jnp.where(nyquist, 0.0, b3) - b2
    return (br * ar + bi * ai, bi * ar - br * ai, b3 * a3 + b4 * a4, b3 * a4 - b4 * a3)


def landscape(units, table_iy, table_ix):
    stacked = []
    for zr, zi in units:
        high, low = two_terms(jnp.concatenate([zr, zi], axis=0))
        stacked.append(jnp.concatenate([high, high, low], axis=0))
    back = bdot(table_iy, jnp.concatenate(stacked, axis=1) if len(stacked) > 1 else stacked[0])
    lanes = GROUP * HALF
    rows = []
    for unit in range(len(units)):
        piece = back[:, unit * lanes : (unit + 1) * lanes]
        rows.append(jnp.concatenate([piece[:P_SIZE], piece[P_SIZE:]], axis=1))
    value = jnp.concatenate(rows, axis=0) if len(rows) > 1 else rows[0]
    high, low = two_terms(value)
    return bdot(jnp.concatenate([high, low, high], axis=1), table_ix)


def exact_dot(a, b):
    terms = []
    for _ in range(3):
        terms.append(a.astype(BF16))
        a = a - terms[-1].astype(F32)
    return bdot(jnp.concatenate(terms, axis=1), jnp.concatenate([b, b, b], axis=0))


def kernel(
    n_gx, n_gy, fine_hbm, coarse_hbm, tile_hbm, mask_hbm, *rest
):
    hbm_tables, (out,), scratch = rest[:4], rest[4:5], rest[5:]
    table_refs, scratch = scratch[:4], scratch[4:]
    (tile, ext, coarse, own, given, got, spec, spec_high, spec_low, ctab, logits, peaks, stats) = scratch[:13]
    send_sem, recv_sem, csend, crecv, local_sem, table_sem, back_sem = scratch[13:20]
    fine_off, coarse_off, mask, small_sem, packs, landed, crossed = scratch[20:27]
    mine, flows, fsend, frecv, known = scratch[27:]
    tx, ty, tiy_ref, tix_ref = table_refs
    pairs, gx, gy, gz = (lax.axis_index(a) for a in ("pairs", "gx", "gy", "gz"))
    rows, width = tile.shape
    half = rows // 2
    edge = ext.shape[2] - width

    def device(x, y, z):
        return (pairs, x, y, z)

    load = pltpu.make_async_copy(tile_hbm, tile, local_sem.at[2])
    load.start()
    small_copies = [
        pltpu.make_async_copy(source, target, small_sem.at[n])
        for n, (source, target) in enumerate(
            ((fine_hbm, fine_off), (coarse_hbm, coarse_off), (mask_hbm, mask))
        )
    ]
    for copy in small_copies:
        copy.start()

    barrier = pltpu.get_barrier_semaphore()
    greeted = [(gx, gy, 1 - gz, None)]
    for z in range(2):
        greeted.append((gx - 1, gy, z, gx >= 1))
        greeted.append((gx + 1, gy, z, gx + 1 < n_gx))
    for x in (gx, gx + 1):
        for z in range(2):
            greeted.append((x, gy + 1, z, (gz == 1) & (gy + 1 < n_gy) & (x < n_gx)))
    for x, y, z, use in greeted:

        def greet():
            pl.semaphore_signal(barrier, inc=1, device_id=device(x, y, z), device_id_type=MESH)

        if use is None:
            greet()
        else:
            pl.when(use)(greet)

    has_left = jnp.where(gx >= 1, 1, 0)
    count = 1 + 2 * has_left + jnp.where(gx + 1 < n_gx, 2, 0) + jnp.where(gy >= 1, 1 + has_left, 0)

    table_copies = [
        pltpu.make_async_copy(source, target, table_sem.at[n])
        for n, (source, target) in enumerate(zip(hbm_tables, table_refs))
    ]
    for copy in table_copies:
        copy.start()
    first_half = pltpu.make_async_copy(
        tile_hbm.at[pl.ds(0, half + P_SIZE), :],
        ext.at[0, pl.ds(0, half + P_SIZE), pl.ds(0, width)],
        local_sem.at[0],
    )
    second_half = pltpu.make_async_copy(
        tile_hbm.at[pl.ds(half, half), :], ext.at[1, pl.ds(0, half), pl.ds(0, width)], local_sem.at[1]
    )

    @pl.when(gz == 0)
    def _():
        first_half.start()

    @pl.when(gz == 1)
    def _():
        second_half.start()

    pool_rows = jnp.where((iota((rows // DOWN, rows), 1) >> 3) == iota((rows // DOWN, rows), 0), 1.0, 0.0)
    lanes = iota((width, 2 * P_SIZE), 1)
    block = iota((width, 2 * P_SIZE), 0) >> 3
    pool = jnp.where(block == (lanes & (P_SIZE - 1)), 1.0, 0.0).astype(BF16)
    pool_rows = pool_rows.astype(BF16)
    load.wait()
    piece = bdot(pool_rows, tile[...])
    terms = []
    for _ in range(3):
        terms.append(piece.astype(BF16))
        piece = piece - terms[-1].astype(F32)
    packed = bdot(jnp.concatenate(terms, axis=1), jnp.concatenate([pool] * 3, axis=0))
    packed = jnp.where(iota((HALF, 2 * P_SIZE), 1) < P_SIZE, packed[:HALF], packed[HALF:])
    packed = (packed * (1.0 / DOWN)).astype(BF16)
    own[...] = packed
    coarse[0, gz] = packed

    @pl.when(gx + 1 >= n_gx)
    def _():
        ext[:, :, width:] = jnp.zeros((2, half + P_SIZE, edge), BF16)
        coarse[1] = jnp.zeros(coarse.shape[1:], BF16)

    @pl.when((gz == 1) & (gy + 1 >= n_gy))
    def _():
        ext[:, half:, :width] = jnp.zeros((2, P_SIZE, width), BF16)
        ext[:, half:, width:] = jnp.zeros((2, P_SIZE, edge), BF16)

    pl.semaphore_wait(barrier, count)

    long, short = half // 2, P_SIZE // 2

    def halo_copy(kind, c, section, x, y):
        if c == 0:
            source, target = (
                (pl.ds(0, half + P_SIZE), pl.ds(0, half + P_SIZE)),
                (pl.ds(half, half), pl.ds(0, half)),
                (pl.ds(0, P_SIZE), pl.ds(half, P_SIZE)),
            )[kind]
            source = tile.at[source, :]
            target = ext.at[section, target, pl.ds(0, width)]
        else:
            source, target = (
                (pl.ds(0, long + short), pl.ds(0, long + short)),
                (pl.ds(long + short, long), pl.ds(0, long)),
                (pl.ds(2 * long + short, short), pl.ds(long, short)),
            )[kind]
            source = packs.at[source, :]
            target = landed.at[section, target, :]
        slot = kind * 4 + c * 2
        return pltpu.make_async_remote_copy(
            src_ref=source,
            dst_ref=target,
            send_sem=send_sem.at[slot],
            recv_sem=recv_sem.at[slot + section],
            device_id=device(x, y, 0 if kind == 0 else 1),
            device_id_type=MESH,
        )

    def coarse_copy(n, place, section):
        return pltpu.make_async_remote_copy(
            src_ref=own,
            dst_ref=coarse.at[place, section],
            send_sem=csend.at[n],
            recv_sem=crecv.at[place, section],
            device_id=device(gx, gy, 1 - gz) if n == 2 else device(gx - 1, gy, n),
            device_id_type=MESH,
        )

    coarse_copy(2, 0, gz).start()

    @pl.when(gx >= 1)
    def _():
        for n in range(2):
            coarse_copy(n, 1, gz).start()

    def tell(way, n):
        x = gx + 1 if way == 0 else gx - 1

        @pl.when((x >= 0) & (x < n_gx))
        def _():
            pl.semaphore_signal(
                known.at[way, n], inc=1, device_id=device(x, gy, gz), device_id_type=MESH
            )

    def relay(way, first, last):
        for n in range(first, last):
            behind = gx - 1 - n if way == 0 else gx + 1 + n

            @pl.when((behind >= 0) & (behind < n_gx))
            def _():
                if n:
                    pl.semaphore_wait(known.at[way, n - 1], 1)
                if n < n_gx - 2:
                    tell(way, n)

    relay(1, 0, 1)
    relay(0, 0, n_gx - 1)

    def sends():
        out = []
        for c in (0, 1):
            for kind in range(3):
                use = gx - c >= 0
                if kind == 2:
                    use = use & (gy - 1 >= 0)
                elif c == 0:
                    use = use & (gz != kind)
                out.append((use, kind, c, gx - c, gy - 1 if kind == 2 else gy))
        return out

    for use, kind, c, x, y in sends():
        if c == 0:

            @pl.when(use)
            def _():
                halo_copy(kind, c, gz, x, y).start()

    @pl.when(gx >= 1)
    def _():
        put = 0
        for top, size in ((0, long), (half, short), (half, long), (0, short)):
            upper = tile[top : top + size, :128].astype(F32)
            lower = tile[top + size : top + 2 * size, :128].astype(F32)
            both = jnp.where(iota((size, 128), 1) < P_SIZE, upper, pltpu.roll(lower, P_SIZE, 1))
            packs[put : put + size] = both.astype(BF16)
            put += size

    for use, kind, c, x, y in sends():
        if c == 1:

            @pl.when(use)
            def _():
                halo_copy(kind, c, gz, x, y).start()

    def arrivals(c, kinds):
        for section in range(2):
            for kind in kinds:
                use = (gz == 0) if kind == 0 else (gz == 1)
                if c == 1:
                    use = use & (gx + 1 < n_gx)
                if kind == 2:
                    use = use & (gy + 1 < n_gy)
                elif c == 0:
                    use = use & (gz != section)

                @pl.when(use)
                def _():
                    halo_copy(kind, c, section, gx, gy).wait_recv()

    tile_width = mask.shape[1] * STRIDE
    patch_rows = half // STRIDE
    groups = mask.shape[1] // GROUP
    lanes = GROUP * HALF
    wide = GROUP * P_SIZE
    for copy in small_copies:
        copy.wait()
    roff, coff, off = fine_off[0], fine_off[1], coarse_off[0]
    for copy in table_copies:
        copy.wait()
    table_iy, table_ix = tiy_ref[...], tix_ref[...]

    span = tx.shape[0] // 2
    at = iota((span, 2 * lanes), 0) - coff - STRIDE * ((iota((span, 2 * lanes), 1) >> 5) & (GROUP - 1))
    inside = jnp.where((at >= 0) & (at < P_SIZE), 1.0, 0.0).astype(BF16)
    block = (2 * P_SIZE, 2 * lanes)
    from_left = (iota(block, 0) & (P_SIZE - 1)) - P_SIZE * ((iota(block, 1) >> 5) & (GROUP - 1)) - off
    plain = [tx[0 : 2 * P_SIZE], tx[span : span + 2 * P_SIZE]]
    for step in range(2):
        at_step = from_left + step * P_SIZE
        keep = jnp.where((at_step >= 0) & (at_step < P_SIZE), 1.0, 0.0).astype(BF16)
        for term in range(2):
            base = (2 * step + term) * 2 * P_SIZE
            ctab[base : base + 2 * P_SIZE] = plain[term] * keep

    nyquist = (iota((P_SIZE, lanes), 1) & (HALF - 1)) == 0
    frow = signed_of(iota((P_SIZE, wide), 0))

    def along_x_of(section, top, size, g):
        data = ext[section, pl.ds(top, size), g * lanes : g * lanes + span]
        value = bdot(jnp.concatenate([data, data], axis=1), tx[...])
        spec[section, 2 * g, pl.ds(top, size), :] = value[:, :lanes]
        spec[section, 2 * g + 1, pl.ds(top, size), :] = value[:, lanes:]

    inner = groups - 1

    @pl.when(gz == 0)
    def _():
        first_half.wait()

    @pl.when(gz == 1)
    def _():
        second_half.wait()

    def split(g, top, size):
        for section in range(2):
            for t in range(2):
                high, low = two_terms(spec[section, 2 * g + t, pl.ds(roff + top, size), :])
                part = slice((2 * g + t) * lanes, (2 * g + t + 1) * lanes)
                spec_high[section, top : top + size, part] = high
                spec_low[section, top : top + size, part] = low

    def forward(g, first_row, last_row):
        part = slice(g * 2 * lanes, (g + 1) * 2 * lanes)
        for row in range(first_row, last_row):
            window = slice(row * STRIDE, row * STRIDE + P_SIZE)
            first, second = (
                bdot(
                    ty[...],
                    jnp.concatenate(
                        [
                            spec_high[t, window, part],
                            spec_high[t, window, part],
                            spec_low[t, window, part],
                        ],
                        axis=0,
                    ),
                )
                for t in range(2)
            )
            for n, plane in enumerate(cross(first, second, 0, nyquist)):
                crossed[g * patch_rows + row, n] = plane
            yield

    upper_rows, middle_row = patch_rows - 2, half - STRIDE

    def upper(g):
        split(g, 0, middle_row)
        yield from forward(g, 0, upper_rows)

    def lower(g):
        split(g, middle_row, P_SIZE)
        yield from forward(g, upper_rows, patch_rows)

    def last_columns():
        for below in range(2):
            use = gx + 1 < n_gx
            if below:
                use = use & ((gz == 0) | (gy + 1 < n_gy))

            @pl.when(use)
            def _():
                for section in range(2):
                    top, size, source = (half, short, long) if below else (0, long, 0)
                    data = landed[section, source : source + size]
                    ext[section, top : top + size, width:] = data
                    data = pltpu.roll(data.astype(F32), P_SIZE, 1).astype(BF16)
                    ext[section, top + size : top + 2 * size, width:] = data

        for section in range(2):
            along_x_of(section, 0, half + P_SIZE, inner)

    relay(1, 1, n_gx - 1)
    coarse_copy(2, 0, 1 - gz).wait_recv()

    @pl.when(gx + 1 < n_gx)
    def _():
        for section in range(2):
            coarse_copy(0, 1, section).wait_recv()

    def own_lines():
        tx[0:span] = tx[0:span] * inside
        tx[span:] = tx[span:] * inside
        yield
        for g in range(inner):
            along_x_of(gz, 0, half, g)
            yield

    beside = own_lines()

    def step(count):
        for _ in range(count):
            next(beside, None)

    left = iota((HALF, 2 * P_SIZE), 1) < P_SIZE
    ones = jnp.where((iota((wide, 128), 0) >> 6) == 0, 1.0, 0.0).astype(BF16)
    fcol = signed_of(iota((1, wide), 1) & (P_SIZE - 1))
    lines = []
    for section in range(2):
        terms = []
        for source in range(2):
            data = coarse[source, section].astype(F32)
            both = jnp.concatenate(
                [jnp.where(left, data, 0.0), jnp.where(left, 0.0, data)], axis=0
            ).astype(BF16)
            terms += [both, both]
        lines.append(jnp.concatenate(terms, axis=1))
    value = bdot(jnp.concatenate(lines, axis=0), ctab[...])
    step(BESIDE)
    first = forward_y(ty[...], value[:P_SIZE])
    second = forward_y(ty[...], value[P_SIZE:])
    step(BESIDE)
    hr, hi, yr, yi = cross(first, second, 0, nyquist)
    value = landscape(
        [(hr - jnp.where(nyquist, yi, 0.0), hi + jnp.where(nyquist, yr, 0.0))], table_iy, table_ix
    )
    step(BESIDE)
    top = segment_max(jnp.broadcast_to(jnp.max(value, axis=0, keepdims=True), (8, wide)))[0:1]
    step(BESIDE)
    weight = jnp.exp2(value - top)
    s0 = jnp.sum(weight, axis=0, keepdims=True)
    s1 = jnp.sum(weight * frow, axis=0, keepdims=True)
    rows = iota((8, wide), 0)
    both = jnp.where(rows == 0, s0, jnp.where(rows == 1, s1, jnp.where(rows == 2, s0 * fcol, 0.0)))
    total = exact_dot(both, ones)
    rows = iota((8, 128), 0)
    found = jnp.where(rows == 0, total[1:2] / total[0:1], total[2:3] / total[0:1])
    mine[...] = found
    flows[gx] = found

    def flow_copy(x, place, z=0):
        return pltpu.make_async_remote_copy(
            src_ref=mine,
            dst_ref=flows.at[place],
            send_sem=fsend.at[x, z],
            recv_sem=frecv.at[place],
            device_id=device(x, gy, z),
            device_id_type=MESH,
        )

    for x in range(n_gx):

        @pl.when((x != gx) & (gz == 1))
        def _():
            for z in range(2):
                flow_copy(x, gx, z).start()

    for _ in beside:
        pass
    arrivals(0, (0, 1))
    for g in range(inner):
        along_x_of(1 - gz, 0, half, g)
    for g in range(inner):
        for _ in upper(g):
            pass
    arrivals(0, (2,))
    for g in range(inner):
        for section in range(2):
            along_x_of(section, half, P_SIZE, g)
    for g in range(inner):
        for _ in lower(g):
            pass
    arrivals(1, (0, 1, 2))
    last_columns()
    for part in (upper, lower):
        for _ in part(inner):
            pass

    columns = mask.shape[1]
    side = columns // 2

    def lane_of(column):
        return (column & 1) * side + (column >> 1)

    put = jnp.where(lane_of(iota((wide, 128), 0) >> 6) == iota((wide, 128), 1), 1.0, 0.0)
    here = pl.ds(pl.multiple_of(gz * patch_rows, 8), patch_rows)
    place = jnp.where(lane_of(iota((columns, 128), 0)) == iota((columns, 128), 1), 1.0, 0.0)
    valid = bdot(mask[here, :].astype(F32).astype(BF16), place.astype(BF16))

    for x in range(n_gx):

        @pl.when(x != gx)
        def _():
            flow_copy(x, x).wait_recv()

    mean = sum(flows[x] for x in range(n_gx)) / float(n_gx)
    blended = [(0.5 * DOWN) * (flows[x] + mean) for x in range(n_gx)]

    def pick(column):
        centre = gx * tile_width + column * STRIDE + coff + P_SIZE // 2
        chosen = jnp.clip(((centre >> 3) - off) >> 6, 0, n_gx - 1)
        total = blended[0]
        for x in range(1, n_gx):
            total = jnp.where(chosen == x, blended[x], total)
        return total

    fky = signed_of(iota((P_SIZE, lanes), 0)) * (1.0 / P_SIZE)
    middle = iota((P_SIZE, lanes), 0) == HALF
    kx = (iota((1, lanes), 1) & (HALF - 1)).astype(F32) * (1.0 / P_SIZE)

    lane = iota((8, 128), 1)
    last_prior = pick(jnp.where(lane < side, 2 * lane, jnp.minimum(2 * (lane - side) + 1, columns - 1)))

    def backward(g):
        prior = pick(g * GROUP + (iota((8, lanes), 1) >> 5))
        dy, dx = prior[0:1], prior[1:2]
        eyr, eyi = cis(fky * dy)
        exr, exi = cis(kx * dx)
        nr, ni = cis(0.5 * dx)
        fr = jnp.where(nyquist, nr * eyr + jnp.where(middle, ni * eyi, 0.0), 0.0)
        eyi = jnp.where(middle, 0.0, eyi)
        fi = jnp.where(nyquist, nr * eyi, 0.0)
        er = eyr * exr - eyi * exi
        ei = eyr * exi + eyi * exr
        for q in range(patch_rows // GROUP):
            base = g * patch_rows + q * GROUP
            units = []
            for unit in range(GROUP):
                xr, xi, yr, yi = (crossed[base + unit, n] for n in range(4))
                hr = xr * er - xi * ei
                hi = xr * ei + xi * er
                units.append((hr - (yr * fi + yi * fr), hi + (yr * fr - yi * fi)))
            value = landscape(units, table_iy, table_ix)
            for unit in range(GROUP):
                piece = value[unit * P_SIZE : (unit + 1) * P_SIZE]
                logits[base + unit] = piece
                peaks[base + unit : base + unit + 1] = jnp.max(piece, axis=0, keepdims=True)

    def weigh(g):
        rows = slice(g * patch_rows, (g + 1) * patch_rows)
        top = segment_max(peaks[rows])
        for row in range(patch_rows):
            n = g * patch_rows + row
            weight = jnp.exp2(logits[n] - top[row : row + 1])
            stats[0, n : n + 1] = jnp.sum(weight, axis=0, keepdims=True)
            stats[1, n : n + 1] = jnp.sum(weight * frow, axis=0, keepdims=True)

    for g in range(groups):
        backward(g)
        if g:
            weigh(g - 1)
    weigh(groups - 1)

    s0 = stats[0]
    sums = exact_dot(jnp.concatenate([s0, stats[1], s0 * fcol], axis=0), put.astype(BF16))
    units = groups * patch_rows

    def gather(stat):
        total = None
        for g in range(groups):
            piece = sums[stat * units + g * patch_rows : stat * units + (g + 1) * patch_rows]
            if g:
                piece = pltpu.roll(piece, g * GROUP // 2, 1)
            total = piece if total is None else total + piece
        return total

    den, along_y, along_x = gather(0), gather(1), gather(2)
    den = jnp.where(iota((patch_rows, 128), 1) < columns, den, 1.0)
    same = ((iota((patch_rows, 128), 0) + gz) & 1) == 0
    kept = []
    for c, total in enumerate((along_y, along_x)):
        value = last_prior[c : c + 1] + valid * (total / den)
        odd = pltpu.roll(value, 128 - side, 1)
        given[c] = jnp.where(same, odd, value)
        kept.append(jnp.where(same, value, odd))
    back = pltpu.make_async_remote_copy(
        src_ref=given,
        dst_ref=got,
        send_sem=back_sem.at[0],
        recv_sem=back_sem.at[1],
        device_id=device(gx, gy, 1 - gz),
        device_id_type=MESH,
    )
    back.start()
    coarse_copy(2, 0, gz).wait_send()

    @pl.when(gx >= 1)
    def _():
        for n in range(2):
            coarse_copy(n, 1, gz).wait_send()

    for x in range(n_gx):

        @pl.when((x != gx) & (gz == 1))
        def _():
            for z in range(2):
                flow_copy(x, gx, z).wait_send()

    for use, kind, c, x, y in sends():

        @pl.when(use)
        def _():
            halo_copy(kind, c, gz, x, y).wait_send()

    back.wait()
    upper = jnp.full((patch_rows, 128), gz, jnp.int32) == 0
    for c in range(2):
        value = jnp.concatenate(
            [jnp.where(upper, kept[c], got[c]), jnp.where(upper, got[c], kept[c])], axis=0
        )
        out[c] = jnp.transpose(value)[:side]


def solution(mesh):
    n_gx, n_gy = mesh.shape["gx"], mesh.shape["gy"]
    tables = make_tables()
    vmem = pl.BlockSpec(memory_space=pltpu.VMEM)
    anywhere = pl.BlockSpec(memory_space=pl.ANY)

    def local(sections, fine_offsets, coarse_offset, tissue_mask):
        tile = sections[0]
        rows, width = tile.shape
        half = rows // 2
        assert rows // DOWN == P_SIZE and width // DOWN == P_SIZE and n_gx % GROUP == 0
        patch_rows, patch_cols = half // STRIDE, width // STRIDE
        dma = pltpu.SemaphoreType.DMA
        groups = patch_cols // GROUP
        units = patch_rows * groups
        wide = GROUP * P_SIZE
        flow = pl.pallas_call(
            lambda *refs: kernel(n_gx, n_gy, *refs),
            out_shape=pltpu.VMEM((2, patch_cols // 2, 2 * patch_rows), F32),
            in_specs=[anywhere] * (4 + len(tables)),
            out_specs=vmem,
            scratch_shapes=[pltpu.VMEM(t.shape, BF16) for t in tables]
            + [
                pltpu.VMEM((rows, width), BF16),
                pltpu.VMEM((2, half + P_SIZE, width + 128), BF16),
                pltpu.VMEM((2, 2, HALF, 2 * P_SIZE), BF16),
                pltpu.VMEM((HALF, 2 * P_SIZE), BF16),
                pltpu.VMEM((2, patch_rows, 128), F32),
                pltpu.VMEM((2, patch_rows, 128), F32),
                pltpu.VMEM((2, 2 * groups, half + P_SIZE, wide // 2), F32),
                pltpu.VMEM((2, half + STRIDE, groups * wide), BF16),
                pltpu.VMEM((2, half + STRIDE, groups * wide), BF16),
                pltpu.VMEM((8 * P_SIZE, wide), BF16),
                pltpu.VMEM((units, P_SIZE, wide), F32),
                pltpu.VMEM((units, wide), F32),
                pltpu.VMEM((2, units, wide), F32),
                dma((12,)),
                dma((12,)),
                dma((3,)),
                dma((2, 2)),
                dma((3,)),
                dma((len(tables),)),
                dma((2,)),
                pltpu.SMEM(fine_offsets.shape, jnp.int32),
                pltpu.SMEM((1,), jnp.int32),
                pltpu.VMEM(tissue_mask.shape, jnp.int32),
                dma((3,)),
                pltpu.VMEM((half + P_SIZE, 128), BF16),
                pltpu.VMEM((2, (half + P_SIZE) // 2, 128), BF16),
                pltpu.VMEM((units, 4, P_SIZE, wide // 2), F32),
                pltpu.VMEM((8, 128), F32),
                pltpu.VMEM((n_gx, 8, 128), F32),
                dma((n_gx, 2)),
                dma((n_gx,)),
                pltpu.SemaphoreType.REGULAR((2, n_gx)),
            ],
            compiler_params=pltpu.CompilerParams(
                collective_id=0, has_side_effects=True, vmem_limit_bytes=VMEM_BYTES
            ),
            name="flow",
        )(fine_offsets, coarse_offset, tile, tissue_mask, *[jnp.asarray(t) for t in tables])
        return jnp.swapaxes(flow, 1, 2)[:, None]

    placed = (P("gz", ("pairs", "gy"), "gx"), P("pairs"), P("pairs"), P(("pairs", "gy"), "gx"))
    return jax.shard_map(
        local,
        mesh=mesh,
        in_specs=placed,
        out_specs=P(None, "gz", ("pairs", "gy"), "gx"),
        check_vma=False,
    )
```

```python
import jax
import jax.numpy as jnp
import numpy as np
from jax import lax
from jax.experimental import pallas as pl
from jax.experimental.pallas import tpu as pltpu
from jax.sharding import PartitionSpec as P

P_SIZE = 64
STRIDE = 32
DOWN = 8
HALF = P_SIZE // 2
GROUP = 4
SHARP = 12.0
BESIDE = 1
VMEM_BYTES = 56 * 2**20
MESH = pl.DeviceIdType.MESH
F32 = jnp.float32
BF16 = jnp.bfloat16


def split_table(table):
    high = np.asarray(table, np.float32).astype(jnp.bfloat16)
    low = (np.asarray(table, np.float64) - high.astype(np.float64)).astype(np.float32)
    return high, low.astype(jnp.bfloat16)


def make_tables():
    turn = 2.0 * np.pi / P_SIZE
    k = np.arange(HALF)
    x = np.arange(2 * GROUP * STRIDE)
    angle = turn * (np.outer(x, k) % P_SIZE)
    real = np.cos(angle)
    imag = -np.sin(angle)
    imag[:, 0] = np.cos(np.pi * x)
    forward_x = np.concatenate([np.tile(real, (1, GROUP)), np.tile(imag, (1, GROUP))], axis=1)
    high, low = split_table(forward_x)
    table_x = np.concatenate([high, low], axis=0)
    ky = np.arange(P_SIZE)
    angle = turn * (np.outer(ky, ky) % P_SIZE)
    high, low = split_table(np.concatenate([np.cos(angle), np.sin(angle)], axis=0))
    table_y = np.concatenate([high, low, high], axis=1)
    angle = turn * (np.outer(ky, ky) % P_SIZE)
    cosine, sine = np.cos(angle), np.sin(angle)
    inverse_y = np.block([[cosine, -sine], [sine, cosine]])
    high, low = split_table(inverse_y)
    table_iy = np.concatenate([high, low, high], axis=1)
    angle = turn * (np.outer(k, ky) % P_SIZE)
    real = 2.0 * np.cos(angle)
    imag = -2.0 * np.sin(angle)
    real[0] = 1.0
    imag[0] = np.cos(np.pi * ky)
    scale = SHARP * np.log2(np.e) / float(P_SIZE) ** 4
    eye = np.eye(GROUP)
    inverse_x = np.concatenate([np.kron(eye, real), np.kron(eye, imag)], axis=0) * scale
    high, low = split_table(inverse_x)
    table_ix = np.concatenate([high, high, low], axis=0)
    return table_x, table_y, table_iy, table_ix


def iota(shape, dim):
    return lax.broadcasted_iota(jnp.int32, shape, dim)


def two_terms(value):
    high = value.astype(BF16)
    return high, (value - high.astype(F32)).astype(BF16)


def bdot(a, b):
    return jnp.dot(a, b, preferred_element_type=F32)


def signed_of(index):
    return jnp.where(index >= HALF, index - P_SIZE, index).astype(F32)


def cis(turns):
    rest = turns - jnp.floor(turns + 0.5)
    a = rest * np.float32(np.pi)
    q = a * a
    s = np.float32(-1 / 39916800.0)
    for c in (1 / 362880.0, -1 / 5040.0, 1 / 120.0, -1 / 6.0, 1.0):
        s = s * q + np.float32(c)
    s = s * a
    c = np.float32(1 / 479001600.0)
    for d in (-1 / 3628800.0, 1 / 40320.0, -1 / 720.0, 1 / 24.0, -0.5, 1.0):
        c = c * q + np.float32(d)
    return 1.0 - 2.0 * s * s, 2.0 * s * c


def segment_max(value):
    width = value.shape[1]
    place = iota(value.shape, 1) & (P_SIZE - 1)
    step = 1
    while step < P_SIZE:
        near = pltpu.roll(value, step, 1)
        far = pltpu.roll(value, width - P_SIZE + step, 1)
        value = jnp.maximum(value, jnp.where(place >= step, near, far))
        step *= 2
    return value


def forward_y(table, spectrum_x):
    high, low = two_terms(spectrum_x)
    return bdot(table, jnp.concatenate([high, high, low], axis=0))


def planes(product, unit):
    base = unit * 2 * P_SIZE
    lanes = GROUP * HALF
    cosine = product[base : base + P_SIZE]
    sine = product[base + P_SIZE : base + 2 * P_SIZE]
    return cosine[:, :lanes], sine[:, :lanes], cosine[:, lanes:], sine[:, lanes:]


def cross(first, second, unit, nyquist):
    a1, a2, a3, a4 = planes(first, unit)
    b1, b2, b3, b4 = planes(second, unit)
    ar = a1 + jnp.where(nyquist, 0.0, a4)
    ai = jnp.where(nyquist, 0.0, a3) - a2
    br = b1 + jnp.where(nyquist, 0.0, b4)
    bi = jnp.where(nyquist, 0.0, b3) - b2
    return (br * ar + bi * ai, bi * ar - br * ai, b3 * a3 + b4 * a4, b3 * a4 - b4 * a3)


def landscape(units, table_iy, table_ix):
    stacked = []
    for zr, zi in units:
        high, low = two_terms(jnp.concatenate([zr, zi], axis=0))
        stacked.append(jnp.concatenate([high, high, low], axis=0))
    back = bdot(table_iy, jnp.concatenate(stacked, axis=1) if len(stacked) > 1 else stacked[0])
    lanes = GROUP * HALF
    rows = []
    for unit in range(len(units)):
        piece = back[:, unit * lanes : (unit + 1) * lanes]
        rows.append(jnp.concatenate([piece[:P_SIZE], piece[P_SIZE:]], axis=1))
    value = jnp.concatenate(rows, axis=0) if len(rows) > 1 else rows[0]
    high, low = two_terms(value)
    return bdot(jnp.concatenate([high, low, high], axis=1), table_ix)


def exact_dot(a, b):
    terms = []
    for _ in range(3):
        terms.append(a.astype(BF16))
        a = a - terms[-1].astype(F32)
    return bdot(jnp.concatenate(terms, axis=1), jnp.concatenate([b, b, b], axis=0))


def kernel(
    n_gx, n_gy, fine_hbm, coarse_hbm, tile_hbm, mask_hbm, *rest
):
    hbm_tables, (out,), scratch = rest[:4], rest[4:5], rest[5:]
    table_refs, scratch = scratch[:4], scratch[4:]
    (tile, ext, coarse, own, given, got, spec, spec_high, spec_low, ctab, logits, peaks, stats) = scratch[:13]
    send_sem, recv_sem, csend, crecv, local_sem, table_sem, back_sem = scratch[13:20]
    fine_off, coarse_off, mask, small_sem, packs, landed, crossed = scratch[20:27]
    mine, flows, fsend, frecv, known = scratch[27:]
    tx, ty, tiy_ref, tix_ref = table_refs
    pairs, gx, gy, gz = (lax.axis_index(a) for a in ("pairs", "gx", "gy", "gz"))
    rows, width = tile.shape
    half = rows // 2
    edge = ext.shape[2] - width

    def device(x, y, z):
        return (pairs, x, y, z)

    load = pltpu.make_async_copy(tile_hbm, tile, local_sem.at[2])
    load.start()
    small_copies = [
        pltpu.make_async_copy(source, target, small_sem.at[n])
        for n, (source, target) in enumerate(
            ((fine_hbm, fine_off), (coarse_hbm, coarse_off), (mask_hbm, mask))
        )
    ]
    for copy in small_copies:
        copy.start()

    barrier = pltpu.get_barrier_semaphore()
    greeted = [(gx, gy, 1 - gz, None)]
    greeted.append((gx - 1, gy, 1, (gz == 1) & (gx >= 1)))
    for z in range(2):
        greeted.append((gx + 1, gy, z, gx + 1 < n_gx))
    for x in (gx, gx + 1):
        for z in range(2):
            greeted.append((x, gy + 1, z, (gz == 1) & (gy + 1 < n_gy) & (x < n_gx)))
    for x, y, z, use in greeted:

        def greet():
            pl.semaphore_signal(barrier, inc=1, device_id=device(x, y, z), device_id_type=MESH)

        if use is None:
            greet()
        else:
            pl.when(use)(greet)

    has_left = jnp.where(gx >= 1, 1, 0)
    count = 1 + 2 * has_left + jnp.where((gz == 1) & (gx + 1 < n_gx), 1, 0) + jnp.where(gy >= 1, 1 + has_left, 0)

    table_copies = [
        pltpu.make_async_copy(source, target, table_sem.at[n])
        for n, (source, target) in enumerate(zip(hbm_tables, table_refs))
    ]
    for copy in table_copies:
        copy.start()
    first_half = pltpu.make_async_copy(
        tile_hbm.at[pl.ds(0, half + P_SIZE), :],
        ext.at[0, pl.ds(0, half + P_SIZE), pl.ds(0, width)],
        local_sem.at[0],
    )
    second_half = pltpu.make_async_copy(
        tile_hbm.at[pl.ds(half, half), :], ext.at[1, pl.ds(0, half), pl.ds(0, width)], local_sem.at[1]
    )

    @pl.when(gz == 0)
    def _():
        first_half.start()

    @pl.when(gz == 1)
    def _():
        second_half.start()

    pool_rows = jnp.where((iota((rows // DOWN, rows), 1) >> 3) == iota((rows // DOWN, rows), 0), 1.0, 0.0)
    lanes = iota((width, 2 * P_SIZE), 1)
    block = iota((width, 2 * P_SIZE), 0) >> 3
    pool = jnp.where(block == (lanes & (P_SIZE - 1)), 1.0, 0.0).astype(BF16)
    pool_rows = pool_rows.astype(BF16)
    load.wait()
    piece = bdot(pool_rows, tile[...])
    terms = []
    for _ in range(3):
        terms.append(piece.astype(BF16))
        piece = piece - terms[-1].astype(F32)
    packed = bdot(jnp.concatenate(terms, axis=1), jnp.concatenate([pool] * 3, axis=0))
    packed = jnp.where(iota((HALF, 2 * P_SIZE), 1) < P_SIZE, packed[:HALF], packed[HALF:])
    packed = (packed * (1.0 / DOWN)).astype(BF16)
    own[...] = packed
    coarse[0, gz] = packed

    @pl.when(gx + 1 >= n_gx)
    def _():
        ext[:, :, width:] = jnp.zeros((2, half + P_SIZE, edge), BF16)
        coarse[1] = jnp.zeros(coarse.shape[1:], BF16)

    @pl.when((gz == 1) & (gy + 1 >= n_gy))
    def _():
        ext[:, half:, :width] = jnp.zeros((2, P_SIZE, width), BF16)
        ext[:, half:, width:] = jnp.zeros((2, P_SIZE, edge), BF16)

    pl.semaphore_wait(barrier, count)

    long, short = half // 2, P_SIZE // 2

    def halo_copy(kind, c, section, x, y):
        if c == 0:
            source, target = (
                (pl.ds(0, half + P_SIZE), pl.ds(0, half + P_SIZE)),
                (pl.ds(half, half), pl.ds(0, half)),
                (pl.ds(0, P_SIZE), pl.ds(half, P_SIZE)),
            )[kind]
            source = tile.at[source, :]
            target = ext.at[section, target, pl.ds(0, width)]
        else:
            source, target = (
                (pl.ds(0, long + short), pl.ds(0, long + short)),
                (pl.ds(long + short, long), pl.ds(0, long)),
                (pl.ds(2 * long + short, short), pl.ds(long, short)),
            )[kind]
            source = packs.at[source, :]
            target = landed.at[section, target, :]
        slot = kind * 4 + c * 2
        return pltpu.make_async_remote_copy(
            src_ref=source,
            dst_ref=target,
            send_sem=send_sem.at[slot],
            recv_sem=recv_sem.at[slot + section],
            device_id=device(x, y, 0 if kind == 0 else 1),
            device_id_type=MESH,
        )

    def coarse_copy(x, z, place, section, source):
        return pltpu.make_async_remote_copy(
            src_ref=source,
            dst_ref=coarse.at[place, section],
            send_sem=csend.at[place, z],
            recv_sem=crecv.at[place, section],
            device_id=device(x, gy, z),
            device_id_type=MESH,
        )

    def to_left():
        return [coarse_copy(gx - 1, z, 1, gz, own) for z in range(2)]

    coarse_copy(gx, 1 - gz, 0, gz, own).start()

    @pl.when(gx >= 1)
    def _():
        for copy in to_left():
            copy.start()

    def tell(way, n):
        x = gx + 1 if way == 0 else gx - 1

        @pl.when((gz == 1) & (x >= 0) & (x < n_gx))
        def _():
            pl.semaphore_signal(
                known.at[way, n], inc=1, device_id=device(x, gy, 1), device_id_type=MESH
            )

    def relay_right():
        for n in range(n_gx - 1):

            @pl.when((gz == 1) & (gx >= 1 + n))
            def _():
                if n:
                    pl.semaphore_wait(known.at[0, n - 1], 1)
                if n < n_gx - 2:
                    tell(0, n)

    def relay_left():
        for n in range(n_gx - 1):

            @pl.when((gz == 1) & (gx + 1 + n < n_gx))
            def _():
                pl.semaphore_wait(known.at[1, n], 1)
                if n < n_gx - 2:
                    tell(1, n + 1)

    tell(1, 0)
    relay_right()

    def sends():
        out = []
        for c in (0, 1):
            for kind in range(3):
                use = gx - c >= 0
                if kind == 2:
                    use = use & (gy - 1 >= 0)
                elif c == 0:
                    use = use & (gz != kind)
                out.append((use, kind, c, gx - c, gy - 1 if kind == 2 else gy))
        return out

    for use, kind, c, x, y in sends():
        if c == 0:

            @pl.when(use)
            def _():
                halo_copy(kind, c, gz, x, y).start()

    @pl.when(gx >= 1)
    def _():
        put = 0
        for top, size in ((0, long), (half, short), (half, long), (0, short)):
            upper = tile[top : top + size, :128].astype(F32)
            lower = tile[top + size : top + 2 * size, :128].astype(F32)
            both = jnp.where(iota((size, 128), 1) < P_SIZE, upper, pltpu.roll(lower, P_SIZE, 1))
            packs[put : put + size] = both.astype(BF16)
            put += size

    for use, kind, c, x, y in sends():
        if c == 1:

            @pl.when(use)
            def _():
                halo_copy(kind, c, gz, x, y).start()

    def arrivals(c, kinds):
        for section in range(2):
            for kind in kinds:
                use = (gz == 0) if kind == 0 else (gz == 1)
                if c == 1:
                    use = use & (gx + 1 < n_gx)
                if kind == 2:
                    use = use & (gy + 1 < n_gy)
                elif c == 0:
                    use = use & (gz != section)

                @pl.when(use)
                def _():
                    halo_copy(kind, c, section, gx, gy).wait_recv()

    tile_width = mask.shape[1] * STRIDE
    patch_rows = half // STRIDE
    groups = mask.shape[1] // GROUP
    lanes = GROUP * HALF
    wide = GROUP * P_SIZE
    for copy in small_copies:
        copy.wait()
    roff, coff, off = fine_off[0], fine_off[1], coarse_off[0]
    for copy in table_copies:
        copy.wait()
    table_iy, table_ix = tiy_ref[...], tix_ref[...]

    span = tx.shape[0] // 2
    at = iota((span, 2 * lanes), 0) - coff - STRIDE * ((iota((span, 2 * lanes), 1) >> 5) & (GROUP - 1))
    inside = jnp.where((at >= 0) & (at < P_SIZE), 1.0, 0.0).astype(BF16)
    block = (2 * P_SIZE, 2 * lanes)
    from_left = (iota(block, 0) & (P_SIZE - 1)) - P_SIZE * ((iota(block, 1) >> 5) & (GROUP - 1)) - off
    plain = [tx[0 : 2 * P_SIZE], tx[span : span + 2 * P_SIZE]]
    for step in range(2):
        at_step = from_left + step * P_SIZE
        keep = jnp.where((at_step >= 0) & (at_step < P_SIZE), 1.0, 0.0).astype(BF16)
        for term in range(2):
            base = (2 * step + term) * 2 * P_SIZE
            ctab[base : base + 2 * P_SIZE] = plain[term] * keep

    nyquist = (iota((P_SIZE, lanes), 1) & (HALF - 1)) == 0
    frow = signed_of(iota((P_SIZE, wide), 0))

    def along_x_of(section, top, size, g):
        data = ext[section, pl.ds(top, size), g * lanes : g * lanes + span]
        value = bdot(jnp.concatenate([data, data], axis=1), tx[...])
        spec[section, 2 * g, pl.ds(top, size), :] = value[:, :lanes]
        spec[section, 2 * g + 1, pl.ds(top, size), :] = value[:, lanes:]

    inner = groups - 1

    @pl.when(gz == 0)
    def _():
        first_half.wait()

    @pl.when(gz == 1)
    def _():
        second_half.wait()

    def split(g, top, size):
        for section in range(2):
            for t in range(2):
                high, low = two_terms(spec[section, 2 * g + t, pl.ds(roff + top, size), :])
                part = slice((2 * g + t) * lanes, (2 * g + t + 1) * lanes)
                spec_high[section, top : top + size, part] = high
                spec_low[section, top : top + size, part] = low

    def forward(g, first_row, last_row):
        part = slice(g * 2 * lanes, (g + 1) * 2 * lanes)
        for row in range(first_row, last_row):
            window = slice(row * STRIDE, row * STRIDE + P_SIZE)
            first, second = (
                bdot(
                    ty[...],
                    jnp.concatenate(
                        [
                            spec_high[t, window, part],
                            spec_high[t, window, part],
                            spec_low[t, window, part],
                        ],
                        axis=0,
                    ),
                )
                for t in range(2)
            )
            for n, plane in enumerate(cross(first, second, 0, nyquist)):
                crossed[g * patch_rows + row, n] = plane
            yield

    upper_rows, middle_row = patch_rows - 2, half - STRIDE

    def upper(g):
        split(g, 0, middle_row)
        yield from forward(g, 0, upper_rows)

    def lower(g):
        split(g, middle_row, P_SIZE)
        yield from forward(g, upper_rows, patch_rows)

    def last_columns():
        for below in range(2):
            use = gx + 1 < n_gx
            if below:
                use = use & ((gz == 0) | (gy + 1 < n_gy))

            @pl.when(use)
            def _():
                for section in range(2):
                    top, size, source = (half, short, long) if below else (0, long, 0)
                    data = landed[section, source : source + size]
                    ext[section, top : top + size, width:] = data
                    data = pltpu.roll(data.astype(F32), P_SIZE, 1).astype(BF16)
                    ext[section, top + size : top + 2 * size, width:] = data

        for section in range(2):
            along_x_of(section, 0, half + P_SIZE, inner)

    relay_left()

    coarse_copy(gx, gz, 0, 1 - gz, own).wait_recv()

    @pl.when(gx + 1 < n_gx)
    def _():
        for section in range(2):
            coarse_copy(gx, 0, 1, section, own).wait_recv()

    def own_lines():
        tx[0:span] = tx[0:span] * inside
        tx[span:] = tx[span:] * inside
        yield
        for g in range(inner):
            along_x_of(gz, 0, half, g)
            yield

    beside = own_lines()

    def step(count):
        for _ in range(count):
            next(beside, None)

    left = iota((HALF, 2 * P_SIZE), 1) < P_SIZE
    ones = jnp.where((iota((wide, 128), 0) >> 6) == 0, 1.0, 0.0).astype(BF16)
    fcol = signed_of(iota((1, wide), 1) & (P_SIZE - 1))
    lines = []
    for section in range(2):
        terms = []
        for source in range(2):
            data = coarse[source, section].astype(F32)
            both = jnp.concatenate(
                [jnp.where(left, data, 0.0), jnp.where(left, 0.0, data)], axis=0
            ).astype(BF16)
            terms += [both, both]
        lines.append(jnp.concatenate(terms, axis=1))
    value = bdot(jnp.concatenate(lines, axis=0), ctab[...])
    step(BESIDE)
    first = forward_y(ty[...], value[:P_SIZE])
    second = forward_y(ty[...], value[P_SIZE:])
    step(BESIDE)
    hr, hi, yr, yi = cross(first, second, 0, nyquist)
    value = landscape(
        [(hr - jnp.where(nyquist, yi, 0.0), hi + jnp.where(nyquist, yr, 0.0))], table_iy, table_ix
    )
    step(BESIDE)
    top = segment_max(jnp.broadcast_to(jnp.max(value, axis=0, keepdims=True), (8, wide)))[0:1]
    step(BESIDE)
    weight = jnp.exp2(value - top)
    s0 = jnp.sum(weight, axis=0, keepdims=True)
    s1 = jnp.sum(weight * frow, axis=0, keepdims=True)
    rows = iota((8, wide), 0)
    both = jnp.where(rows == 0, s0, jnp.where(rows == 1, s1, jnp.where(rows == 2, s0 * fcol, 0.0)))
    total = exact_dot(both, ones)
    rows = iota((8, 128), 0)
    found = jnp.where(rows == 0, total[1:2] / total[0:1], total[2:3] / total[0:1])
    mine[...] = found
    flows[gx] = found

    def flow_copy(x, place, z=0):
        return pltpu.make_async_remote_copy(
            src_ref=mine,
            dst_ref=flows.at[place],
            send_sem=fsend.at[x, z],
            recv_sem=frecv.at[place],
            device_id=device(x, gy, z),
            device_id_type=MESH,
        )

    for x in range(n_gx):

        @pl.when((x != gx) & (gz == 1))
        def _():
            for z in range(2):
                flow_copy(x, gx, z).start()

    for _ in beside:
        pass
    arrivals(0, (0, 1))
    for g in range(inner):
        along_x_of(1 - gz, 0, half, g)
    for g in range(inner):
        for _ in upper(g):
            pass
    arrivals(0, (2,))
    for g in range(inner):
        for section in range(2):
            along_x_of(section, half, P_SIZE, g)
    for g in range(inner):
        for _ in lower(g):
            pass
    arrivals(1, (0, 1, 2))
    last_columns()
    for part in (upper, lower):
        for _ in part(inner):
            pass

    columns = mask.shape[1]
    side = columns // 2

    def lane_of(column):
        return (column & 1) * side + (column >> 1)

    put = jnp.where(lane_of(iota((wide, 128), 0) >> 6) == iota((wide, 128), 1), 1.0, 0.0)
    here = pl.ds(pl.multiple_of(gz * patch_rows, 8), patch_rows)
    place = jnp.where(lane_of(iota((columns, 128), 0)) == iota((columns, 128), 1), 1.0, 0.0)
    valid = bdot(mask[here, :].astype(F32).astype(BF16), place.astype(BF16))

    for x in range(n_gx):

        @pl.when(x != gx)
        def _():
            flow_copy(x, x).wait_recv()

    mean = sum(flows[x] for x in range(n_gx)) / float(n_gx)
    blended = [(0.5 * DOWN) * (flows[x] + mean) for x in range(n_gx)]

    def pick(column):
        centre = gx * tile_width + column * STRIDE + coff + P_SIZE // 2
        chosen = jnp.clip(((centre >> 3) - off) >> 6, 0, n_gx - 1)
        total = blended[0]
        for x in range(1, n_gx):
            total = jnp.where(chosen == x, blended[x], total)
        return total

    fky = signed_of(iota((P_SIZE, lanes), 0)) * (1.0 / P_SIZE)
    middle = iota((P_SIZE, lanes), 0) == HALF
    kx = (iota((1, lanes), 1) & (HALF - 1)).astype(F32) * (1.0 / P_SIZE)

    lane = iota((8, 128), 1)
    last_prior = pick(jnp.where(lane < side, 2 * lane, jnp.minimum(2 * (lane - side) + 1, columns - 1)))

    def backward(g):
        prior = pick(g * GROUP + (iota((8, lanes), 1) >> 5))
        dy, dx = prior[0:1], prior[1:2]
        eyr, eyi = cis(fky * dy)
        exr, exi = cis(kx * dx)
        nr, ni = cis(0.5 * dx)
        fr = jnp.where(nyquist, nr * eyr + jnp.where(middle, ni * eyi, 0.0), 0.0)
        eyi = jnp.where(middle, 0.0, eyi)
        fi = jnp.where(nyquist, nr * eyi, 0.0)
        er = eyr * exr - eyi * exi
        ei = eyr * exi + eyi * exr
        base = g * patch_rows
        units = []
        for unit in range(patch_rows):
            xr, xi, yr, yi = (crossed[base + unit, n] for n in range(4))
            hr = xr * er - xi * ei
            hi = xr * ei + xi * er
            units.append((hr - (yr * fi + yi * fr), hi + (yr * fr - yi * fi)))
        value = landscape(units, table_iy, table_ix)
        for unit in range(patch_rows):
            piece = value[unit * P_SIZE : (unit + 1) * P_SIZE]
            logits[base + unit] = piece
            peaks[base + unit : base + unit + 1] = jnp.max(piece, axis=0, keepdims=True)

    def weigh(g):
        rows = slice(g * patch_rows, (g + 1) * patch_rows)
        top = segment_max(peaks[rows])
        for row in range(patch_rows):
            n = g * patch_rows + row
            weight = jnp.exp2(logits[n] - top[row : row + 1])
            stats[0, n : n + 1] = jnp.sum(weight, axis=0, keepdims=True)
            stats[1, n : n + 1] = jnp.sum(weight * frow, axis=0, keepdims=True)

    for g in range(groups):
        backward(g)
        if g:
            weigh(g - 1)
    weigh(groups - 1)

    s0 = stats[0]
    sums = exact_dot(jnp.concatenate([s0, stats[1], s0 * fcol], axis=0), put.astype(BF16))
    units = groups * patch_rows

    def gather(stat):
        total = None
        for g in range(groups):
            piece = sums[stat * units + g * patch_rows : stat * units + (g + 1) * patch_rows]
            if g:
                piece = pltpu.roll(piece, g * GROUP // 2, 1)
            total = piece if total is None else total + piece
        return total

    den, along_y, along_x = gather(0), gather(1), gather(2)
    den = jnp.where(iota((patch_rows, 128), 1) < columns, den, 1.0)
    same = ((iota((patch_rows, 128), 0) + gz) & 1) == 0
    kept = []
    for c, total in enumerate((along_y, along_x)):
        value = last_prior[c : c + 1] + valid * (total / den)
        odd = pltpu.roll(value, 128 - side, 1)
        given[c] = jnp.where(same, odd, value)
        kept.append(jnp.where(same, value, odd))
    back = pltpu.make_async_remote_copy(
        src_ref=given,
        dst_ref=got,
        send_sem=back_sem.at[0],
        recv_sem=back_sem.at[1],
        device_id=device(gx, gy, 1 - gz),
        device_id_type=MESH,
    )
    back.start()
    coarse_copy(gx, 1 - gz, 0, gz, own).wait_send()

    @pl.when(gx >= 1)
    def _():
        for copy in to_left():
            copy.wait_send()

    for x in range(n_gx):

        @pl.when((x != gx) & (gz == 1))
        def _():
            for z in range(2):
                flow_copy(x, gx, z).wait_send()

    for use, kind, c, x, y in sends():

        @pl.when(use)
        def _():
            halo_copy(kind, c, gz, x, y).wait_send()

    back.wait()
    upper = jnp.full((patch_rows, 128), gz, jnp.int32) == 0
    for c in range(2):
        value = jnp.concatenate(
            [jnp.where(upper, kept[c], got[c]), jnp.where(upper, got[c], kept[c])], axis=0
        )
        out[c] = jnp.transpose(value)[:side]


def solution(mesh):
    n_gx, n_gy = mesh.shape["gx"], mesh.shape["gy"]
    tables = make_tables()
    vmem = pl.BlockSpec(memory_space=pltpu.VMEM)
    anywhere = pl.BlockSpec(memory_space=pl.ANY)

    def local(sections, fine_offsets, coarse_offset, tissue_mask):
        tile = sections[0]
        rows, width = tile.shape
        half = rows // 2
        assert rows // DOWN == P_SIZE and width // DOWN == P_SIZE and n_gx % GROUP == 0
        patch_rows, patch_cols = half // STRIDE, width // STRIDE
        dma = pltpu.SemaphoreType.DMA
        groups = patch_cols // GROUP
        units = patch_rows * groups
        wide = GROUP * P_SIZE
        flow = pl.pallas_call(
            lambda *refs: kernel(n_gx, n_gy, *refs),
            out_shape=pltpu.VMEM((2, patch_cols // 2, 2 * patch_rows), F32),
            in_specs=[anywhere] * (4 + len(tables)),
            out_specs=vmem,
            scratch_shapes=[pltpu.VMEM(t.shape, BF16) for t in tables]
            + [
                pltpu.VMEM((rows, width), BF16),
                pltpu.VMEM((2, half + P_SIZE, width + 128), BF16),
                pltpu.VMEM((2, 2, HALF, 2 * P_SIZE), BF16),
                pltpu.VMEM((HALF, 2 * P_SIZE), BF16),
                pltpu.VMEM((2, patch_rows, 128), F32),
                pltpu.VMEM((2, patch_rows, 128), F32),
                pltpu.VMEM((2, 2 * groups, half + P_SIZE, wide // 2), F32),
                pltpu.VMEM((2, half + STRIDE, groups * wide), BF16),
                pltpu.VMEM((2, half + STRIDE, groups * wide), BF16),
                pltpu.VMEM((8 * P_SIZE, wide), BF16),
                pltpu.VMEM((units, P_SIZE, wide), F32),
                pltpu.VMEM((units, wide), F32),
                pltpu.VMEM((2, units, wide), F32),
                dma((12,)),
                dma((12,)),
                dma((2, 2)),
                dma((2, 2)),
                dma((3,)),
                dma((len(tables),)),
                dma((2,)),
                pltpu.SMEM(fine_offsets.shape, jnp.int32),
                pltpu.SMEM((1,), jnp.int32),
                pltpu.VMEM(tissue_mask.shape, jnp.int32),
                dma((3,)),
                pltpu.VMEM((half + P_SIZE, 128), BF16),
                pltpu.VMEM((2, (half + P_SIZE) // 2, 128), BF16),
                pltpu.VMEM((units, 4, P_SIZE, wide // 2), F32),
                pltpu.VMEM((8, 128), F32),
                pltpu.VMEM((n_gx, 8, 128), F32),
                dma((n_gx, 2)),
                dma((n_gx,)),
                pltpu.SemaphoreType.REGULAR((2, n_gx)),
            ],
            compiler_params=pltpu.CompilerParams(
                collective_id=0, has_side_effects=True, vmem_limit_bytes=VMEM_BYTES
            ),
            name="flow",
        )(fine_offsets, coarse_offset, tile, tissue_mask, *[jnp.asarray(t) for t in tables])
        return jnp.swapaxes(flow, 1, 2)[:, None]

    placed = (P("gz", ("pairs", "gy"), "gx"), P("pairs"), P("pairs"), P(("pairs", "gy"), "gx"))
    return jax.shard_map(
        local,
        mesh=mesh,
        in_specs=placed,
        out_specs=P(None, "gz", ("pairs", "gy"), "gx"),
        check_vma=False,
    )
```

```python
import jax
import jax.numpy as jnp
import numpy as np
from jax import lax
from jax.experimental import pallas as pl
from jax.experimental.pallas import tpu as pltpu
from jax.sharding import PartitionSpec as P

P_SIZE = 64
STRIDE = 32
DOWN = 8
HALF = P_SIZE // 2
GROUP = 4
SHARP = 12.0
BESIDE = 1
VMEM_BYTES = 56 * 2**20
MESH = pl.DeviceIdType.MESH
F32 = jnp.float32
BF16 = jnp.bfloat16


def split_table(table):
    high = np.asarray(table, np.float32).astype(jnp.bfloat16)
    low = (np.asarray(table, np.float64) - high.astype(np.float64)).astype(np.float32)
    return high, low.astype(jnp.bfloat16)


def make_tables():
    turn = 2.0 * np.pi / P_SIZE
    k = np.arange(HALF)
    x = np.arange(2 * GROUP * STRIDE)
    angle = turn * (np.outer(x, k) % P_SIZE)
    real = np.cos(angle)
    imag = -np.sin(angle)
    imag[:, 0] = np.cos(np.pi * x)
    forward_x = np.concatenate([np.tile(real, (1, GROUP)), np.tile(imag, (1, GROUP))], axis=1)
    high, low = split_table(forward_x)
    table_x = np.concatenate([high, low], axis=0)
    ky = np.arange(P_SIZE)
    angle = turn * (np.outer(ky, ky) % P_SIZE)
    high, low = split_table(np.concatenate([np.cos(angle), np.sin(angle)], axis=0))
    table_y = np.concatenate([high, low, high], axis=1)
    angle = turn * (np.outer(ky, ky) % P_SIZE)
    cosine, sine = np.cos(angle), np.sin(angle)
    inverse_y = np.block([[cosine, -sine], [sine, cosine]])
    high, low = split_table(inverse_y)
    table_iy = np.concatenate([high, low, high], axis=1)
    angle = turn * (np.outer(k, ky) % P_SIZE)
    real = 2.0 * np.cos(angle)
    imag = -2.0 * np.sin(angle)
    real[0] = 1.0
    imag[0] = np.cos(np.pi * ky)
    scale = SHARP * np.log2(np.e) / float(P_SIZE) ** 4
    eye = np.eye(GROUP)
    inverse_x = np.concatenate([np.kron(eye, real), np.kron(eye, imag)], axis=0) * scale
    high, low = split_table(inverse_x)
    table_ix = np.concatenate([high, high, low], axis=0)
    return table_x, table_y, table_iy, table_ix


def iota(shape, dim):
    return lax.broadcasted_iota(jnp.int32, shape, dim)


def two_terms(value):
    high = value.astype(BF16)
    return high, (value - high.astype(F32)).astype(BF16)


def bdot(a, b):
    return jnp.dot(a, b, preferred_element_type=F32)


def signed_of(index):
    return jnp.where(index >= HALF, index - P_SIZE, index).astype(F32)


def cis(turns):
    rest = turns - jnp.floor(turns + 0.5)
    a = rest * np.float32(np.pi)
    q = a * a
    s = np.float32(-1 / 39916800.0)
    for c in (1 / 362880.0, -1 / 5040.0, 1 / 120.0, -1 / 6.0, 1.0):
        s = s * q + np.float32(c)
    s = s * a
    c = np.float32(1 / 479001600.0)
    for d in (-1 / 3628800.0, 1 / 40320.0, -1 / 720.0, 1 / 24.0, -0.5, 1.0):
        c = c * q + np.float32(d)
    return 1.0 - 2.0 * s * s, 2.0 * s * c


def segment_max(value):
    width = value.shape[1]
    place = iota(value.shape, 1) & (P_SIZE - 1)
    step = 1
    while step < P_SIZE:
        near = pltpu.roll(value, step, 1)
        far = pltpu.roll(value, width - P_SIZE + step, 1)
        value = jnp.maximum(value, jnp.where(place >= step, near, far))
        step *= 2
    return value


def forward_y(table, spectrum_x):
    high, low = two_terms(spectrum_x)
    return bdot(table, jnp.concatenate([high, high, low], axis=0))


def planes(product, unit):
    base = unit * 2 * P_SIZE
    lanes = GROUP * HALF
    cosine = product[base : base + P_SIZE]
    sine = product[base + P_SIZE : base + 2 * P_SIZE]
    return cosine[:, :lanes], sine[:, :lanes], cosine[:, lanes:], sine[:, lanes:]


def cross(first, second, unit, nyquist):
    a1, a2, a3, a4 = planes(first, unit)
    b1, b2, b3, b4 = planes(second, unit)
    ar = a1 + jnp.where(nyquist, 0.0, a4)
    ai = jnp.where(nyquist, 0.0, a3) - a2
    br = b1 + jnp.where(nyquist, 0.0, b4)
    bi = jnp.where(nyquist, 0.0, b3) - b2
    return (br * ar + bi * ai, bi * ar - br * ai, b3 * a3 + b4 * a4, b3 * a4 - b4 * a3)


def landscape(units, table_iy, table_ix):
    stacked = []
    for zr, zi in units:
        high, low = two_terms(jnp.concatenate([zr, zi], axis=0))
        stacked.append(jnp.concatenate([high, high, low], axis=0))
    back = bdot(table_iy, jnp.concatenate(stacked, axis=1) if len(stacked) > 1 else stacked[0])
    lanes = GROUP * HALF
    rows = []
    for unit in range(len(units)):
        piece = back[:, unit * lanes : (unit + 1) * lanes]
        rows.append(jnp.concatenate([piece[:P_SIZE], piece[P_SIZE:]], axis=1))
    value = jnp.concatenate(rows, axis=0) if len(rows) > 1 else rows[0]
    high, low = two_terms(value)
    return bdot(jnp.concatenate([high, low, high], axis=1), table_ix)


def exact_dot(a, b):
    terms = []
    for _ in range(3):
        terms.append(a.astype(BF16))
        a = a - terms[-1].astype(F32)
    return bdot(jnp.concatenate(terms, axis=1), jnp.concatenate([b, b, b], axis=0))


def kernel(
    n_gx, n_gy, fine_hbm, coarse_hbm, tile_hbm, mask_hbm, *rest
):
    hbm_tables, (out,), scratch = rest[:4], rest[4:5], rest[5:]
    table_refs, scratch = scratch[:4], scratch[4:]
    (tile, ext, coarse, own, given, got, spec, spec_high, spec_low, ctab, logits, peaks, stats) = scratch[:13]
    send_sem, recv_sem, csend, crecv, local_sem, table_sem, back_sem = scratch[13:20]
    fine_off, coarse_off, mask, small_sem, packs, landed, crossed = scratch[20:27]
    mine, flows, fsend, frecv, known = scratch[27:]
    tx, ty, tiy_ref, tix_ref = table_refs
    pairs, gx, gy, gz = (lax.axis_index(a) for a in ("pairs", "gx", "gy", "gz"))
    rows, width = tile.shape
    half = rows // 2
    edge = ext.shape[2] - width

    def device(x, y, z):
        return (pairs, x, y, z)

    load = pltpu.make_async_copy(tile_hbm, tile, local_sem.at[2])
    load.start()
    small_copies = [
        pltpu.make_async_copy(source, target, small_sem.at[n])
        for n, (source, target) in enumerate(
            ((fine_hbm, fine_off), (coarse_hbm, coarse_off), (mask_hbm, mask))
        )
    ]
    for copy in small_copies:
        copy.start()

    barrier = pltpu.get_barrier_semaphore()
    greeted = [(gx, gy, 1 - gz, None)]
    greeted.append((gx - 1, gy, 1, (gz == 1) & (gx >= 1)))
    for z in range(2):
        greeted.append((gx + 1, gy, z, gx + 1 < n_gx))
    for x in (gx, gx + 1):
        for z in range(2):
            greeted.append((x, gy + 1, z, (gz == 1) & (gy + 1 < n_gy) & (x < n_gx)))
    for x, y, z, use in greeted:

        def greet():
            pl.semaphore_signal(barrier, inc=1, device_id=device(x, y, z), device_id_type=MESH)

        if use is None:
            greet()
        else:
            pl.when(use)(greet)

    has_left = jnp.where(gx >= 1, 1, 0)
    count = 1 + 2 * has_left + jnp.where((gz == 1) & (gx + 1 < n_gx), 1, 0) + jnp.where(gy >= 1, 1 + has_left, 0)

    table_copies = [
        pltpu.make_async_copy(source, target, table_sem.at[n])
        for n, (source, target) in enumerate(zip(hbm_tables, table_refs))
    ]
    for copy in table_copies:
        copy.start()
    first_half = pltpu.make_async_copy(
        tile_hbm.at[pl.ds(0, half + P_SIZE), :],
        ext.at[0, pl.ds(0, half + P_SIZE), pl.ds(0, width)],
        local_sem.at[0],
    )
    second_half = pltpu.make_async_copy(
        tile_hbm.at[pl.ds(half, half), :], ext.at[1, pl.ds(0, half), pl.ds(0, width)], local_sem.at[1]
    )

    @pl.when(gz == 0)
    def _():
        first_half.start()

    @pl.when(gz == 1)
    def _():
        second_half.start()

    pool_rows = jnp.where((iota((rows // DOWN, rows), 1) >> 3) == iota((rows // DOWN, rows), 0), 1.0, 0.0)
    lanes = iota((width, 2 * P_SIZE), 1)
    block = iota((width, 2 * P_SIZE), 0) >> 3
    pool = jnp.where(block == (lanes & (P_SIZE - 1)), 1.0, 0.0).astype(BF16)
    pool_rows = pool_rows.astype(BF16)
    load.wait()
    piece = bdot(pool_rows, tile[...])
    terms = []
    for _ in range(3):
        terms.append(piece.astype(BF16))
        piece = piece - terms[-1].astype(F32)
    packed = bdot(jnp.concatenate(terms, axis=1), jnp.concatenate([pool] * 3, axis=0))
    packed = jnp.where(iota((HALF, 2 * P_SIZE), 1) < P_SIZE, packed[:HALF], packed[HALF:])
    packed = (packed * (1.0 / DOWN)).astype(BF16)
    own[...] = packed
    coarse[0, gz] = packed

    @pl.when(gx + 1 >= n_gx)
    def _():
        ext[:, :, width:] = jnp.zeros((2, half + P_SIZE, edge), BF16)
        coarse[1] = jnp.zeros(coarse.shape[1:], BF16)

    @pl.when((gz == 1) & (gy + 1 >= n_gy))
    def _():
        ext[:, half:, :width] = jnp.zeros((2, P_SIZE, width), BF16)
        ext[:, half:, width:] = jnp.zeros((2, P_SIZE, edge), BF16)

    pl.semaphore_wait(barrier, count)

    long, short = half // 2, P_SIZE // 2

    def halo_copy(kind, c, section, x, y):
        if c == 0:
            source, target = (
                (pl.ds(0, half + P_SIZE), pl.ds(0, half + P_SIZE)),
                (pl.ds(half, half), pl.ds(0, half)),
                (pl.ds(0, P_SIZE), pl.ds(half, P_SIZE)),
            )[kind]
            source = tile.at[source, :]
            target = ext.at[section, target, pl.ds(0, width)]
        else:
            source, target = (
                (pl.ds(0, long + short), pl.ds(0, long + short)),
                (pl.ds(long + short, long), pl.ds(0, long)),
                (pl.ds(2 * long + short, short), pl.ds(long, short)),
            )[kind]
            source = packs.at[source, :]
            target = landed.at[section, target, :]
        slot = kind * 4 + c * 2
        return pltpu.make_async_remote_copy(
            src_ref=source,
            dst_ref=target,
            send_sem=send_sem.at[slot],
            recv_sem=recv_sem.at[slot + section],
            device_id=device(x, y, 0 if kind == 0 else 1),
            device_id_type=MESH,
        )

    def coarse_copy(x, z, place, section, source):
        return pltpu.make_async_remote_copy(
            src_ref=source,
            dst_ref=coarse.at[place, section],
            send_sem=csend.at[place, z],
            recv_sem=crecv.at[place, section],
            device_id=device(x, gy, z),
            device_id_type=MESH,
        )

    def to_left():
        return [coarse_copy(gx - 1, z, 1, gz, own) for z in range(2)]

    coarse_copy(gx, 1 - gz, 0, gz, own).start()

    @pl.when(gx >= 1)
    def _():
        for copy in to_left():
            copy.start()

    def tell(way, n):
        x = gx + 1 if way == 0 else gx - 1

        @pl.when((gz == 1) & (x >= 0) & (x < n_gx))
        def _():
            pl.semaphore_signal(
                known.at[way, n], inc=1, device_id=device(x, gy, 1), device_id_type=MESH
            )

    def relay_right():
        for n in range(n_gx - 1):

            @pl.when((gz == 1) & (gx >= 1 + n))
            def _():
                if n:
                    pl.semaphore_wait(known.at[0, n - 1], 1)
                if n < n_gx - 2:
                    tell(0, n)

    def relay_left():
        for n in range(n_gx - 1):

            @pl.when((gz == 1) & (gx + 1 + n < n_gx))
            def _():
                pl.semaphore_wait(known.at[1, n], 1)
                if n < n_gx - 2:
                    tell(1, n + 1)

    tell(1, 0)
    relay_right()

    def sends():
        out = []
        for c in (0, 1):
            for kind in range(3):
                use = gx - c >= 0
                if kind == 2:
                    use = use & (gy - 1 >= 0)
                elif c == 0:
                    use = use & (gz != kind)
                out.append((use, kind, c, gx - c, gy - 1 if kind == 2 else gy))
        return out

    for use, kind, c, x, y in sends():
        if c == 0:

            @pl.when(use)
            def _():
                halo_copy(kind, c, gz, x, y).start()

    @pl.when(gx >= 1)
    def _():
        put = 0
        for top, size in ((0, long), (half, short), (half, long), (0, short)):
            upper = tile[top : top + size, :128].astype(F32)
            lower = tile[top + size : top + 2 * size, :128].astype(F32)
            both = jnp.where(iota((size, 128), 1) < P_SIZE, upper, pltpu.roll(lower, P_SIZE, 1))
            packs[put : put + size] = both.astype(BF16)
            put += size

    for use, kind, c, x, y in sends():
        if c == 1:

            @pl.when(use)
            def _():
                halo_copy(kind, c, gz, x, y).start()

    def arrivals(c, kinds):
        for section in range(2):
            for kind in kinds:
                use = (gz == 0) if kind == 0 else (gz == 1)
                if c == 1:
                    use = use & (gx + 1 < n_gx)
                if kind == 2:
                    use = use & (gy + 1 < n_gy)
                elif c == 0:
                    use = use & (gz != section)

                @pl.when(use)
                def _():
                    halo_copy(kind, c, section, gx, gy).wait_recv()

    tile_width = mask.shape[1] * STRIDE
    patch_rows = half // STRIDE
    groups = mask.shape[1] // GROUP
    lanes = GROUP * HALF
    wide = GROUP * P_SIZE
    for copy in small_copies:
        copy.wait()
    roff, coff, off = fine_off[0], fine_off[1], coarse_off[0]
    for copy in table_copies:
        copy.wait()
    table_iy, table_ix = tiy_ref[...], tix_ref[...]

    span = tx.shape[0] // 2
    at = iota((span, 2 * lanes), 0) - coff - STRIDE * ((iota((span, 2 * lanes), 1) >> 5) & (GROUP - 1))
    inside = jnp.where((at >= 0) & (at < P_SIZE), 1.0, 0.0).astype(BF16)
    block = (2 * P_SIZE, 2 * lanes)
    from_left = (iota(block, 0) & (P_SIZE - 1)) - P_SIZE * ((iota(block, 1) >> 5) & (GROUP - 1)) - off
    plain = [tx[0 : 2 * P_SIZE], tx[span : span + 2 * P_SIZE]]
    for step in range(2):
        at_step = from_left + step * P_SIZE
        keep = jnp.where((at_step >= 0) & (at_step < P_SIZE), 1.0, 0.0).astype(BF16)
        for term in range(2):
            base = (2 * step + term) * 2 * P_SIZE
            ctab[base : base + 2 * P_SIZE] = plain[term] * keep

    nyquist = (iota((P_SIZE, lanes), 1) & (HALF - 1)) == 0
    frow = signed_of(iota((P_SIZE, wide), 0))

    def along_x_of(section, top, size, g):
        data = ext[section, pl.ds(top, size), g * lanes : g * lanes + span]
        value = bdot(jnp.concatenate([data, data], axis=1), tx[...])
        spec[section, 2 * g, pl.ds(top, size), :] = value[:, :lanes]
        spec[section, 2 * g + 1, pl.ds(top, size), :] = value[:, lanes:]

    inner = groups - 1

    @pl.when(gz == 0)
    def _():
        first_half.wait()

    @pl.when(gz == 1)
    def _():
        second_half.wait()

    def split(g, top, size):
        for section in range(2):
            for t in range(2):
                high, low = two_terms(spec[section, 2 * g + t, pl.ds(roff + top, size), :])
                part = slice((2 * g + t) * lanes, (2 * g + t + 1) * lanes)
                spec_high[section, top : top + size, part] = high
                spec_low[section, top : top + size, part] = low

    def forward(g, first_row, last_row):
        part = slice(g * 2 * lanes, (g + 1) * 2 * lanes)
        for row in range(first_row, last_row):
            window = slice(row * STRIDE, row * STRIDE + P_SIZE)
            first, second = (
                bdot(
                    ty[...],
                    jnp.concatenate(
                        [
                            spec_high[t, window, part],
                            spec_high[t, window, part],
                            spec_low[t, window, part],
                        ],
                        axis=0,
                    ),
                )
                for t in range(2)
            )
            for n, plane in enumerate(cross(first, second, 0, nyquist)):
                crossed[g * patch_rows + row, n] = plane
            yield

    upper_rows, middle_row = patch_rows - 2, half - STRIDE

    def upper(g):
        split(g, 0, middle_row)
        yield from forward(g, 0, upper_rows)

    def lower(g):
        split(g, middle_row, P_SIZE)
        yield from forward(g, upper_rows, patch_rows)

    def last_columns():
        for below in range(2):
            use = gx + 1 < n_gx
            if below:
                use = use & ((gz == 0) | (gy + 1 < n_gy))

            @pl.when(use)
            def _():
                for section in range(2):
                    top, size, source = (half, short, long) if below else (0, long, 0)
                    data = landed[section, source : source + size]
                    ext[section, top : top + size, width:] = data
                    data = pltpu.roll(data.astype(F32), P_SIZE, 1).astype(BF16)
                    ext[section, top + size : top + 2 * size, width:] = data

        for section in range(2):
            along_x_of(section, 0, half + P_SIZE, inner)

    relay_left()

    coarse_copy(gx, gz, 0, 1 - gz, own).wait_recv()

    @pl.when(gx + 1 < n_gx)
    def _():
        for section in range(2):
            coarse_copy(gx, 0, 1, section, own).wait_recv()

    def own_lines():
        tx[0:span] = tx[0:span] * inside
        tx[span:] = tx[span:] * inside
        yield
        for g in range(inner):
            along_x_of(gz, 0, half, g)
            yield

    beside = own_lines()

    def step(count):
        for _ in range(count):
            next(beside, None)

    left = iota((HALF, 2 * P_SIZE), 1) < P_SIZE
    fcol = signed_of(iota((1, wide), 1) & (P_SIZE - 1))
    lines = []
    for section in range(2):
        terms = []
        for source in range(2):
            data = coarse[source, section].astype(F32)
            both = jnp.concatenate(
                [jnp.where(left, data, 0.0), jnp.where(left, 0.0, data)], axis=0
            ).astype(BF16)
            terms += [both, both]
        lines.append(jnp.concatenate(terms, axis=1))
    value = bdot(jnp.concatenate(lines, axis=0), ctab[...])
    step(BESIDE)
    first = forward_y(ty[...], value[:P_SIZE])
    second = forward_y(ty[...], value[P_SIZE:])
    step(BESIDE)
    hr, hi, yr, yi = cross(first, second, 0, nyquist)
    value = landscape(
        [(hr - jnp.where(nyquist, yi, 0.0), hi + jnp.where(nyquist, yr, 0.0))],
        table_iy,
        table_ix[:, : 2 * P_SIZE],
    )
    step(BESIDE)
    ours = iota((P_SIZE, 2 * P_SIZE), 1) < P_SIZE
    value = jnp.where(ours, value, -jnp.inf)
    top = jnp.broadcast_to(jnp.max(value, axis=0, keepdims=True), (8, 2 * P_SIZE))
    top = jnp.max(top, axis=1, keepdims=True)[0:1]
    step(BESIDE)
    weight = jnp.exp2(value - top)
    s0 = jnp.sum(weight, axis=0, keepdims=True)
    s1 = jnp.sum(weight * frow[:, : 2 * P_SIZE], axis=0, keepdims=True)
    rows = iota((8, 2 * P_SIZE), 0)
    both = jnp.where(rows == 0, s0, jnp.where(rows == 1, s1, s0 * fcol[:, : 2 * P_SIZE]))
    total = jnp.sum(both, axis=1, keepdims=True)
    rows = iota((8, 128), 0)
    found = jnp.where(rows == 0, total[1:2] / total[0:1], total[2:3] / total[0:1])
    mine[...] = found
    flows[gx] = found

    def flow_copy(x, place, z=0):
        return pltpu.make_async_remote_copy(
            src_ref=mine,
            dst_ref=flows.at[place],
            send_sem=fsend.at[x, z],
            recv_sem=frecv.at[place],
            device_id=device(x, gy, z),
            device_id_type=MESH,
        )

    for x in range(n_gx):

        @pl.when((x != gx) & (gz == 1))
        def _():
            for z in range(2):
                flow_copy(x, gx, z).start()

    for _ in beside:
        pass
    arrivals(0, (0, 1))
    for g in range(inner):
        along_x_of(1 - gz, 0, half, g)
    for g in range(inner):
        for _ in upper(g):
            pass
    arrivals(0, (2,))
    for g in range(inner):
        for section in range(2):
            along_x_of(section, half, P_SIZE, g)
    for g in range(inner):
        for _ in lower(g):
            pass
    arrivals(1, (0, 1, 2))
    last_columns()
    for part in (upper, lower):
        for _ in part(inner):
            pass

    columns = mask.shape[1]
    side = columns // 2

    def lane_of(column):
        return (column & 1) * side + (column >> 1)

    put = jnp.where(lane_of(iota((wide, 128), 0) >> 6) == iota((wide, 128), 1), 1.0, 0.0)
    here = pl.ds(pl.multiple_of(gz * patch_rows, 8), patch_rows)
    place = jnp.where(lane_of(iota((columns, 128), 0)) == iota((columns, 128), 1), 1.0, 0.0)
    valid = bdot(mask[here, :].astype(F32).astype(BF16), place.astype(BF16))

    for x in range(n_gx):

        @pl.when(x != gx)
        def _():
            flow_copy(x, x).wait_recv()

    mean = sum(flows[x] for x in range(n_gx)) / float(n_gx)
    blended = [(0.5 * DOWN) * (flows[x] + mean) for x in range(n_gx)]

    def pick(column):
        centre = gx * tile_width + column * STRIDE + coff + P_SIZE // 2
        chosen = jnp.clip(((centre >> 3) - off) >> 6, 0, n_gx - 1)
        total = blended[0]
        for x in range(1, n_gx):
            total = jnp.where(chosen == x, blended[x], total)
        return total

    fky = signed_of(iota((P_SIZE, lanes), 0)) * (1.0 / P_SIZE)
    middle = iota((P_SIZE, lanes), 0) == HALF
    kx = (iota((1, lanes), 1) & (HALF - 1)).astype(F32) * (1.0 / P_SIZE)

    lane = iota((8, 128), 1)
    last_prior = pick(jnp.where(lane < side, 2 * lane, jnp.minimum(2 * (lane - side) + 1, columns - 1)))

    def backward(g):
        prior = pick(g * GROUP + (iota((8, lanes), 1) >> 5))
        dy, dx = prior[0:1], prior[1:2]
        eyr, eyi = cis(fky * dy)
        exr, exi = cis(kx * dx)
        nr, ni = cis(0.5 * dx)
        fr = jnp.where(nyquist, nr * eyr + jnp.where(middle, ni * eyi, 0.0), 0.0)
        eyi = jnp.where(middle, 0.0, eyi)
        fi = jnp.where(nyquist, nr * eyi, 0.0)
        er = eyr * exr - eyi * exi
        ei = eyr * exi + eyi * exr
        base = g * patch_rows
        units = []
        for unit in range(patch_rows):
            xr, xi, yr, yi = (crossed[base + unit, n] for n in range(4))
            hr = xr * er - xi * ei
            hi = xr * ei + xi * er
            units.append((hr - (yr * fi + yi * fr), hi + (yr * fr - yi * fi)))
        value = landscape(units, table_iy, table_ix)
        for unit in range(patch_rows):
            piece = value[unit * P_SIZE : (unit + 1) * P_SIZE]
            logits[base + unit] = piece
            peaks[base + unit : base + unit + 1] = jnp.max(piece, axis=0, keepdims=True)

    def weigh(g):
        rows = slice(g * patch_rows, (g + 1) * patch_rows)
        top = segment_max(peaks[rows])
        for row in range(patch_rows):
            n = g * patch_rows + row
            weight = jnp.exp2(logits[n] - top[row : row + 1])
            stats[0, n : n + 1] = jnp.sum(weight, axis=0, keepdims=True)
            stats[1, n : n + 1] = jnp.sum(weight * frow, axis=0, keepdims=True)

    for g in range(groups):
        backward(g)
        if g:
            weigh(g - 1)
    weigh(groups - 1)

    s0 = stats[0]
    sums = exact_dot(jnp.concatenate([s0, stats[1], s0 * fcol], axis=0), put.astype(BF16))
    units = groups * patch_rows

    def gather(stat):
        total = None
        for g in range(groups):
            piece = sums[stat * units + g * patch_rows : stat * units + (g + 1) * patch_rows]
            if g:
                piece = pltpu.roll(piece, g * GROUP // 2, 1)
            total = piece if total is None else total + piece
        return total

    den, along_y, along_x = gather(0), gather(1), gather(2)
    den = jnp.where(iota((patch_rows, 128), 1) < columns, den, 1.0)
    same = ((iota((patch_rows, 128), 0) + gz) & 1) == 0
    kept = []
    for c, total in enumerate((along_y, along_x)):
        value = last_prior[c : c + 1] + valid * (total / den)
        odd = pltpu.roll(value, 128 - side, 1)
        given[c] = jnp.where(same, odd, value)
        kept.append(jnp.where(same, value, odd))
    back = pltpu.make_async_remote_copy(
        src_ref=given,
        dst_ref=got,
        send_sem=back_sem.at[0],
        recv_sem=back_sem.at[1],
        device_id=device(gx, gy, 1 - gz),
        device_id_type=MESH,
    )
    back.start()
    coarse_copy(gx, 1 - gz, 0, gz, own).wait_send()

    @pl.when(gx >= 1)
    def _():
        for copy in to_left():
            copy.wait_send()

    for x in range(n_gx):

        @pl.when((x != gx) & (gz == 1))
        def _():
            for z in range(2):
                flow_copy(x, gx, z).wait_send()

    for use, kind, c, x, y in sends():

        @pl.when(use)
        def _():
            halo_copy(kind, c, gz, x, y).wait_send()

    back.wait()
    upper = jnp.full((patch_rows, 128), gz, jnp.int32) == 0
    for c in range(2):
        value = jnp.concatenate(
            [jnp.where(upper, kept[c], got[c]), jnp.where(upper, got[c], kept[c])], axis=0
        )
        out[c] = jnp.transpose(value)[:side]


def solution(mesh):
    n_gx, n_gy = mesh.shape["gx"], mesh.shape["gy"]
    tables = make_tables()
    vmem = pl.BlockSpec(memory_space=pltpu.VMEM)
    anywhere = pl.BlockSpec(memory_space=pl.ANY)

    def local(sections, fine_offsets, coarse_offset, tissue_mask):
        tile = sections[0]
        rows, width = tile.shape
        half = rows // 2
        assert rows // DOWN == P_SIZE and width // DOWN == P_SIZE and n_gx % GROUP == 0
        patch_rows, patch_cols = half // STRIDE, width // STRIDE
        dma = pltpu.SemaphoreType.DMA
        groups = patch_cols // GROUP
        units = patch_rows * groups
        wide = GROUP * P_SIZE
        flow = pl.pallas_call(
            lambda *refs: kernel(n_gx, n_gy, *refs),
            out_shape=pltpu.VMEM((2, patch_cols // 2, 2 * patch_rows), F32),
            in_specs=[anywhere] * (4 + len(tables)),
            out_specs=vmem,
            scratch_shapes=[pltpu.VMEM(t.shape, BF16) for t in tables]
            + [
                pltpu.VMEM((rows, width), BF16),
                pltpu.VMEM((2, half + P_SIZE, width + 128), BF16),
                pltpu.VMEM((2, 2, HALF, 2 * P_SIZE), BF16),
                pltpu.VMEM((HALF, 2 * P_SIZE), BF16),
                pltpu.VMEM((2, patch_rows, 128), F32),
                pltpu.VMEM((2, patch_rows, 128), F32),
                pltpu.VMEM((2, 2 * groups, half + P_SIZE, wide // 2), F32),
                pltpu.VMEM((2, half + STRIDE, groups * wide), BF16),
                pltpu.VMEM((2, half + STRIDE, groups * wide), BF16),
                pltpu.VMEM((8 * P_SIZE, wide), BF16),
                pltpu.VMEM((units, P_SIZE, wide), F32),
                pltpu.VMEM((units, wide), F32),
                pltpu.VMEM((2, units, wide), F32),
                dma((12,)),
                dma((12,)),
                dma((2, 2)),
                dma((2, 2)),
                dma((3,)),
                dma((len(tables),)),
                dma((2,)),
                pltpu.SMEM(fine_offsets.shape, jnp.int32),
                pltpu.SMEM((1,), jnp.int32),
                pltpu.VMEM(tissue_mask.shape, jnp.int32),
                dma((3,)),
                pltpu.VMEM((half + P_SIZE, 128), BF16),
                pltpu.VMEM((2, (half + P_SIZE) // 2, 128), BF16),
                pltpu.VMEM((units, 4, P_SIZE, wide // 2), F32),
                pltpu.VMEM((8, 128), F32),
                pltpu.VMEM((n_gx, 8, 128), F32),
                dma((n_gx, 2)),
                dma((n_gx,)),
                pltpu.SemaphoreType.REGULAR((2, n_gx)),
            ],
            compiler_params=pltpu.CompilerParams(
                collective_id=0, has_side_effects=True, vmem_limit_bytes=VMEM_BYTES
            ),
            name="flow",
        )(fine_offsets, coarse_offset, tile, tissue_mask, *[jnp.asarray(t) for t in tables])
        return jnp.swapaxes(flow, 1, 2)[:, None]

    placed = (P("gz", ("pairs", "gy"), "gx"), P("pairs"), P("pairs"), P(("pairs", "gy"), "gx"))
    return jax.shard_map(
        local,
        mesh=mesh,
        in_specs=placed,
        out_specs=P(None, "gz", ("pairs", "gy"), "gx"),
        check_vma=False,
    )
```

```python
import jax
import jax.numpy as jnp
import numpy as np
from jax import lax
from jax.experimental import pallas as pl
from jax.experimental.pallas import tpu as pltpu
from jax.sharding import PartitionSpec as P

P_SIZE = 64
STRIDE = 32
DOWN = 8
HALF = P_SIZE // 2
GROUP = 4
SHARP = 12.0
BESIDE = 1
VMEM_BYTES = 56 * 2**20
MESH = pl.DeviceIdType.MESH
F32 = jnp.float32
BF16 = jnp.bfloat16


def split_table(table):
    high = np.asarray(table, np.float32).astype(jnp.bfloat16)
    low = (np.asarray(table, np.float64) - high.astype(np.float64)).astype(np.float32)
    return high, low.astype(jnp.bfloat16)


def make_tables():
    turn = 2.0 * np.pi / P_SIZE
    k = np.arange(HALF)
    x = np.arange(2 * GROUP * STRIDE)
    angle = turn * (np.outer(x, k) % P_SIZE)
    real = np.cos(angle)
    imag = -np.sin(angle)
    imag[:, 0] = np.cos(np.pi * x)
    forward_x = np.concatenate([np.tile(real, (1, GROUP)), np.tile(imag, (1, GROUP))], axis=1)
    high, low = split_table(forward_x)
    table_x = np.concatenate([high, low], axis=0)
    ky = np.arange(P_SIZE)
    angle = turn * (np.outer(ky, ky) % P_SIZE)
    high, low = split_table(np.concatenate([np.cos(angle), np.sin(angle)], axis=0))
    table_y = np.concatenate([high, low, high], axis=1)
    angle = turn * (np.outer(ky, ky) % P_SIZE)
    cosine, sine = np.cos(angle), np.sin(angle)
    inverse_y = np.block([[cosine, -sine], [sine, cosine]])
    high, low = split_table(inverse_y)
    table_iy = np.concatenate([high, low, high], axis=1)
    angle = turn * (np.outer(k, ky) % P_SIZE)
    real = 2.0 * np.cos(angle)
    imag = -2.0 * np.sin(angle)
    real[0] = 1.0
    imag[0] = np.cos(np.pi * ky)
    scale = SHARP * np.log2(np.e) / float(P_SIZE) ** 4
    eye = np.eye(GROUP)
    inverse_x = np.concatenate([np.kron(eye, real), np.kron(eye, imag)], axis=0) * scale
    high, low = split_table(inverse_x)
    table_ix = np.concatenate([high, high, low], axis=0)
    return table_x, table_y, table_iy, table_ix


def iota(shape, dim):
    return lax.broadcasted_iota(jnp.int32, shape, dim)


def two_terms(value):
    high = value.astype(BF16)
    return high, (value - high.astype(F32)).astype(BF16)


def bdot(a, b):
    return jnp.dot(a, b, preferred_element_type=F32)


def signed_of(index):
    return jnp.where(index >= HALF, index - P_SIZE, index).astype(F32)


def cis(turns):
    rest = turns - jnp.floor(turns + 0.5)
    a = rest * np.float32(np.pi)
    q = a * a
    s = np.float32(-1 / 39916800.0)
    for c in (1 / 362880.0, -1 / 5040.0, 1 / 120.0, -1 / 6.0, 1.0):
        s = s * q + np.float32(c)
    s = s * a
    c = np.float32(1 / 479001600.0)
    for d in (-1 / 3628800.0, 1 / 40320.0, -1 / 720.0, 1 / 24.0, -0.5, 1.0):
        c = c * q + np.float32(d)
    return 1.0 - 2.0 * s * s, 2.0 * s * c


def segment_max(value):
    segment = iota(value.shape, 1) >> 6
    total = value
    for n in range(value.shape[1] // P_SIZE):
        inside = segment == n
        top = jnp.max(jnp.where(inside, value, -jnp.inf), axis=1, keepdims=True)
        total = jnp.where(inside, top, total)
    return total


def forward_y(table, spectrum_x):
    high, low = two_terms(spectrum_x)
    return bdot(table, jnp.concatenate([high, high, low], axis=0))


def planes(product, unit):
    base = unit * 2 * P_SIZE
    lanes = GROUP * HALF
    cosine = product[base : base + P_SIZE]
    sine = product[base + P_SIZE : base + 2 * P_SIZE]
    return cosine[:, :lanes], sine[:, :lanes], cosine[:, lanes:], sine[:, lanes:]


def cross(first, second, unit, nyquist):
    a1, a2, a3, a4 = planes(first, unit)
    b1, b2, b3, b4 = planes(second, unit)
    ar = a1 + jnp.where(nyquist, 0.0, a4)
    ai = jnp.where(nyquist, 0.0, a3) - a2
    br = b1 + jnp.where(nyquist, 0.0, b4)
    bi = jnp.where(nyquist, 0.0, b3) - b2
    return (br * ar + bi * ai, bi * ar - br * ai, b3 * a3 + b4 * a4, b3 * a4 - b4 * a3)


def landscape(units, table_iy, table_ix):
    stacked = []
    for zr, zi in units:
        high, low = two_terms(jnp.concatenate([zr, zi], axis=0))
        stacked.append(jnp.concatenate([high, high, low], axis=0))
    back = bdot(table_iy, jnp.concatenate(stacked, axis=1) if len(stacked) > 1 else stacked[0])
    lanes = GROUP * HALF
    rows = []
    for unit in range(len(units)):
        piece = back[:, unit * lanes : (unit + 1) * lanes]
        rows.append(jnp.concatenate([piece[:P_SIZE], piece[P_SIZE:]], axis=1))
    value = jnp.concatenate(rows, axis=0) if len(rows) > 1 else rows[0]
    high, low = two_terms(value)
    return bdot(jnp.concatenate([high, low, high], axis=1), table_ix)


def exact_dot(a, b):
    terms = []
    for _ in range(3):
        terms.append(a.astype(BF16))
        a = a - terms[-1].astype(F32)
    return bdot(jnp.concatenate(terms, axis=1), jnp.concatenate([b, b, b], axis=0))


def kernel(
    n_gx, n_gy, fine_hbm, coarse_hbm, tile_hbm, mask_hbm, *rest
):
    hbm_tables, (out,), scratch = rest[:4], rest[4:5], rest[5:]
    table_refs, scratch = scratch[:4], scratch[4:]
    (tile, ext, coarse, own, given, got, spec, spec_high, spec_low, ctab, logits, peaks, stats) = scratch[:13]
    send_sem, recv_sem, csend, crecv, local_sem, table_sem, back_sem = scratch[13:20]
    fine_off, coarse_off, mask, small_sem, packs, landed, crossed = scratch[20:27]
    mine, flows, fsend, frecv, known = scratch[27:]
    tx, ty, tiy_ref, tix_ref = table_refs
    pairs, gx, gy, gz = (lax.axis_index(a) for a in ("pairs", "gx", "gy", "gz"))
    rows, width = tile.shape
    half = rows // 2
    edge = ext.shape[2] - width

    def device(x, y, z):
        return (pairs, x, y, z)

    load = pltpu.make_async_copy(tile_hbm, tile, local_sem.at[2])
    load.start()
    small_copies = [
        pltpu.make_async_copy(source, target, small_sem.at[n])
        for n, (source, target) in enumerate(
            ((fine_hbm, fine_off), (coarse_hbm, coarse_off), (mask_hbm, mask))
        )
    ]
    for copy in small_copies:
        copy.start()

    barrier = pltpu.get_barrier_semaphore()
    greeted = [(gx, gy, 1 - gz, None)]
    greeted.append((gx - 1, gy, 1, (gz == 1) & (gx >= 1)))
    for z in range(2):
        greeted.append((gx + 1, gy, z, gx + 1 < n_gx))
    for x in (gx, gx + 1):
        for z in range(2):
            greeted.append((x, gy + 1, z, (gz == 1) & (gy + 1 < n_gy) & (x < n_gx)))
    for x, y, z, use in greeted:

        def greet():
            pl.semaphore_signal(barrier, inc=1, device_id=device(x, y, z), device_id_type=MESH)

        if use is None:
            greet()
        else:
            pl.when(use)(greet)

    has_left = jnp.where(gx >= 1, 1, 0)
    count = 1 + 2 * has_left + jnp.where((gz == 1) & (gx + 1 < n_gx), 1, 0) + jnp.where(gy >= 1, 1 + has_left, 0)

    table_copies = [
        pltpu.make_async_copy(source, target, table_sem.at[n])
        for n, (source, target) in enumerate(zip(hbm_tables, table_refs))
    ]
    for copy in table_copies:
        copy.start()
    first_half = pltpu.make_async_copy(
        tile_hbm.at[pl.ds(0, half + P_SIZE), :],
        ext.at[0, pl.ds(0, half + P_SIZE), pl.ds(0, width)],
        local_sem.at[0],
    )
    second_half = pltpu.make_async_copy(
        tile_hbm.at[pl.ds(half, half), :], ext.at[1, pl.ds(0, half), pl.ds(0, width)], local_sem.at[1]
    )

    @pl.when(gz == 0)
    def _():
        first_half.start()

    @pl.when(gz == 1)
    def _():
        second_half.start()

    pool_rows = jnp.where((iota((rows // DOWN, rows), 1) >> 3) == iota((rows // DOWN, rows), 0), 1.0, 0.0)
    lanes = iota((width, 2 * P_SIZE), 1)
    block = iota((width, 2 * P_SIZE), 0) >> 3
    pool = jnp.where(block == (lanes & (P_SIZE - 1)), 1.0, 0.0).astype(BF16)
    pool_rows = pool_rows.astype(BF16)
    load.wait()
    piece = bdot(pool_rows, tile[...])
    terms = []
    for _ in range(3):
        terms.append(piece.astype(BF16))
        piece = piece - terms[-1].astype(F32)
    packed = bdot(jnp.concatenate(terms, axis=1), jnp.concatenate([pool] * 3, axis=0))
    packed = jnp.where(iota((HALF, 2 * P_SIZE), 1) < P_SIZE, packed[:HALF], packed[HALF:])
    packed = (packed * (1.0 / DOWN)).astype(BF16)
    own[...] = packed
    coarse[0, gz] = packed

    @pl.when(gx + 1 >= n_gx)
    def _():
        ext[:, :, width:] = jnp.zeros((2, half + P_SIZE, edge), BF16)
        coarse[1] = jnp.zeros(coarse.shape[1:], BF16)

    @pl.when((gz == 1) & (gy + 1 >= n_gy))
    def _():
        ext[:, half:, :width] = jnp.zeros((2, P_SIZE, width), BF16)
        ext[:, half:, width:] = jnp.zeros((2, P_SIZE, edge), BF16)

    pl.semaphore_wait(barrier, count)

    long, short = half // 2, P_SIZE // 2

    def halo_copy(kind, c, section, x, y):
        if c == 0:
            source, target = (
                (pl.ds(0, half + P_SIZE), pl.ds(0, half + P_SIZE)),
                (pl.ds(half, half), pl.ds(0, half)),
                (pl.ds(0, P_SIZE), pl.ds(half, P_SIZE)),
            )[kind]
            source = tile.at[source, :]
            target = ext.at[section, target, pl.ds(0, width)]
        else:
            source, target = (
                (pl.ds(0, long + short), pl.ds(0, long + short)),
                (pl.ds(long + short, long), pl.ds(0, long)),
                (pl.ds(2 * long + short, short), pl.ds(long, short)),
            )[kind]
            source = packs.at[source, :]
            target = landed.at[section, target, :]
        slot = kind * 4 + c * 2
        return pltpu.make_async_remote_copy(
            src_ref=source,
            dst_ref=target,
            send_sem=send_sem.at[slot],
            recv_sem=recv_sem.at[slot + section],
            device_id=device(x, y, 0 if kind == 0 else 1),
            device_id_type=MESH,
        )

    def coarse_copy(x, z, place, section, source):
        return pltpu.make_async_remote_copy(
            src_ref=source,
            dst_ref=coarse.at[place, section],
            send_sem=csend.at[place, z],
            recv_sem=crecv.at[place, section],
            device_id=device(x, gy, z),
            device_id_type=MESH,
        )

    def to_left():
        return [coarse_copy(gx - 1, z, 1, gz, own) for z in range(2)]

    coarse_copy(gx, 1 - gz, 0, gz, own).start()

    @pl.when(gx >= 1)
    def _():
        for copy in to_left():
            copy.start()

    def tell(way, n):
        x = gx + 1 if way == 0 else gx - 1

        @pl.when((gz == 1) & (x >= 0) & (x < n_gx))
        def _():
            pl.semaphore_signal(
                known.at[way, n], inc=1, device_id=device(x, gy, 1), device_id_type=MESH
            )

    def relay_right():
        for n in range(n_gx - 1):

            @pl.when((gz == 1) & (gx >= 1 + n))
            def _():
                if n:
                    pl.semaphore_wait(known.at[0, n - 1], 1)
                if n < n_gx - 2:
                    tell(0, n)

    def relay_left():
        for n in range(n_gx - 1):

            @pl.when((gz == 1) & (gx + 1 + n < n_gx))
            def _():
                pl.semaphore_wait(known.at[1, n], 1)
                if n < n_gx - 2:
                    tell(1, n + 1)

    tell(1, 0)
    relay_right()

    def sends():
        out = []
        for c in (0, 1):
            for kind in range(3):
                use = gx - c >= 0
                if kind == 2:
                    use = use & (gy - 1 >= 0)
                elif c == 0:
                    use = use & (gz != kind)
                out.append((use, kind, c, gx - c, gy - 1 if kind == 2 else gy))
        return out

    for use, kind, c, x, y in sends():
        if c == 0:

            @pl.when(use)
            def _():
                halo_copy(kind, c, gz, x, y).start()

    @pl.when(gx >= 1)
    def _():
        put = 0
        for top, size in ((0, long), (half, short), (half, long), (0, short)):
            upper = tile[top : top + size, :128].astype(F32)
            lower = tile[top + size : top + 2 * size, :128].astype(F32)
            both = jnp.where(iota((size, 128), 1) < P_SIZE, upper, pltpu.roll(lower, P_SIZE, 1))
            packs[put : put + size] = both.astype(BF16)
            put += size

    for use, kind, c, x, y in sends():
        if c == 1:

            @pl.when(use)
            def _():
                halo_copy(kind, c, gz, x, y).start()

    def arrivals(c, kinds):
        for section in range(2):
            for kind in kinds:
                use = (gz == 0) if kind == 0 else (gz == 1)
                if c == 1:
                    use = use & (gx + 1 < n_gx)
                if kind == 2:
                    use = use & (gy + 1 < n_gy)
                elif c == 0:
                    use = use & (gz != section)

                @pl.when(use)
                def _():
                    halo_copy(kind, c, section, gx, gy).wait_recv()

    tile_width = mask.shape[1] * STRIDE
    patch_rows = half // STRIDE
    groups = mask.shape[1] // GROUP
    lanes = GROUP * HALF
    wide = GROUP * P_SIZE
    for copy in small_copies:
        copy.wait()
    roff, coff, off = fine_off[0], fine_off[1], coarse_off[0]
    for copy in table_copies:
        copy.wait()
    table_iy, table_ix = tiy_ref[...], tix_ref[...]

    span = tx.shape[0] // 2
    at = iota((span, 2 * lanes), 0) - coff - STRIDE * ((iota((span, 2 * lanes), 1) >> 5) & (GROUP - 1))
    inside = jnp.where((at >= 0) & (at < P_SIZE), 1.0, 0.0).astype(BF16)
    block = (2 * P_SIZE, 2 * lanes)
    from_left = (iota(block, 0) & (P_SIZE - 1)) - P_SIZE * ((iota(block, 1) >> 5) & (GROUP - 1)) - off
    plain = [tx[0 : 2 * P_SIZE], tx[span : span + 2 * P_SIZE]]
    for step in range(2):
        at_step = from_left + step * P_SIZE
        keep = jnp.where((at_step >= 0) & (at_step < P_SIZE), 1.0, 0.0).astype(BF16)
        for term in range(2):
            base = (2 * step + term) * 2 * P_SIZE
            ctab[base : base + 2 * P_SIZE] = plain[term] * keep

    nyquist = (iota((P_SIZE, lanes), 1) & (HALF - 1)) == 0
    frow = signed_of(iota((P_SIZE, wide), 0))

    def along_x_of(section, top, size, g):
        data = ext[section, pl.ds(top, size), g * lanes : g * lanes + span]
        value = bdot(jnp.concatenate([data, data], axis=1), tx[...])
        spec[section, 2 * g, pl.ds(top, size), :] = value[:, :lanes]
        spec[section, 2 * g + 1, pl.ds(top, size), :] = value[:, lanes:]

    inner = groups - 1

    @pl.when(gz == 0)
    def _():
        first_half.wait()

    @pl.when(gz == 1)
    def _():
        second_half.wait()

    def split(g, top, size):
        for section in range(2):
            for t in range(2):
                high, low = two_terms(spec[section, 2 * g + t, pl.ds(roff + top, size), :])
                part = slice((2 * g + t) * lanes, (2 * g + t + 1) * lanes)
                spec_high[section, top : top + size, part] = high
                spec_low[section, top : top + size, part] = low

    def forward(g, first_row, last_row):
        part = slice(g * 2 * lanes, (g + 1) * 2 * lanes)
        for row in range(first_row, last_row):
            window = slice(row * STRIDE, row * STRIDE + P_SIZE)
            first, second = (
                bdot(
                    ty[...],
                    jnp.concatenate(
                        [
                            spec_high[t, window, part],
                            spec_high[t, window, part],
                            spec_low[t, window, part],
                        ],
                        axis=0,
                    ),
                )
                for t in range(2)
            )
            for n, plane in enumerate(cross(first, second, 0, nyquist)):
                crossed[g * patch_rows + row, n] = plane
            yield

    upper_rows, middle_row = patch_rows - 2, half - STRIDE

    def upper(g):
        split(g, 0, middle_row)
        yield from forward(g, 0, upper_rows)

    def lower(g):
        split(g, middle_row, P_SIZE)
        yield from forward(g, upper_rows, patch_rows)

    def last_columns():
        for below in range(2):
            use = gx + 1 < n_gx
            if below:
                use = use & ((gz == 0) | (gy + 1 < n_gy))

            @pl.when(use)
            def _():
                for section in range(2):
                    top, size, source = (half, short, long) if below else (0, long, 0)
                    data = landed[section, source : source + size]
                    ext[section, top : top + size, width:] = data
                    data = pltpu.roll(data.astype(F32), P_SIZE, 1).astype(BF16)
                    ext[section, top + size : top + 2 * size, width:] = data

        for section in range(2):
            along_x_of(section, 0, half + P_SIZE, inner)

    relay_left()

    coarse_copy(gx, gz, 0, 1 - gz, own).wait_recv()

    @pl.when(gx + 1 < n_gx)
    def _():
        for section in range(2):
            coarse_copy(gx, 0, 1, section, own).wait_recv()

    def own_lines():
        tx[0:span] = tx[0:span] * inside
        tx[span:] = tx[span:] * inside
        yield
        for g in range(inner):
            along_x_of(gz, 0, half, g)
            yield

    beside = own_lines()

    def step(count):
        for _ in range(count):
            next(beside, None)

    left = iota((HALF, 2 * P_SIZE), 1) < P_SIZE
    fcol = signed_of(iota((1, wide), 1) & (P_SIZE - 1))
    lines = []
    for section in range(2):
        terms = []
        for source in range(2):
            data = coarse[source, section].astype(F32)
            both = jnp.concatenate(
                [jnp.where(left, data, 0.0), jnp.where(left, 0.0, data)], axis=0
            ).astype(BF16)
            terms += [both, both]
        lines.append(jnp.concatenate(terms, axis=1))
    value = bdot(jnp.concatenate(lines, axis=0), ctab[...])
    step(BESIDE)
    first = forward_y(ty[...], value[:P_SIZE])
    second = forward_y(ty[...], value[P_SIZE:])
    step(BESIDE)
    hr, hi, yr, yi = cross(first, second, 0, nyquist)
    value = landscape(
        [(hr - jnp.where(nyquist, yi, 0.0), hi + jnp.where(nyquist, yr, 0.0))],
        table_iy,
        table_ix[:, : 2 * P_SIZE],
    )
    step(BESIDE)
    ours = iota((P_SIZE, 2 * P_SIZE), 1) < P_SIZE
    value = jnp.where(ours, value, -jnp.inf)
    top = jnp.broadcast_to(jnp.max(value, axis=0, keepdims=True), (8, 2 * P_SIZE))
    top = jnp.max(top, axis=1, keepdims=True)[0:1]
    step(BESIDE)
    weight = jnp.exp2(value - top)
    s0 = jnp.sum(weight, axis=0, keepdims=True)
    s1 = jnp.sum(weight * frow[:, : 2 * P_SIZE], axis=0, keepdims=True)
    rows = iota((8, 2 * P_SIZE), 0)
    both = jnp.where(rows == 0, s0, jnp.where(rows == 1, s1, s0 * fcol[:, : 2 * P_SIZE]))
    total = jnp.sum(both, axis=1, keepdims=True)
    rows = iota((8, 128), 0)
    found = jnp.where(rows == 0, total[1:2] / total[0:1], total[2:3] / total[0:1])
    mine[...] = found
    flows[gx] = found

    def flow_copy(x, place, z=0):
        return pltpu.make_async_remote_copy(
            src_ref=mine,
            dst_ref=flows.at[place],
            send_sem=fsend.at[x, z],
            recv_sem=frecv.at[place],
            device_id=device(x, gy, z),
            device_id_type=MESH,
        )

    for x in range(n_gx):

        @pl.when((x != gx) & (gz == 1))
        def _():
            for z in range(2):
                flow_copy(x, gx, z).start()

    for _ in beside:
        pass
    arrivals(0, (0, 1))
    for g in range(inner):
        along_x_of(1 - gz, 0, half, g)
    for g in range(inner):
        for _ in upper(g):
            pass
    arrivals(0, (2,))
    for g in range(inner):
        for section in range(2):
            along_x_of(section, half, P_SIZE, g)
    for g in range(inner):
        for _ in lower(g):
            pass
    arrivals(1, (0, 1, 2))
    last_columns()
    for part in (upper, lower):
        for _ in part(inner):
            pass

    columns = mask.shape[1]
    side = columns // 2

    def lane_of(column):
        return (column & 1) * side + (column >> 1)

    put = jnp.where(lane_of(iota((wide, 128), 0) >> 6) == iota((wide, 128), 1), 1.0, 0.0)
    here = pl.ds(pl.multiple_of(gz * patch_rows, 8), patch_rows)
    place = jnp.where(lane_of(iota((columns, 128), 0)) == iota((columns, 128), 1), 1.0, 0.0)
    valid = bdot(mask[here, :].astype(F32).astype(BF16), place.astype(BF16))

    for x in range(n_gx):

        @pl.when(x != gx)
        def _():
            flow_copy(x, x).wait_recv()

    mean = sum(flows[x] for x in range(n_gx)) / float(n_gx)
    blended = [(0.5 * DOWN) * (flows[x] + mean) for x in range(n_gx)]

    def pick(column):
        centre = gx * tile_width + column * STRIDE + coff + P_SIZE // 2
        chosen = jnp.clip(((centre >> 3) - off) >> 6, 0, n_gx - 1)
        total = blended[0]
        for x in range(1, n_gx):
            total = jnp.where(chosen == x, blended[x], total)
        return total

    fky = signed_of(iota((P_SIZE, lanes), 0)) * (1.0 / P_SIZE)
    middle = iota((P_SIZE, lanes), 0) == HALF
    kx = (iota((1, lanes), 1) & (HALF - 1)).astype(F32) * (1.0 / P_SIZE)

    lane = iota((8, 128), 1)
    last_prior = pick(jnp.where(lane < side, 2 * lane, jnp.minimum(2 * (lane - side) + 1, columns - 1)))

    def backward(g):
        prior = pick(g * GROUP + (iota((8, lanes), 1) >> 5))
        dy, dx = prior[0:1], prior[1:2]
        eyr, eyi = cis(fky * dy)
        exr, exi = cis(kx * dx)
        nr, ni = cis(0.5 * dx)
        fr = jnp.where(nyquist, nr * eyr + jnp.where(middle, ni * eyi, 0.0), 0.0)
        eyi = jnp.where(middle, 0.0, eyi)
        fi = jnp.where(nyquist, nr * eyi, 0.0)
        er = eyr * exr - eyi * exi
        ei = eyr * exi + eyi * exr
        base = g * patch_rows
        units = []
        for unit in range(patch_rows):
            xr, xi, yr, yi = (crossed[base + unit, n] for n in range(4))
            hr = xr * er - xi * ei
            hi = xr * ei + xi * er
            units.append((hr - (yr * fi + yi * fr), hi + (yr * fr - yi * fi)))
        value = landscape(units, table_iy, table_ix)
        for unit in range(patch_rows):
            piece = value[unit * P_SIZE : (unit + 1) * P_SIZE]
            logits[base + unit] = piece
            peaks[base + unit : base + unit + 1] = jnp.max(piece, axis=0, keepdims=True)

    def weigh(g):
        rows = slice(g * patch_rows, (g + 1) * patch_rows)
        top = segment_max(peaks[rows])
        for row in range(patch_rows):
            n = g * patch_rows + row
            weight = jnp.exp2(logits[n] - top[row : row + 1])
            stats[0, n : n + 1] = jnp.sum(weight, axis=0, keepdims=True)
            stats[1, n : n + 1] = jnp.sum(weight * frow, axis=0, keepdims=True)

    for g in range(groups):
        backward(g)
        if g:
            weigh(g - 1)
    weigh(groups - 1)

    s0 = stats[0]
    sums = exact_dot(jnp.concatenate([s0, stats[1], s0 * fcol], axis=0), put.astype(BF16))
    units = groups * patch_rows

    def gather(stat):
        total = None
        for g in range(groups):
            piece = sums[stat * units + g * patch_rows : stat * units + (g + 1) * patch_rows]
            if g:
                piece = pltpu.roll(piece, g * GROUP // 2, 1)
            total = piece if total is None else total + piece
        return total

    den, along_y, along_x = gather(0), gather(1), gather(2)
    den = jnp.where(iota((patch_rows, 128), 1) < columns, den, 1.0)
    same = ((iota((patch_rows, 128), 0) + gz) & 1) == 0
    kept = []
    for c, total in enumerate((along_y, along_x)):
        value = last_prior[c : c + 1] + valid * (total / den)
        odd = pltpu.roll(value, 128 - side, 1)
        given[c] = jnp.where(same, odd, value)
        kept.append(jnp.where(same, value, odd))
    back = pltpu.make_async_remote_copy(
        src_ref=given,
        dst_ref=got,
        send_sem=back_sem.at[0],
        recv_sem=back_sem.at[1],
        device_id=device(gx, gy, 1 - gz),
        device_id_type=MESH,
    )
    back.start()
    coarse_copy(gx, 1 - gz, 0, gz, own).wait_send()

    @pl.when(gx >= 1)
    def _():
        for copy in to_left():
            copy.wait_send()

    for x in range(n_gx):

        @pl.when((x != gx) & (gz == 1))
        def _():
            for z in range(2):
                flow_copy(x, gx, z).wait_send()

    for use, kind, c, x, y in sends():

        @pl.when(use)
        def _():
            halo_copy(kind, c, gz, x, y).wait_send()

    back.wait()
    upper = jnp.full((patch_rows, 128), gz, jnp.int32) == 0
    for c in range(2):
        value = jnp.concatenate(
            [jnp.where(upper, kept[c], got[c]), jnp.where(upper, got[c], kept[c])], axis=0
        )
        out[c] = jnp.transpose(value)[:side]


def solution(mesh):
    n_gx, n_gy = mesh.shape["gx"], mesh.shape["gy"]
    tables = make_tables()
    vmem = pl.BlockSpec(memory_space=pltpu.VMEM)
    anywhere = pl.BlockSpec(memory_space=pl.ANY)

    def local(sections, fine_offsets, coarse_offset, tissue_mask):
        tile = sections[0]
        rows, width = tile.shape
        half = rows // 2
        assert rows // DOWN == P_SIZE and width // DOWN == P_SIZE and n_gx % GROUP == 0
        patch_rows, patch_cols = half // STRIDE, width // STRIDE
        dma = pltpu.SemaphoreType.DMA
        groups = patch_cols // GROUP
        units = patch_rows * groups
        wide = GROUP * P_SIZE
        flow = pl.pallas_call(
            lambda *refs: kernel(n_gx, n_gy, *refs),
            out_shape=pltpu.VMEM((2, patch_cols // 2, 2 * patch_rows), F32),
            in_specs=[anywhere] * (4 + len(tables)),
            out_specs=vmem,
            scratch_shapes=[pltpu.VMEM(t.shape, BF16) for t in tables]
            + [
                pltpu.VMEM((rows, width), BF16),
                pltpu.VMEM((2, half + P_SIZE, width + 128), BF16),
                pltpu.VMEM((2, 2, HALF, 2 * P_SIZE), BF16),
                pltpu.VMEM((HALF, 2 * P_SIZE), BF16),
                pltpu.VMEM((2, patch_rows, 128), F32),
                pltpu.VMEM((2, patch_rows, 128), F32),
                pltpu.VMEM((2, 2 * groups, half + P_SIZE, wide // 2), F32),
                pltpu.VMEM((2, half + STRIDE, groups * wide), BF16),
                pltpu.VMEM((2, half + STRIDE, groups * wide), BF16),
                pltpu.VMEM((8 * P_SIZE, wide), BF16),
                pltpu.VMEM((units, P_SIZE, wide), F32),
                pltpu.VMEM((units, wide), F32),
                pltpu.VMEM((2, units, wide), F32),
                dma((12,)),
                dma((12,)),
                dma((2, 2)),
                dma((2, 2)),
                dma((3,)),
                dma((len(tables),)),
                dma((2,)),
                pltpu.SMEM(fine_offsets.shape, jnp.int32),
                pltpu.SMEM((1,), jnp.int32),
                pltpu.VMEM(tissue_mask.shape, jnp.int32),
                dma((3,)),
                pltpu.VMEM((half + P_SIZE, 128), BF16),
                pltpu.VMEM((2, (half + P_SIZE) // 2, 128), BF16),
                pltpu.VMEM((units, 4, P_SIZE, wide // 2), F32),
                pltpu.VMEM((8, 128), F32),
                pltpu.VMEM((n_gx, 8, 128), F32),
                dma((n_gx, 2)),
                dma((n_gx,)),
                pltpu.SemaphoreType.REGULAR((2, n_gx)),
            ],
            compiler_params=pltpu.CompilerParams(
                collective_id=0, has_side_effects=True, vmem_limit_bytes=VMEM_BYTES
            ),
            name="flow",
        )(fine_offsets, coarse_offset, tile, tissue_mask, *[jnp.asarray(t) for t in tables])
        return jnp.swapaxes(flow, 1, 2)[:, None]

    placed = (P("gz", ("pairs", "gy"), "gx"), P("pairs"), P("pairs"), P(("pairs", "gy"), "gx"))
    return jax.shard_map(
        local,
        mesh=mesh,
        in_specs=placed,
        out_specs=P(None, "gz", ("pairs", "gy"), "gx"),
        check_vma=False,
    )
```
